128 devices in a mesh: space: 16 (over z_lo, y, core), dp: 8 (over z_hi, x).
Axes of the slice: x: 4, y: 4, z: 4 (z_hi: 2, z_lo: 2; z = z_hi * 2 + z_lo), core: 2. Of those that a mesh axis runs over, the one named last changes fastest.
Arguments:
- volume: bfloat16 [8, 64, 96, 512], P('dp', 'space'), may hold values from -6 to 6
- neighbours: int32 [8, 64, 26], P('dp'), may hold values from -1 to 63, as said below
- active: int32 [8, 64], P('dp'), may hold values from 0 to 1, as said below
- cotangent: bfloat16 [8, 64, 96, 512], P('dp', 'space'), may hold values from -0.01171875 to 0.01171875
- weight_one: bfloat16 [96, 2592], replicated, may hold values from -0.125 to 0.125
- weight_two: bfloat16 [96, 2592], replicated, may hold values from -0.125 to 0.125
- bias_one: float32 [96], replicated, may hold values from -3 to 3
- bias_two: float32 [96], replicated, may hold values from -3 to 3
Outputs:
- output: bfloat16 [8, 64, 96, 512], P('dp', 'space')
- grad_weight_one: float32 [96, 2592], replicated
- grad_weight_two: float32 [96, 2592], replicated
- grad_bias_one: float32 [96], replicated
- grad_bias_two: float32 [96], replicated
The draws below stay inside these ranges and needn't reach their ends.
Inputs may be any that keep to these rules, and one draw needn't show every extreme that they name: `neighbours`: each volume is a grid of 16 x 2 x 2 bricks; brick (l, y, z) sits in one slot, and slot g lies on space index g // 4. Entry k of a slot is the slot of the brick at the k-th offset, -1 where the offset leaves the grid. The bricks of brick layers 2m and 2m + 1 lie on space indices 2m and 2m + 1, one brick of each (y, z) on each of the two. `active`: the bricks on space indices 0 and 1 are all live.
All inputs are finite; a program needn't handle non-finite values.
Results may differ from the reference program's by a relative error of at most 0.0065.
Values may be sent and summed in bfloat16 or wider, within the bound.
A program may use at most 128 MiB of HBM per device.

```python
import jax
import jax.numpy as jnp
from jax import lax

C = 96
EDGE = 8
LY = 2
LZ = 2
BPD = 4
SLOTS = 64
VOLS = 8
CELLS = 512
N_SPACE = 16


OFFSETS = [(a, b, c) for a in (-1, 0, 1) for b in (-1, 0, 1) for c in (-1, 0, 1) if (a, b, c) != (0, 0, 0)]


def brick_layout(key):
    first_key, second_key = jax.random.split(key)
    swapped = jax.random.randint(first_key, (VOLS, N_SPACE // 2, BPD), 0, 2)
    many_keys = jax.random.split(second_key, VOLS * N_SPACE)
    orders = jax.vmap(lambda single: jax.random.permutation(single, BPD))(many_keys).reshape(VOLS, N_SPACE, BPD).astype(jnp.int32)
    layer_ids = jnp.arange(N_SPACE, dtype=jnp.int32)[None, :, None]
    owners = jnp.bitwise_xor(layer_ids, jnp.repeat(swapped, 2, axis=1)).astype(jnp.int32)
    return owners * BPD + jnp.take_along_axis(orders, owners, axis=1)


def by_slot(slot_of, values):
    flat_slots = slot_of.reshape(VOLS, SLOTS)
    flat_values = values.reshape(VOLS, SLOTS, -1)

    def place_one(slots_one, values_one):
        return jnp.zeros((SLOTS, values_one.shape[1]), jnp.int32).at[slots_one].set(values_one)
    return jax.vmap(place_one)(flat_slots, flat_values)


def draw_neighbours(key, part):
    slot_of = brick_layout(jax.random.fold_in(key, 7))
    grid = slot_of.reshape(VOLS, N_SPACE, LY, LZ)
    framed = jnp.pad(grid, ((0, 0), (1, 1), (1, 1), (1, 1)), constant_values=-1)
    columns = []
    for a, b, c in OFFSETS:
        columns.append(framed[:, 1 + a:1 + a + N_SPACE, 1 + b:1 + b + LY, 1 + c:1 + c + LZ])
    stacked = jnp.stack(columns, axis=-1)
    return by_slot(slot_of, stacked)


def draw_active(key, part):
    slot_of = brick_layout(jax.random.fold_in(key, 7))
    layer_ids = jnp.broadcast_to(jnp.arange(N_SPACE, dtype=jnp.int32)[None, :, None], (VOLS, N_SPACE, BPD))
    base_layer = layer_ids - layer_ids % 2
    scores = jax.random.randint(jax.random.fold_in(key, 11), (VOLS, N_SPACE, BPD), 0, 8 * N_SPACE)
    alive_bricks = (scores >= 7 * base_layer).astype(jnp.int32)
    return by_slot(slot_of, alive_bricks)[:, :, 0]


def shard_levels(key, extent, cuts, smallest, top_value):
    level, own = 1.0, jax.random.fold_in(key, 6)
    for axis_at, shards_of in cuts:
        steps = jnp.exp(jax.random.uniform(jax.random.fold_in(own, axis_at), (shards_of,), jnp.float32, smallest / len(cuts), top_value / len(cuts)))
        level = level * jnp.repeat(steps, extent[axis_at] // shards_of).reshape([-1 if axis == axis_at else 1 for axis in range(len(extent))])
    return level


def normal_values(stream_key, extent, scale, most, cuts=(), held_as=jnp.bfloat16):
    entries = jax.random.normal(stream_key, extent, jnp.float32) * scale
    if len(cuts) > 0:
        entries = shard_levels(stream_key, extent, cuts, -0.22, 0.18) * entries
    return jnp.clip(entries, min=-most, max=most).astype(held_as)


def setup_inputs(seed: int = 0) -> dict:
    keys = jax.random.split(jax.random.key(seed), 9)
    volume = normal_values(keys[0], (VOLS, SLOTS, C, CELLS), 1.0, 6.0, ((0, 8), (1, 16)))
    neighbours = draw_neighbours(jax.random.fold_in(keys[8], 71), 0)
    active = draw_active(jax.random.fold_in(keys[8], 71), 0)
    cotangent = normal_values(keys[3], (VOLS, SLOTS, C, CELLS), (VOLS * SLOTS * CELLS) ** -0.5, 0.01171875, ((0, 8), (1, 16)))
    weight_one = normal_values(keys[4], (C, 27 * C), (27 * C) ** -0.5, 0.125)
    weight_two = normal_values(keys[5], (C, 27 * C), (27 * C) ** -0.5, 0.125)
    bias_one = normal_values(keys[6], (C,), 0.5, 3.0, (), jnp.float32)
    bias_two = normal_values(keys[7], (C,), 0.5, 3.0, (), jnp.float32)
    return {"volume": volume, "neighbours": neighbours, "active": active, "cotangent": cotangent, "weight_one": weight_one, "weight_two": weight_two, "bias_one": bias_one, "bias_two": bias_two}


OFFSETS = [(a, b, c) for a in (-1, 0, 1) for b in (-1, 0, 1) for c in (-1, 0, 1) if (a, b, c) != (0, 0, 0)]

def collect_faces(bricks):
    edge_len = bricks.shape[-1]
    sides = [bricks[:, :, 0], bricks[:, :, edge_len - 1], bricks[:, :, :, 0], bricks[:, :, :, edge_len - 1], bricks[:, :, :, :, 0], bricks[:, :, :, :, edge_len - 1]]
    stacked = jnp.stack(sides, axis=2)
    return stacked.reshape(bricks.shape[0], bricks.shape[1], 6 * edge_len * edge_len)

def face_index(offset):
    if offset[0] != 0:
        return 1 if offset[0] < 0 else 0
    if offset[1] != 0:
        return 3 if offset[1] < 0 else 2
    return 5 if offset[2] < 0 else 4

def face_span(shift_by, edge_len):
    if shift_by < 0:
        return slice(edge_len - 1, edge_len)
    if shift_by > 0:
        return slice(0, 1)
    return slice(0, edge_len)

def target(shift_by, edge_len):
    if shift_by < 0:
        return slice(0, 1)
    if shift_by > 0:
        return slice(edge_len + 1, edge_len + 2)
    return slice(1, edge_len + 1)

def pad_bricks(center, pool, pool_rows):
    brick_count, channels, edge_len = (center.shape[0], center.shape[1], center.shape[2])
    face_area = edge_len * edge_len
    padded = jnp.zeros((brick_count, channels, edge_len + 2, edge_len + 2, edge_len + 2), center.dtype)
    padded = padded.at[:, :, 1:edge_len + 1, 1:edge_len + 1, 1:edge_len + 1].set(center)
    for k, offset in enumerate(OFFSETS):
        a, b, c = offset
        side_index = face_index(offset)
        source = pool[:, :, side_index * face_area:(side_index + 1) * face_area]
        face_cells = jnp.take(source, pool_rows[:, k], axis=0).reshape(brick_count, channels, edge_len, edge_len)
        if a != 0:
            piece_cells = face_cells[:, :, face_span(b, edge_len), face_span(c, edge_len)][:, :, None]
        elif b != 0:
            piece_cells = face_cells[:, :, :, face_span(c, edge_len)][:, :, :, None]
        else:
            piece_cells = face_cells[:, :, :, :, None]
        padded = padded.at[:, :, target(a, edge_len), target(b, edge_len), target(c, edge_len)].set(piece_cells)
    return padded

def pad_volume(flat_bricks, pool_rows):
    slot_count, channels, cell_count = flat_bricks.shape
    edge_len = EDGE
    center = flat_bricks.reshape(slot_count, channels, edge_len, edge_len, edge_len)
    outer_faces = collect_faces(center)
    zero_row = jnp.zeros((1, channels, outer_faces.shape[2]), outer_faces.dtype)
    pool = jnp.concatenate([outer_faces, zero_row], axis=0)
    return pad_bricks(center, pool, pool_rows)

def tap_slice(padded_wide, tap_index, edge_len):
    a, b, c = (tap_index // 9, tap_index // 3 % 3, tap_index % 3)
    window = padded_wide[:, :, a:a + edge_len, b:b + edge_len, c:c + edge_len]
    return window.reshape(padded_wide.shape[0], padded_wide.shape[1], edge_len ** 3)

def convolve(padded, weight_taps):
    padded_wide = padded.astype(jnp.float32)
    summed = jnp.zeros((padded.shape[0], weight_taps.shape[0], EDGE ** 3), jnp.float32)
    for tap_index in range(27):
        piece_cells = tap_slice(padded_wide, tap_index, EDGE)
        summed = summed + jnp.einsum('oi,sip->sop', weight_taps[:, tap_index], piece_cells, precision=lax.Precision.HIGHEST)
    return summed

def convolve_back(padded, weight_taps):
    padded_wide = padded.astype(jnp.float32)
    summed = jnp.zeros((padded.shape[0], weight_taps.shape[2], EDGE ** 3), jnp.float32)
    for tap_index in range(27):
        piece_cells = tap_slice(padded_wide, tap_index, EDGE)
        summed = summed + jnp.einsum('oi,sop->sip', weight_taps[:, 26 - tap_index], piece_cells, precision=lax.Precision.HIGHEST)
    return summed

def weight_grad(grad_cells, padded):
    padded_wide = padded.astype(jnp.float32)
    grad_wide = grad_cells.astype(jnp.float32)
    per_tap = []
    for tap_index in range(27):
        piece_cells = tap_slice(padded_wide, tap_index, EDGE)
        per_tap.append(jnp.einsum('sop,sip->oi', grad_wide, piece_cells, precision=lax.Precision.HIGHEST))
    return jnp.stack(per_tap, axis=1)

def silu_slope(values):
    sigma = jax.nn.sigmoid(values)
    return sigma * (1.0 + values * (1.0 - sigma))

def reference(volume, neighbours, active, cotangent, weight_one, weight_two, bias_one, bias_two):
    channels = volume.shape[2]
    taps_one = weight_one.astype(jnp.float32).reshape(channels, 27, channels)
    taps_two = weight_two.astype(jnp.float32).reshape(channels, 27, channels)

    def one_volume(carry, inputs):
        bricks, near_table, alive_slots, upstream = inputs
        slot_count = bricks.shape[0]
        live_mask = alive_slots.astype(jnp.float32)[:, None, None]
        masked = bricks * live_mask.astype(jnp.bfloat16)
        pool_rows = jnp.where(near_table < 0, slot_count, near_table).astype(jnp.int32)
        padded_x = pad_volume(masked, pool_rows)
        hidden_pre = convolve(padded_x, taps_one) + bias_one[None, :, None]
        hidden = (jax.nn.silu(hidden_pre) * live_mask).astype(jnp.bfloat16)
        padded_h = pad_volume(hidden, pool_rows)
        out_pre = convolve(padded_h, taps_two) + bias_two[None, :, None]
        result = (jax.nn.silu(out_pre) * live_mask).astype(jnp.bfloat16)
        grad_out = (upstream.astype(jnp.float32) * live_mask * silu_slope(out_pre)).astype(jnp.bfloat16)
        grad_w_two = weight_grad(grad_out, padded_h)
        grad_b_two = lax.optimization_barrier(jnp.sum(grad_out.astype(jnp.float32), axis=(0, 2)))
        padded_g = pad_volume(grad_out, pool_rows)
        hidden_grad = convolve_back(padded_g, taps_two)
        grad_hidden = (hidden_grad * live_mask * silu_slope(hidden_pre)).astype(jnp.bfloat16)
        grad_w_one = weight_grad(grad_hidden, padded_x)
        grad_b_one = lax.optimization_barrier(jnp.sum(grad_hidden.astype(jnp.float32), axis=(0, 2)))
        carry = (carry[0] + grad_w_one, carry[1] + grad_w_two, carry[2] + grad_b_one, carry[3] + grad_b_two)
        return (carry, result)
    start = (jnp.zeros((channels, 27, channels), jnp.float32), jnp.zeros((channels, 27, channels), jnp.float32), jnp.zeros((channels,), jnp.float32), jnp.zeros((channels,), jnp.float32))
    totals, outputs = lax.scan(one_volume, start, (volume, neighbours, active, cotangent))
    return (outputs, totals[0].reshape(channels, 27 * channels), totals[1].reshape(channels, 27 * channels), totals[2], totals[3])
```

```python
import jax
import jax.numpy as jnp
from jax import lax
from jax.sharding import PartitionSpec as P

EDGE = 8


OFFSETS = [
    (a, b, c) for a in (-1, 0, 1) for b in (-1, 0, 1) for c in (-1, 0, 1) if (a, b, c) != (0, 0, 0)
]
brick_block = 4
grid_width = 896
flat_width = 1280


def shifted(value, axis, steps):
    count = lax.axis_size(axis)
    leading, last = (max(0, -steps), min(count, count - steps))
    return lax.ppermute(value, axis, [(source, source + steps) for source in range(leading, last)])


def collect_faces(bricks):
    edge_len = bricks.shape[-1]
    sides = [
        bricks[:, :, 0],
        bricks[:, :, edge_len - 1],
        bricks[:, :, :, 0],
        bricks[:, :, :, edge_len - 1],
        bricks[:, :, :, :, 0],
        bricks[:, :, :, :, edge_len - 1],
    ]
    stacked = jnp.stack(sides, axis=2)
    return stacked.reshape(bricks.shape[0], bricks.shape[1], 6 * edge_len * edge_len)


def face_index(offset):
    if offset[0] != 0:
        return 1 if offset[0] < 0 else 0
    if offset[1] != 0:
        return 3 if offset[1] < 0 else 2
    return 5 if offset[2] < 0 else 4


def face_span(shift_by, edge_len):
    if shift_by < 0:
        return slice(edge_len - 1, edge_len)
    if shift_by > 0:
        return slice(0, 1)
    return slice(0, edge_len)


def target(shift_by, edge_len):
    if shift_by < 0:
        return slice(0, 1)
    if shift_by > 0:
        return slice(edge_len + 1, edge_len + 2)
    return slice(1, edge_len + 1)


def pad_bricks(center, pool, pool_rows):
    brick_count, channels, edge_len = (center.shape[0], center.shape[1], center.shape[2])
    face_area = edge_len * edge_len
    fetched = jnp.take(pool, pool_rows, axis=0)
    padded = jnp.zeros(
        (brick_count, channels, edge_len + 2, edge_len + 2, edge_len + 2), center.dtype
    )
    padded = padded.at[:, :, 1 : edge_len + 1, 1 : edge_len + 1, 1 : edge_len + 1].set(center)
    for k, offset in enumerate(OFFSETS):
        a, b, c = offset
        side_index = face_index(offset)
        face_cells = fetched[
            :, k, :, side_index * face_area : (side_index + 1) * face_area
        ].reshape(brick_count, channels, edge_len, edge_len)
        if a != 0:
            piece_cells = face_cells[:, :, face_span(b, edge_len), face_span(c, edge_len)][
                :, :, None
            ]
        elif b != 0:
            piece_cells = face_cells[:, :, :, face_span(c, edge_len)][:, :, :, None]
        else:
            piece_cells = face_cells[:, :, :, :, None]
        padded = padded.at[:, :, target(a, edge_len), target(b, edge_len), target(c, edge_len)].set(
            piece_cells
        )
    side_total = (edge_len + 2) ** 3
    flat = padded.reshape(brick_count, channels, side_total)
    return jnp.pad(flat, ((0, 0), (0, 0), (0, flat_width - side_total)))


def build_pool(center):
    outer_faces = collect_faces(center)
    slot_count, channels, width = outer_faces.shape
    face_area = width // 6
    first_faces = outer_faces[:, :, : 2 * face_area]
    filler = jnp.zeros((slot_count, channels, width - 2 * face_area), outer_faces.dtype)
    received = {}
    for offset in (-1, 1):
        received[offset] = shifted(outer_faces, "space", -offset)
    for offset in (-3, -2, 2, 3):
        received[offset] = jnp.concatenate([shifted(first_faces, "space", -offset), filler], axis=2)
    received[0] = outer_faces
    zero_row = jnp.zeros((1, channels, width), outer_faces.dtype)
    return jnp.concatenate(
        [
            received[-3],
            received[-2],
            received[-1],
            received[0],
            received[1],
            received[2],
            received[3],
            zero_row,
        ],
        axis=0,
    )


def halo_pad(flat_bricks, pool_rows):
    slot_count, channels, cell_count = flat_bricks.shape
    center = flat_bricks.reshape(slot_count, channels, EDGE, EDGE, EDGE)
    return pad_bricks(center, build_pool(center), pool_rows)


def tap_offset(tap_index):
    side = EDGE + 2
    return tap_index // 9 * side * side + tap_index // 3 % 3 * side + tap_index % 3


def to_grid(cells):
    slot_count, channels = (cells.shape[0], cells.shape[1])
    side = EDGE + 2
    shaped = cells.reshape(slot_count, channels, EDGE, EDGE, EDGE)
    shaped = jnp.pad(shaped, ((0, 0), (0, 0), (0, 0), (0, 2), (0, 2)))
    flat = shaped.reshape(slot_count, channels, EDGE * side * side)
    return jnp.pad(flat, ((0, 0), (0, 0), (0, grid_width - EDGE * side * side)))


def from_grid(grid_cells):
    slot_count, channels = (grid_cells.shape[0], grid_cells.shape[1])
    side = EDGE + 2
    shaped = grid_cells[:, :, : EDGE * side * side].reshape(slot_count, channels, EDGE, side, side)
    return shaped[:, :, :, :EDGE, :EDGE].reshape(slot_count, channels, EDGE**3)


def conv_forward(padded_block, weight_taps):
    summed = jnp.zeros((padded_block.shape[0], weight_taps.shape[0], grid_width), jnp.float32)
    for tap_index in range(27):
        start = tap_offset(tap_index)
        piece_cells = padded_block[:, :, start : start + grid_width]
        summed = summed + jnp.einsum(
            "oi,kip->kop",
            weight_taps[:, tap_index],
            piece_cells,
            preferred_element_type=jnp.float32,
        )
    return summed


def conv_backward(padded_block, weight_taps):
    summed = jnp.zeros((padded_block.shape[0], weight_taps.shape[2], grid_width), jnp.float32)
    for tap_index in range(27):
        start = tap_offset(tap_index)
        piece_cells = padded_block[:, :, start : start + grid_width]
        summed = summed + jnp.einsum(
            "oi,kop->kip",
            weight_taps[:, 26 - tap_index],
            piece_cells,
            preferred_element_type=jnp.float32,
        )
    return summed


def run_blocks(conv_fn, padded, weight_taps, live_count):
    slot_count = padded.shape[0]
    block_total = (live_count + brick_block - 1) // brick_block
    start_out = jnp.zeros((slot_count, weight_taps.shape[0], grid_width), jnp.float32)

    def run_one_block(block_id, current):
        return conv_fn(padded, weight_taps)

    return from_grid(lax.fori_loop(0, block_total, run_one_block, start_out))


def accumulate(grad_cells, padded, live_count, channels):
    block_total = (live_count + brick_block - 1) // brick_block
    grad_grid = to_grid(grad_cells)
    start_grad = jnp.zeros((channels, 27, channels), jnp.float32)

    def accumulate_one_block(block_id, current):
        per_tap = []
        for tap_index in range(27):
            start = tap_offset(tap_index)
            piece_cells = padded[:, :, start : start + grid_width]
            per_tap.append(
                jnp.einsum(
                    "kop,kip->oi", grad_grid, piece_cells, preferred_element_type=jnp.float32
                )
            )
        return current + jnp.stack(per_tap, axis=1)

    return lax.fori_loop(0, block_total, accumulate_one_block, start_grad)


MESH_AXES = ("space", "dp")
RING_AXES = (("core", 2), ("x", 4), ("y", 4), ("z", 4))


def chip_coords(space, dp):
    return {"core": space % 2, "x": dp % 4, "y": space // 2 % 4, "z": dp // 4 * 2 + space // 8}


def linear_of(coords):
    space = ((coords["z"] % 2) * 4 + coords["y"]) * 2 + coords["core"]
    return space * 8 + coords["z"] // 2 * 4 + coords["x"]


def ring_pairs(name, size, steps):
    result = []
    for space in range(16):
        for dp in range(8):
            coords = chip_coords(space, dp)
            moved = dict(coords)
            moved[name] = (coords[name] + steps) % size
            result.append((space * 8 + dp, linear_of(moved)))
    return result


def all_reduce_sum(flat):
    coords = chip_coords(lax.axis_index("space"), lax.axis_index("dp"))
    pieces = flat
    for name, size in RING_AXES:
        me = coords[name]
        chunks = pieces.reshape(size, pieces.shape[0] // size, pieces.shape[1])
        total = lax.dynamic_index_in_dim(chunks, me, 0, keepdims=False)
        for steps in range(1, size):
            outgoing = lax.dynamic_index_in_dim(chunks, (me + steps) % size, 0, keepdims=False)
            total = total + lax.ppermute(outgoing, MESH_AXES, ring_pairs(name, size, steps))
        pieces = total
    for name, size in reversed(RING_AXES):
        me = coords[name]
        stacked = jnp.zeros((size,) + pieces.shape, pieces.dtype)
        stacked = lax.dynamic_update_index_in_dim(stacked, pieces, me, 0)
        for steps in range(1, size):
            arrived = lax.ppermute(pieces, MESH_AXES, ring_pairs(name, size, steps))
            stacked = lax.dynamic_update_index_in_dim(stacked, arrived, (me - steps) % size, 0)
        pieces = stacked.reshape(size * pieces.shape[0], pieces.shape[1])
    return pieces


def share_grads(weight_sums, bias_sums):
    flat = jnp.concatenate([weight_sums.reshape(-1), bias_sums.reshape(-1)])
    rows = 4096
    padded = jnp.pad(flat, (0, rows * 128 - flat.shape[0])).reshape(rows, 128)
    summed = all_reduce_sum(padded).reshape(-1)
    weight_total = summed[: weight_sums.size].reshape(weight_sums.shape)
    bias_total = summed[weight_sums.size : flat.shape[0]].reshape(bias_sums.shape)
    return weight_total, bias_total


def silu_slope(values):
    sigma = jax.nn.sigmoid(values)
    return sigma * (1.0 + values * (1.0 - sigma))


def local(volume, neighbours, active, cotangent, weight_one, weight_two, bias_one, bias_two):
    slot_count, channels = (volume.shape[1], volume.shape[2])
    position = lax.axis_index("space")
    group_count = lax.axis_size("space")
    alive_all = active[0]
    alive_grid = alive_all.reshape(group_count, slot_count)
    live_rank = jnp.cumsum(alive_grid, axis=1) - 1
    dead_rank = jnp.sum(alive_grid, axis=1, keepdims=True) + jnp.cumsum(1 - alive_grid, axis=1) - 1
    place_flat = jnp.where(alive_grid > 0, live_rank, dead_rank).reshape(-1)
    compact_place = lax.dynamic_slice_in_dim(place_flat, position * slot_count, slot_count, 0)
    compact_order = (
        jnp.zeros((slot_count,), jnp.int32)
        .at[compact_place]
        .set(jnp.arange(slot_count, dtype=jnp.int32))
    )
    own_alive = lax.dynamic_slice_in_dim(alive_all, position * slot_count, slot_count, 0)
    live_count = jnp.sum(own_alive)
    near_table = lax.dynamic_slice_in_dim(neighbours[0], position * slot_count, slot_count, 0)
    near_table = jnp.take(near_table, compact_order, axis=0)
    safe_slot = jnp.maximum(near_table, 0)
    source_offset = safe_slot // slot_count - position + 3
    pool_rows = jnp.where(
        near_table < 0, 7 * slot_count, source_offset * slot_count + jnp.take(place_flat, safe_slot)
    )
    live_mask = (jnp.arange(slot_count) < live_count).astype(jnp.float32)[:, None, None]
    taps_one = weight_one.reshape(channels, 27, channels)
    taps_two = weight_two.reshape(channels, 27, channels)
    masked = jnp.take(volume[0], compact_order, axis=0) * live_mask.astype(jnp.bfloat16)
    padded_x = halo_pad(masked, pool_rows)
    hidden_pre = run_blocks(conv_forward, padded_x, taps_one, live_count) + bias_one[None, :, None]
    hidden = (jax.nn.silu(hidden_pre) * live_mask).astype(jnp.bfloat16)
    padded_h = halo_pad(hidden, pool_rows)
    out_pre = run_blocks(conv_forward, padded_h, taps_two, live_count) + bias_two[None, :, None]
    result = (jax.nn.silu(out_pre) * live_mask).astype(jnp.bfloat16)
    upstream = jnp.take(cotangent[0], compact_order, axis=0)
    grad_out = (upstream.astype(jnp.float32) * live_mask * silu_slope(out_pre)).astype(jnp.bfloat16)
    grad_w_two = accumulate(grad_out, padded_h, live_count, channels).reshape(
        channels, 27 * channels
    )
    grad_b_two = jnp.sum(grad_out.astype(jnp.float32), axis=(0, 2))
    padded_g = halo_pad(grad_out, pool_rows)
    hidden_grad = run_blocks(conv_backward, padded_g, taps_two, live_count)
    grad_hidden = (hidden_grad * live_mask * silu_slope(hidden_pre)).astype(jnp.bfloat16)
    grad_w_one = accumulate(grad_hidden, padded_x, live_count, channels).reshape(
        channels, 27 * channels
    )
    grad_b_one = jnp.sum(grad_hidden.astype(jnp.float32), axis=(0, 2))
    shared_all = share_grads(
        jnp.concatenate([grad_w_one, grad_w_two], axis=0),
        jnp.stack([grad_b_one, grad_b_two], axis=0),
    )
    total_w_one, total_w_two = (shared_all[0][:channels], shared_all[0][channels:])
    total_b_one, total_b_two = (shared_all[1][0], shared_all[1][1])
    output = jnp.take(result, compact_place, axis=0)[None]
    return (output, total_w_one, total_w_two, total_b_one, total_b_two)


def solution(mesh):
    in_specs = (
        P("dp", "space", None, None),
        P("dp", None, None),
        P("dp", None),
        P("dp", "space", None, None),
        P(),
        P(),
        P(),
        P(),
    )
    out_specs = (P("dp", "space", None, None), P(), P(), P(), P())
    return jax.shard_map(local, mesh=mesh, in_specs=in_specs, out_specs=out_specs, check_vma=False)
```

```python
import jax
import jax.numpy as jnp
from jax import lax
from jax.sharding import PartitionSpec as P
from jax.experimental import pallas as pl
from jax.experimental.pallas import tpu as pltpu

EDGE = 8


OFFSETS = [
    (a, b, c) for a in (-1, 0, 1) for b in (-1, 0, 1) for c in (-1, 0, 1) if (a, b, c) != (0, 0, 0)
]
brick_block = 4
grid_width = 896
flat_width = 1280


def shifted(value, axis, steps):
    count = lax.axis_size(axis)
    leading, last = (max(0, -steps), min(count, count - steps))
    return lax.ppermute(value, axis, [(source, source + steps) for source in range(leading, last)])


def collect_faces(bricks):
    edge_len = bricks.shape[-1]
    sides = [
        bricks[:, :, 0],
        bricks[:, :, edge_len - 1],
        bricks[:, :, :, 0],
        bricks[:, :, :, edge_len - 1],
        bricks[:, :, :, :, 0],
        bricks[:, :, :, :, edge_len - 1],
    ]
    stacked = jnp.stack(sides, axis=2)
    return stacked.reshape(bricks.shape[0], bricks.shape[1], 6 * edge_len * edge_len)


def face_index(offset):
    if offset[0] != 0:
        return 1 if offset[0] < 0 else 0
    if offset[1] != 0:
        return 3 if offset[1] < 0 else 2
    return 5 if offset[2] < 0 else 4


def face_span(shift_by, edge_len):
    if shift_by < 0:
        return slice(edge_len - 1, edge_len)
    if shift_by > 0:
        return slice(0, 1)
    return slice(0, edge_len)


def target(shift_by, edge_len):
    if shift_by < 0:
        return slice(0, 1)
    if shift_by > 0:
        return slice(edge_len + 1, edge_len + 2)
    return slice(1, edge_len + 1)


def pad_bricks(center, pool, pool_rows):
    brick_count, channels, edge_len = (center.shape[0], center.shape[1], center.shape[2])
    face_area = edge_len * edge_len
    fetched = jnp.take(pool, pool_rows, axis=0)
    padded = jnp.zeros(
        (brick_count, channels, edge_len + 2, edge_len + 2, edge_len + 2), center.dtype
    )
    padded = padded.at[:, :, 1 : edge_len + 1, 1 : edge_len + 1, 1 : edge_len + 1].set(center)
    for k, offset in enumerate(OFFSETS):
        a, b, c = offset
        side_index = face_index(offset)
        face_cells = fetched[
            :, k, :, side_index * face_area : (side_index + 1) * face_area
        ].reshape(brick_count, channels, edge_len, edge_len)
        if a != 0:
            piece_cells = face_cells[:, :, face_span(b, edge_len), face_span(c, edge_len)][
                :, :, None
            ]
        elif b != 0:
            piece_cells = face_cells[:, :, :, face_span(c, edge_len)][:, :, :, None]
        else:
            piece_cells = face_cells[:, :, :, :, None]
        padded = padded.at[:, :, target(a, edge_len), target(b, edge_len), target(c, edge_len)].set(
            piece_cells
        )
    side_total = (edge_len + 2) ** 3
    flat = padded.reshape(brick_count, channels, side_total)
    return jnp.pad(flat, ((0, 0), (0, 0), (0, flat_width - side_total)))


def build_pool(center):
    outer_faces = collect_faces(center)
    slot_count, channels, width = outer_faces.shape
    face_area = width // 6
    first_faces = outer_faces[:, :, : 2 * face_area]
    filler = jnp.zeros((slot_count, channels, width - 2 * face_area), outer_faces.dtype)
    received = {}
    for offset in (-1, 1):
        received[offset] = shifted(outer_faces, "space", -offset)
    for offset in (-3, -2, 2, 3):
        received[offset] = jnp.concatenate([shifted(first_faces, "space", -offset), filler], axis=2)
    received[0] = outer_faces
    zero_row = jnp.zeros((1, channels, width), outer_faces.dtype)
    return jnp.concatenate(
        [
            received[-3],
            received[-2],
            received[-1],
            received[0],
            received[1],
            received[2],
            received[3],
            zero_row,
        ],
        axis=0,
    )


def halo_pad(flat_bricks, pool_rows):
    slot_count, channels, cell_count = flat_bricks.shape
    center = flat_bricks.reshape(slot_count, channels, EDGE, EDGE, EDGE)
    return pad_bricks(center, build_pool(center), pool_rows)


def tap_offset(tap_index):
    side = EDGE + 2
    return tap_index // 9 * side * side + tap_index // 3 % 3 * side + tap_index % 3


def to_grid(cells):
    slot_count, channels = (cells.shape[0], cells.shape[1])
    side = EDGE + 2
    shaped = cells.reshape(slot_count, channels, EDGE, EDGE, EDGE)
    shaped = jnp.pad(shaped, ((0, 0), (0, 0), (0, 0), (0, 2), (0, 2)))
    flat = shaped.reshape(slot_count, channels, EDGE * side * side)
    return jnp.pad(flat, ((0, 0), (0, 0), (0, grid_width - EDGE * side * side)))


def from_grid(grid_cells):
    slot_count, channels = (grid_cells.shape[0], grid_cells.shape[1])
    side = EDGE + 2
    shaped = grid_cells[:, :, : EDGE * side * side].reshape(slot_count, channels, EDGE, side, side)
    return shaped[:, :, :, :EDGE, :EDGE].reshape(slot_count, channels, EDGE**3)


def conv_forward(padded_block, weight_taps):
    summed = jnp.zeros((padded_block.shape[0], weight_taps.shape[0], grid_width), jnp.float32)
    for tap_index in range(27):
        start = tap_offset(tap_index)
        piece_cells = padded_block[:, :, start : start + grid_width]
        summed = summed + jnp.einsum(
            "oi,kip->kop",
            weight_taps[:, tap_index],
            piece_cells,
            preferred_element_type=jnp.float32,
        )
    return summed


def conv_backward(padded_block, weight_taps):
    summed = jnp.zeros((padded_block.shape[0], weight_taps.shape[2], grid_width), jnp.float32)
    for tap_index in range(27):
        start = tap_offset(tap_index)
        piece_cells = padded_block[:, :, start : start + grid_width]
        summed = summed + jnp.einsum(
            "oi,kop->kip",
            weight_taps[:, 26 - tap_index],
            piece_cells,
            preferred_element_type=jnp.float32,
        )
    return summed


def tap_window(whole, tap_index):
    start = tap_offset(tap_index)
    if start:
        whole = pltpu.roll(whole, flat_width - start, 1)
    return whole[:, :grid_width].astype(jnp.bfloat16)


def conv_kernel(padded_ref, taps_ref, out_ref):
    for brick in range(padded_ref.shape[0]):
        whole = padded_ref[brick].astype(jnp.float32)
        summed = jnp.zeros(out_ref.shape[1:], jnp.float32)
        for tap_index in range(27):
            summed = summed + jnp.dot(
                taps_ref[tap_index],
                tap_window(whole, tap_index),
                preferred_element_type=jnp.float32,
            )
        out_ref[brick] = summed


def weight_grad_kernel(grad_ref, padded_ref, out_ref):
    out_ref[...] = jnp.zeros(out_ref.shape, jnp.float32)
    for brick in range(padded_ref.shape[0]):
        whole = padded_ref[brick].astype(jnp.float32)
        grad_cells = grad_ref[brick]
        for tap_index in range(27):
            out_ref[tap_index] += lax.dot_general(
                grad_cells,
                tap_window(whole, tap_index),
                (((1,), (1,)), ((), ())),
                preferred_element_type=jnp.float32,
            )


def vmem_specs(count):
    return [pl.BlockSpec(memory_space=pltpu.VMEM)] * count


def conv_taps(padded, tap_major):
    slot_count, channels = (padded.shape[0], tap_major.shape[1])
    return pl.pallas_call(
        conv_kernel,
        out_shape=jax.ShapeDtypeStruct((slot_count, channels, grid_width), jnp.float32),
        in_specs=vmem_specs(2),
        out_specs=pl.BlockSpec(memory_space=pltpu.VMEM),
        cost_estimate=pl.CostEstimate(
            flops=2 * slot_count * 27 * channels * channels * grid_width,
            bytes_accessed=padded.size * 2 + tap_major.size * 2 + slot_count * channels * grid_width * 4,
            transcendentals=0,
        ),
    )(padded, tap_major)


def run_blocks(conv_fn, padded, weight_taps, live_count):
    return from_grid(conv_fn(padded, weight_taps))


def conv_forward(padded_block, weight_taps):
    return conv_taps(padded_block, jnp.transpose(weight_taps, (1, 0, 2)))


def conv_backward(padded_block, weight_taps):
    return conv_taps(padded_block, jnp.transpose(weight_taps[:, ::-1], (1, 2, 0)))


def accumulate(grad_cells, padded, live_count, channels):
    grad_grid = to_grid(grad_cells)
    slot_count = padded.shape[0]
    per_tap = pl.pallas_call(
        weight_grad_kernel,
        out_shape=jax.ShapeDtypeStruct((27, channels, channels), jnp.float32),
        in_specs=vmem_specs(2),
        out_specs=pl.BlockSpec(memory_space=pltpu.VMEM),
        cost_estimate=pl.CostEstimate(
            flops=2 * slot_count * 27 * channels * channels * grid_width,
            bytes_accessed=padded.size * 2 + grad_grid.size * 2 + 27 * channels * channels * 4,
            transcendentals=0,
        ),
    )(grad_grid, padded)
    return jnp.transpose(per_tap, (1, 0, 2))


MESH_AXES = ("space", "dp")
RING_AXES = (("core", 2), ("x", 4), ("y", 4), ("z", 4))


def chip_coords(space, dp):
    return {"core": space % 2, "x": dp % 4, "y": space // 2 % 4, "z": dp // 4 * 2 + space // 8}


def linear_of(coords):
    space = ((coords["z"] % 2) * 4 + coords["y"]) * 2 + coords["core"]
    return space * 8 + coords["z"] // 2 * 4 + coords["x"]


def ring_pairs(name, size, steps):
    result = []
    for space in range(16):
        for dp in range(8):
            coords = chip_coords(space, dp)
            moved = dict(coords)
            moved[name] = (coords[name] + steps) % size
            result.append((space * 8 + dp, linear_of(moved)))
    return result


def all_reduce_sum(flat):
    coords = chip_coords(lax.axis_index("space"), lax.axis_index("dp"))
    pieces = flat
    for name, size in RING_AXES:
        me = coords[name]
        chunks = pieces.reshape(size, pieces.shape[0] // size, pieces.shape[1])
        total = lax.dynamic_index_in_dim(chunks, me, 0, keepdims=False)
        for steps in range(1, size):
            outgoing = lax.dynamic_index_in_dim(chunks, (me + steps) % size, 0, keepdims=False)
            total = total + lax.ppermute(outgoing, MESH_AXES, ring_pairs(name, size, steps))
        pieces = total
    for name, size in reversed(RING_AXES):
        me = coords[name]
        stacked = jnp.zeros((size,) + pieces.shape, pieces.dtype)
        stacked = lax.dynamic_update_index_in_dim(stacked, pieces, me, 0)
        for steps in range(1, size):
            arrived = lax.ppermute(pieces, MESH_AXES, ring_pairs(name, size, steps))
            stacked = lax.dynamic_update_index_in_dim(stacked, arrived, (me - steps) % size, 0)
        pieces = stacked.reshape(size * pieces.shape[0], pieces.shape[1])
    return pieces


def share_grads(weight_sums, bias_sums):
    flat = jnp.concatenate([weight_sums.reshape(-1), bias_sums.reshape(-1)])
    rows = 4096
    padded = jnp.pad(flat, (0, rows * 128 - flat.shape[0])).reshape(rows, 128)
    summed = all_reduce_sum(padded).reshape(-1)
    weight_total = summed[: weight_sums.size].reshape(weight_sums.shape)
    bias_total = summed[weight_sums.size : flat.shape[0]].reshape(bias_sums.shape)
    return weight_total, bias_total


def silu_slope(values):
    sigma = jax.nn.sigmoid(values)
    return sigma * (1.0 + values * (1.0 - sigma))


def local(volume, neighbours, active, cotangent, weight_one, weight_two, bias_one, bias_two):
    slot_count, channels = (volume.shape[1], volume.shape[2])
    position = lax.axis_index("space")
    group_count = lax.axis_size("space")
    alive_all = active[0]
    alive_grid = alive_all.reshape(group_count, slot_count)
    live_rank = jnp.cumsum(alive_grid, axis=1) - 1
    dead_rank = jnp.sum(alive_grid, axis=1, keepdims=True) + jnp.cumsum(1 - alive_grid, axis=1) - 1
    place_flat = jnp.where(alive_grid > 0, live_rank, dead_rank).reshape(-1)
    compact_place = lax.dynamic_slice_in_dim(place_flat, position * slot_count, slot_count, 0)
    compact_order = (
        jnp.zeros((slot_count,), jnp.int32)
        .at[compact_place]
        .set(jnp.arange(slot_count, dtype=jnp.int32))
    )
    own_alive = lax.dynamic_slice_in_dim(alive_all, position * slot_count, slot_count, 0)
    live_count = jnp.sum(own_alive)
    near_table = lax.dynamic_slice_in_dim(neighbours[0], position * slot_count, slot_count, 0)
    near_table = jnp.take(near_table, compact_order, axis=0)
    safe_slot = jnp.maximum(near_table, 0)
    source_offset = safe_slot // slot_count - position + 3
    pool_rows = jnp.where(
        near_table < 0, 7 * slot_count, source_offset * slot_count + jnp.take(place_flat, safe_slot)
    )
    live_mask = (jnp.arange(slot_count) < live_count).astype(jnp.float32)[:, None, None]
    taps_one = weight_one.reshape(channels, 27, channels)
    taps_two = weight_two.reshape(channels, 27, channels)
    masked = jnp.take(volume[0], compact_order, axis=0) * live_mask.astype(jnp.bfloat16)
    padded_x = halo_pad(masked, pool_rows)
    hidden_pre = run_blocks(conv_forward, padded_x, taps_one, live_count) + bias_one[None, :, None]
    hidden = (jax.nn.silu(hidden_pre) * live_mask).astype(jnp.bfloat16)
    padded_h = halo_pad(hidden, pool_rows)
    out_pre = run_blocks(conv_forward, padded_h, taps_two, live_count) + bias_two[None, :, None]
    result = (jax.nn.silu(out_pre) * live_mask).astype(jnp.bfloat16)
    upstream = jnp.take(cotangent[0], compact_order, axis=0)
    grad_out = (upstream.astype(jnp.float32) * live_mask * silu_slope(out_pre)).astype(jnp.bfloat16)
    grad_w_two = accumulate(grad_out, padded_h, live_count, channels).reshape(
        channels, 27 * channels
    )
    grad_b_two = jnp.sum(grad_out.astype(jnp.float32), axis=(0, 2))
    padded_g = halo_pad(grad_out, pool_rows)
    hidden_grad = run_blocks(conv_backward, padded_g, taps_two, live_count)
    grad_hidden = (hidden_grad * live_mask * silu_slope(hidden_pre)).astype(jnp.bfloat16)
    grad_w_one = accumulate(grad_hidden, padded_x, live_count, channels).reshape(
        channels, 27 * channels
    )
    grad_b_one = jnp.sum(grad_hidden.astype(jnp.float32), axis=(0, 2))
    shared_all = share_grads(
        jnp.concatenate([grad_w_one, grad_w_two], axis=0),
        jnp.stack([grad_b_one, grad_b_two], axis=0),
    )
    total_w_one, total_w_two = (shared_all[0][:channels], shared_all[0][channels:])
    total_b_one, total_b_two = (shared_all[1][0], shared_all[1][1])
    output = jnp.take(result, compact_place, axis=0)[None]
    return (output, total_w_one, total_w_two, total_b_one, total_b_two)


def solution(mesh):
    in_specs = (
        P("dp", "space", None, None),
        P("dp", None, None),
        P("dp", None),
        P("dp", "space", None, None),
        P(),
        P(),
        P(),
        P(),
    )
    out_specs = (P("dp", "space", None, None), P(), P(), P(), P())
    return jax.shard_map(local, mesh=mesh, in_specs=in_specs, out_specs=out_specs, check_vma=False)
```

```python
import jax
import jax.numpy as jnp
from jax import lax
from jax.sharding import PartitionSpec as P
from jax.experimental import pallas as pl
from jax.experimental.pallas import tpu as pltpu

EDGE = 8


OFFSETS = [
    (a, b, c) for a in (-1, 0, 1) for b in (-1, 0, 1) for c in (-1, 0, 1) if (a, b, c) != (0, 0, 0)
]
brick_block = 4
grid_width = 896
flat_width = 1280


def shifted(value, axis, steps):
    count = lax.axis_size(axis)
    leading, last = (max(0, -steps), min(count, count - steps))
    return lax.ppermute(value, axis, [(source, source + steps) for source in range(leading, last)])


def collect_faces(bricks):
    edge_len = bricks.shape[-1]
    sides = [
        bricks[:, :, 0],
        bricks[:, :, edge_len - 1],
        bricks[:, :, :, 0],
        bricks[:, :, :, edge_len - 1],
        bricks[:, :, :, :, 0],
        bricks[:, :, :, :, edge_len - 1],
    ]
    stacked = jnp.stack(sides, axis=2)
    return stacked.reshape(bricks.shape[0], bricks.shape[1], 6 * edge_len * edge_len)


def face_index(offset):
    if offset[0] != 0:
        return 1 if offset[0] < 0 else 0
    if offset[1] != 0:
        return 3 if offset[1] < 0 else 2
    return 5 if offset[2] < 0 else 4


def face_span(shift_by, edge_len):
    if shift_by < 0:
        return slice(edge_len - 1, edge_len)
    if shift_by > 0:
        return slice(0, 1)
    return slice(0, edge_len)


def target(shift_by, edge_len):
    if shift_by < 0:
        return slice(0, 1)
    if shift_by > 0:
        return slice(edge_len + 1, edge_len + 2)
    return slice(1, edge_len + 1)


def build_pool(center):
    outer_faces = collect_faces(center)
    slot_count, channels, width = outer_faces.shape
    face_area = width // 6
    first_faces = outer_faces[:, :, : 2 * face_area]
    filler = jnp.zeros((slot_count, channels, width - 2 * face_area), outer_faces.dtype)
    received = {}
    for offset in (-1, 1):
        received[offset] = shifted(outer_faces, "space", -offset)
    for offset in (-3, -2, 2, 3):
        received[offset] = jnp.concatenate([shifted(first_faces, "space", -offset), filler], axis=2)
    received[0] = outer_faces
    zero_row = jnp.zeros((1, channels, width), outer_faces.dtype)
    return jnp.concatenate(
        [
            received[-3],
            received[-2],
            received[-1],
            received[0],
            received[1],
            received[2],
            received[3],
            zero_row,
        ],
        axis=0,
    )


def piece_source(pool, offset):
    a, b, c = offset
    rows, channels, edge_len = (pool.shape[0], pool.shape[1], EDGE)
    face = pool.reshape(rows, channels, 6, edge_len, edge_len)[:, :, face_index(offset)]
    if a != 0:
        part = face[:, :, face_span(b, edge_len), face_span(c, edge_len)]
    elif b != 0:
        part = face[:, :, :, face_span(c, edge_len)]
    else:
        part = face
    return part.reshape(rows, channels, -1)


def piece_extent(shift_by):
    return EDGE if shift_by == 0 else 1


def halo_pad(flat_bricks, pool_rows):
    slot_count, channels, cell_count = flat_bricks.shape
    center = flat_bricks.reshape(slot_count, channels, EDGE, EDGE, EDGE)
    pool = build_pool(center)
    rows = pool.shape[0]
    choose = (pool_rows[:, :, None] == jnp.arange(rows, dtype=jnp.int32)[None, None, :]).astype(pool.dtype)
    pieces = {(0, 0, 0): center}
    for nonzero in (1, 2, 3):
        group = [k for k, offset in enumerate(OFFSETS) if sum(v != 0 for v in offset) == nonzero]
        sources = jnp.stack([piece_source(pool, OFFSETS[k]) for k in group], axis=0)
        picks = jnp.stack([choose[:, k] for k in group], axis=0)
        gathered = jnp.einsum(
            "gjs,gscn->gjcn", picks, sources, preferred_element_type=jnp.float32
        ).astype(pool.dtype)
        for index, k in enumerate(group):
            a, b, c = OFFSETS[k]
            pieces[OFFSETS[k]] = gathered[index].reshape(
                slot_count, channels, piece_extent(a), piece_extent(b), piece_extent(c)
            )
    planes = []
    for a in (-1, 0, 1):
        lines = []
        for b in (-1, 0, 1):
            lines.append(jnp.concatenate([pieces[(a, b, c)] for c in (-1, 0, 1)], axis=4))
        planes.append(jnp.concatenate(lines, axis=3))
    padded = jnp.concatenate(planes, axis=2)
    side_total = (EDGE + 2) ** 3
    flat = padded.reshape(slot_count, channels, side_total)
    return jnp.pad(flat, ((0, 0), (0, 0), (0, flat_width - side_total)))


def tap_offset(tap_index):
    side = EDGE + 2
    return tap_index // 9 * side * side + tap_index // 3 % 3 * side + tap_index % 3


def to_grid(cells):
    slot_count, channels = (cells.shape[0], cells.shape[1])
    side = EDGE + 2
    shaped = cells.reshape(slot_count, channels, EDGE, EDGE, EDGE)
    shaped = jnp.pad(shaped, ((0, 0), (0, 0), (0, 0), (0, 2), (0, 2)))
    flat = shaped.reshape(slot_count, channels, EDGE * side * side)
    return jnp.pad(flat, ((0, 0), (0, 0), (0, grid_width - EDGE * side * side)))


def from_grid(grid_cells):
    slot_count, channels = (grid_cells.shape[0], grid_cells.shape[1])
    side = EDGE + 2
    shaped = grid_cells[:, :, : EDGE * side * side].reshape(slot_count, channels, EDGE, side, side)
    return shaped[:, :, :, :EDGE, :EDGE].reshape(slot_count, channels, EDGE**3)


def conv_forward(padded_block, weight_taps):
    summed = jnp.zeros((padded_block.shape[0], weight_taps.shape[0], grid_width), jnp.float32)
    for tap_index in range(27):
        start = tap_offset(tap_index)
        piece_cells = padded_block[:, :, start : start + grid_width]
        summed = summed + jnp.einsum(
            "oi,kip->kop",
            weight_taps[:, tap_index],
            piece_cells,
            preferred_element_type=jnp.float32,
        )
    return summed


def conv_backward(padded_block, weight_taps):
    summed = jnp.zeros((padded_block.shape[0], weight_taps.shape[2], grid_width), jnp.float32)
    for tap_index in range(27):
        start = tap_offset(tap_index)
        piece_cells = padded_block[:, :, start : start + grid_width]
        summed = summed + jnp.einsum(
            "oi,kop->kip",
            weight_taps[:, 26 - tap_index],
            piece_cells,
            preferred_element_type=jnp.float32,
        )
    return summed


def tap_window(whole, tap_index):
    start = tap_offset(tap_index)
    if start:
        whole = pltpu.roll(whole, flat_width - start, 1)
    return whole[:, :grid_width].astype(jnp.bfloat16)


def conv_kernel(padded_ref, taps_ref, out_ref):
    for brick in range(padded_ref.shape[0]):
        whole = padded_ref[brick].astype(jnp.float32)
        summed = jnp.zeros(out_ref.shape[1:], jnp.float32)
        for tap_index in range(27):
            summed = summed + jnp.dot(
                taps_ref[tap_index],
                tap_window(whole, tap_index),
                preferred_element_type=jnp.float32,
            )
        out_ref[brick] = summed


def weight_grad_kernel(grad_ref, padded_ref, out_ref):
    out_ref[...] = jnp.zeros(out_ref.shape, jnp.float32)
    for brick in range(padded_ref.shape[0]):
        whole = padded_ref[brick].astype(jnp.float32)
        grad_cells = grad_ref[brick]
        for tap_index in range(27):
            out_ref[tap_index] += lax.dot_general(
                grad_cells,
                tap_window(whole, tap_index),
                (((1,), (1,)), ((), ())),
                preferred_element_type=jnp.float32,
            )


def vmem_specs(count):
    return [pl.BlockSpec(memory_space=pltpu.VMEM)] * count


def conv_taps(padded, tap_major):
    slot_count, channels = (padded.shape[0], tap_major.shape[1])
    return pl.pallas_call(
        conv_kernel,
        out_shape=jax.ShapeDtypeStruct((slot_count, channels, grid_width), jnp.float32),
        in_specs=vmem_specs(2),
        out_specs=pl.BlockSpec(memory_space=pltpu.VMEM),
        cost_estimate=pl.CostEstimate(
            flops=2 * slot_count * 27 * channels * channels * grid_width,
            bytes_accessed=padded.size * 2 + tap_major.size * 2 + slot_count * channels * grid_width * 4,
            transcendentals=0,
        ),
    )(padded, tap_major)


def run_blocks(conv_fn, padded, weight_taps, live_count):
    return from_grid(conv_fn(padded, weight_taps))


def conv_forward(padded_block, weight_taps):
    return conv_taps(padded_block, jnp.transpose(weight_taps, (1, 0, 2)))


def conv_backward(padded_block, weight_taps):
    return conv_taps(padded_block, jnp.transpose(weight_taps[:, ::-1], (1, 2, 0)))


def accumulate(grad_cells, padded, live_count, channels):
    grad_grid = to_grid(grad_cells)
    slot_count = padded.shape[0]
    per_tap = pl.pallas_call(
        weight_grad_kernel,
        out_shape=jax.ShapeDtypeStruct((27, channels, channels), jnp.float32),
        in_specs=vmem_specs(2),
        out_specs=pl.BlockSpec(memory_space=pltpu.VMEM),
        cost_estimate=pl.CostEstimate(
            flops=2 * slot_count * 27 * channels * channels * grid_width,
            bytes_accessed=padded.size * 2 + grad_grid.size * 2 + 27 * channels * channels * 4,
            transcendentals=0,
        ),
    )(grad_grid, padded)
    return jnp.transpose(per_tap, (1, 0, 2))


MESH_AXES = ("space", "dp")
RING_AXES = (("core", 2), ("x", 4), ("y", 4), ("z", 4))


def chip_coords(space, dp):
    return {"core": space % 2, "x": dp % 4, "y": space // 2 % 4, "z": dp // 4 * 2 + space // 8}


def linear_of(coords):
    space = ((coords["z"] % 2) * 4 + coords["y"]) * 2 + coords["core"]
    return space * 8 + coords["z"] // 2 * 4 + coords["x"]


def ring_pairs(name, size, steps):
    result = []
    for space in range(16):
        for dp in range(8):
            coords = chip_coords(space, dp)
            moved = dict(coords)
            moved[name] = (coords[name] + steps) % size
            result.append((space * 8 + dp, linear_of(moved)))
    return result


def all_reduce_sum(flat):
    coords = chip_coords(lax.axis_index("space"), lax.axis_index("dp"))
    pieces = flat
    for name, size in RING_AXES:
        me = coords[name]
        chunks = pieces.reshape(size, pieces.shape[0] // size, pieces.shape[1])
        total = lax.dynamic_index_in_dim(chunks, me, 0, keepdims=False)
        for steps in range(1, size):
            outgoing = lax.dynamic_index_in_dim(chunks, (me + steps) % size, 0, keepdims=False)
            total = total + lax.ppermute(outgoing, MESH_AXES, ring_pairs(name, size, steps))
        pieces = total
    for name, size in reversed(RING_AXES):
        me = coords[name]
        stacked = jnp.zeros((size,) + pieces.shape, pieces.dtype)
        stacked = lax.dynamic_update_index_in_dim(stacked, pieces, me, 0)
        for steps in range(1, size):
            arrived = lax.ppermute(pieces, MESH_AXES, ring_pairs(name, size, steps))
            stacked = lax.dynamic_update_index_in_dim(stacked, arrived, (me - steps) % size, 0)
        pieces = stacked.reshape(size * pieces.shape[0], pieces.shape[1])
    return pieces


def share_grads(weight_sums, bias_sums):
    flat = jnp.concatenate([weight_sums.reshape(-1), bias_sums.reshape(-1)])
    rows = 4096
    padded = jnp.pad(flat, (0, rows * 128 - flat.shape[0])).reshape(rows, 128)
    summed = all_reduce_sum(padded).reshape(-1)
    weight_total = summed[: weight_sums.size].reshape(weight_sums.shape)
    bias_total = summed[weight_sums.size : flat.shape[0]].reshape(bias_sums.shape)
    return weight_total, bias_total


def silu_slope(values):
    sigma = jax.nn.sigmoid(values)
    return sigma * (1.0 + values * (1.0 - sigma))


def local(volume, neighbours, active, cotangent, weight_one, weight_two, bias_one, bias_two):
    slot_count, channels = (volume.shape[1], volume.shape[2])
    position = lax.axis_index("space")
    own_alive = lax.dynamic_slice_in_dim(active[0], position * slot_count, slot_count, 0)
    live_count = jnp.sum(own_alive)
    near_table = lax.dynamic_slice_in_dim(neighbours[0], position * slot_count, slot_count, 0)
    safe_slot = jnp.maximum(near_table, 0)
    source_offset = safe_slot // slot_count - position + 3
    pool_rows = jnp.where(
        near_table < 0, 7 * slot_count, source_offset * slot_count + safe_slot % slot_count
    )
    live_mask = own_alive.astype(jnp.float32)[:, None, None]
    taps_one = weight_one.reshape(channels, 27, channels)
    taps_two = weight_two.reshape(channels, 27, channels)
    masked = volume[0] * live_mask.astype(jnp.bfloat16)
    padded_x = halo_pad(masked, pool_rows)
    hidden_pre = run_blocks(conv_forward, padded_x, taps_one, live_count) + bias_one[None, :, None]
    hidden = (jax.nn.silu(hidden_pre) * live_mask).astype(jnp.bfloat16)
    padded_h = halo_pad(hidden, pool_rows)
    out_pre = run_blocks(conv_forward, padded_h, taps_two, live_count) + bias_two[None, :, None]
    result = (jax.nn.silu(out_pre) * live_mask).astype(jnp.bfloat16)
    upstream = cotangent[0]
    grad_out = (upstream.astype(jnp.float32) * live_mask * silu_slope(out_pre)).astype(jnp.bfloat16)
    grad_w_two = accumulate(grad_out, padded_h, live_count, channels).reshape(
        channels, 27 * channels
    )
    grad_b_two = jnp.sum(grad_out.astype(jnp.float32), axis=(0, 2))
    padded_g = halo_pad(grad_out, pool_rows)
    hidden_grad = run_blocks(conv_backward, padded_g, taps_two, live_count)
    grad_hidden = (hidden_grad * live_mask * silu_slope(hidden_pre)).astype(jnp.bfloat16)
    grad_w_one = accumulate(grad_hidden, padded_x, live_count, channels).reshape(
        channels, 27 * channels
    )
    grad_b_one = jnp.sum(grad_hidden.astype(jnp.float32), axis=(0, 2))
    shared_all = share_grads(
        jnp.concatenate([grad_w_one, grad_w_two], axis=0),
        jnp.stack([grad_b_one, grad_b_two], axis=0),
    )
    total_w_one, total_w_two = (shared_all[0][:channels], shared_all[0][channels:])
    total_b_one, total_b_two = (shared_all[1][0], shared_all[1][1])
    output = result[None]
    return (output, total_w_one, total_w_two, total_b_one, total_b_two)


def solution(mesh):
    in_specs = (
        P("dp", "space", None, None),
        P("dp", None, None),
        P("dp", None),
        P("dp", "space", None, None),
        P(),
        P(),
        P(),
        P(),
    )
    out_specs = (P("dp", "space", None, None), P(), P(), P(), P())
    return jax.shard_map(local, mesh=mesh, in_specs=in_specs, out_specs=out_specs, check_vma=False)
```

```python
import jax
import numpy as np
import jax.numpy as jnp
from jax import lax
from jax.sharding import PartitionSpec as P
from jax.experimental import pallas as pl
from jax.experimental.pallas import tpu as pltpu

EDGE = 8


OFFSETS = [
    (a, b, c) for a in (-1, 0, 1) for b in (-1, 0, 1) for c in (-1, 0, 1) if (a, b, c) != (0, 0, 0)
]
grid_width = 896
flat_width = 1280


def shifted(value, axis, steps):
    count = lax.axis_size(axis)
    leading, last = (max(0, -steps), min(count, count - steps))
    return lax.ppermute(value, axis, [(source, source + steps) for source in range(leading, last)])


def face_index(offset):
    if offset[0] != 0:
        return 1 if offset[0] < 0 else 0
    if offset[1] != 0:
        return 3 if offset[1] < 0 else 2
    return 5 if offset[2] < 0 else 4


def face_span(shift_by, edge_len):
    if shift_by < 0:
        return slice(edge_len - 1, edge_len)
    if shift_by > 0:
        return slice(0, 1)
    return slice(0, edge_len)


def target(shift_by, edge_len):
    if shift_by < 0:
        return slice(0, 1)
    if shift_by > 0:
        return slice(edge_len + 1, edge_len + 2)
    return slice(1, edge_len + 1)


def grid_at(p, q, r):
    return p * (EDGE + 2) ** 2 + q * (EDGE + 2) + r


def face_cells():
    last = EDGE - 1
    cells = []
    for fixed_axis in range(3):
        for fixed_at in (0, last):
            for u in range(EDGE):
                for w in range(EDGE):
                    spot = [u, w]
                    spot.insert(fixed_axis, fixed_at)
                    cells.append(grid_at(*spot))
    return np.array(cells, np.int32)


def piece_layout():
    sources, targets, groups = [], [], []
    face_area = EDGE * EDGE
    for nonzero in (1, 2, 3):
        for k, offset in enumerate(OFFSETS):
            if sum(v != 0 for v in offset) != nonzero:
                continue
            a, b, c = offset
            base = face_index(offset) * face_area
            face = np.arange(base, base + face_area).reshape(EDGE, EDGE)
            if a != 0:
                part = face[face_span(b, EDGE), face_span(c, EDGE)]
            elif b != 0:
                part = face[:, face_span(c, EDGE)]
            else:
                part = face
            sources.extend(part.reshape(-1).tolist())
            groups.extend([k] * part.size)
            for pp in range(EDGE + 2)[target(a, EDGE)]:
                for qq in range(EDGE + 2)[target(b, EDGE)]:
                    for rr in range(EDGE + 2)[target(c, EDGE)]:
                        targets.append(grid_at(pp, qq, rr))
    return np.array(sources, np.int32), np.array(targets, np.int32), np.array(groups, np.int32)


def cell_grid():
    return np.array(
        [grid_at(p, q, r) for p in range(EDGE) for q in range(EDGE) for r in range(EDGE)], np.int32
    )


def one_hot(rows, columns):
    return (jnp.asarray(rows)[:, None] == jnp.asarray(columns)[None, :]).astype(jnp.bfloat16)


def placement():
    grid_ids = jnp.arange(grid_width, dtype=jnp.int32)
    cells = jnp.asarray(cell_grid())
    valid = jnp.zeros((grid_width,), jnp.int32).at[cells].set(1)
    center_target = jnp.where(valid > 0, grid_ids + grid_at(1, 1, 1), -1)
    from_center = one_hot(center_target, jnp.arange(flat_width, dtype=jnp.int32))
    piece_sources, piece_targets, piece_groups = piece_layout()
    from_pieces = one_hot(piece_targets, jnp.arange(flat_width, dtype=jnp.int32))
    return from_center, from_pieces


def exact_dot(left, right, spec):
    return jnp.einsum(spec, left, right, preferred_element_type=jnp.float32).astype(left.dtype)


def padded_whole(grid_ref, piece_ref, center_ref, halo_ref, brick):
    whole = jnp.dot(grid_ref[brick], center_ref[...], preferred_element_type=jnp.float32)
    return whole + jnp.dot(piece_ref[brick], halo_ref[...], preferred_element_type=jnp.float32)


def stacked_windows(whole):
    windows = []
    for b in range(3):
        for c in range(3):
            start = b * (EDGE + 2) + c
            moved = whole if start == 0 else pltpu.roll(whole, flat_width - start, 1)
            windows.append(moved.astype(jnp.bfloat16))
    return jnp.concatenate(windows, axis=0)


def conv_kernel(grid_ref, piece_ref, center_ref, halo_ref, taps_ref, out_ref):
    plane = (EDGE + 2) ** 2
    depth = taps_ref.shape[1] // 3

    def one_brick(brick, carry):
        windows = stacked_windows(padded_whole(grid_ref, piece_ref, center_ref, halo_ref, brick))
        summed = None
        for a in range(3):
            product = jnp.dot(
                taps_ref[:, a * depth : (a + 1) * depth], windows, preferred_element_type=jnp.float32
            )
            if a:
                product = pltpu.roll(product, flat_width - a * plane, 1)
            summed = product if summed is None else summed + product
        out_ref[brick] = summed[:, :grid_width]
        return carry

    lax.fori_loop(0, grid_ref.shape[0], one_brick, 0)


def weight_grad_kernel(grad_ref, grid_ref, piece_ref, center_ref, halo_ref, out_ref):
    plane = (EDGE + 2) ** 2
    depth = out_ref.shape[1] // 3
    out_ref[...] = jnp.zeros(out_ref.shape, jnp.float32)

    def one_brick(brick, carry):
        windows = stacked_windows(padded_whole(grid_ref, piece_ref, center_ref, halo_ref, brick))
        grad_cells = grad_ref[brick].astype(jnp.float32)
        grad_wide = jnp.concatenate(
            [grad_cells, jnp.zeros((grad_cells.shape[0], flat_width - grid_width), jnp.float32)],
            axis=1,
        )
        for a in range(3):
            moved = grad_wide if a == 0 else pltpu.roll(grad_wide, a * plane, 1)
            out_ref[:, a * depth : (a + 1) * depth] += lax.dot_general(
                moved.astype(jnp.bfloat16),
                windows,
                (((1,), (1,)), ((), ())),
                preferred_element_type=jnp.float32,
            )
        return carry

    lax.fori_loop(0, grid_ref.shape[0], one_brick, 0)


def vmem_specs(count):
    return [pl.BlockSpec(memory_space=pltpu.VMEM)] * count


def conv_grid(grid_cells, pieces, place, weight_rows):
    slot_count, channels = (grid_cells.shape[0], weight_rows.shape[0])
    return pl.pallas_call(
        conv_kernel,
        out_shape=jax.ShapeDtypeStruct((slot_count, channels, grid_width), jnp.float32),
        in_specs=vmem_specs(5),
        out_specs=pl.BlockSpec(memory_space=pltpu.VMEM),
        cost_estimate=pl.CostEstimate(
            flops=2 * slot_count * channels * flat_width * (weight_rows.shape[1] + 1400),
            bytes_accessed=grid_cells.size * 2 + pieces.size * 2 + 3 * 2**20 + slot_count * channels * grid_width * 4,
            transcendentals=0,
        ),
    )(grid_cells, pieces, place[0], place[1], weight_rows)


def weight_grad(grad_cells, grid_cells, pieces, place):
    slot_count, channels = (grid_cells.shape[0], grid_cells.shape[1])
    return pl.pallas_call(
        weight_grad_kernel,
        out_shape=jax.ShapeDtypeStruct((channels, 27 * channels), jnp.float32),
        in_specs=vmem_specs(5),
        out_specs=pl.BlockSpec(memory_space=pltpu.VMEM),
        cost_estimate=pl.CostEstimate(
            flops=2 * slot_count * channels * flat_width * (27 * channels + 1400),
            bytes_accessed=grid_cells.size * 4 + pieces.size * 2 + 3 * 2**20 + 27 * channels * channels * 4,
            transcendentals=0,
        ),
    )(grad_cells, grid_cells, pieces, place[0], place[1])


def build_pool(outer_faces):
    slot_count, channels, width = outer_faces.shape
    face_area = width // 6
    first_faces = outer_faces[:, :, : 2 * face_area]
    filler = jnp.zeros((slot_count, channels, width - 2 * face_area), outer_faces.dtype)
    received = {}
    for offset in (-1, 1):
        received[offset] = shifted(outer_faces, "space", -offset)
    for offset in (-3, -2, 2, 3):
        received[offset] = jnp.concatenate([shifted(first_faces, "space", -offset), filler], axis=2)
    received[0] = outer_faces
    zero_row = jnp.zeros((1, channels, width), outer_faces.dtype)
    return jnp.concatenate([received[k] for k in (-3, -2, -1, 0, 1, 2, 3)] + [zero_row], axis=0)


def halo_pieces(grid_cells, pool_rows):
    faces = exact_dot(grid_cells, one_hot(jnp.arange(grid_width, dtype=jnp.int32), face_cells()), "scg,gf->scf")
    pool = build_pool(faces)
    rows = pool.shape[0]
    piece_sources, piece_targets, piece_groups = piece_layout()
    table = exact_dot(pool, one_hot(jnp.arange(faces.shape[2], dtype=jnp.int32), piece_sources), "scf,fe->sce")
    chosen = jnp.take(pool_rows, jnp.asarray(piece_groups), axis=1)
    pick = (chosen[:, None, :] == jnp.arange(rows, dtype=jnp.int32)[None, :, None]).astype(jnp.float32)
    picked = jnp.sum(pick[:, :, None, :] * table.astype(jnp.float32)[None], axis=1)
    return picked.astype(grid_cells.dtype)


MESH_AXES = ("space", "dp")
RING_AXES = (("core", 2), ("x", 4), ("y", 4), ("z", 4))


def chip_coords(space, dp):
    return {"core": space % 2, "x": dp % 4, "y": space // 2 % 4, "z": dp // 4 * 2 + space // 8}


def linear_of(coords):
    space = ((coords["z"] % 2) * 4 + coords["y"]) * 2 + coords["core"]
    return space * 8 + coords["z"] // 2 * 4 + coords["x"]


def ring_pairs(name, size, steps):
    result = []
    for space in range(16):
        for dp in range(8):
            coords = chip_coords(space, dp)
            moved = dict(coords)
            moved[name] = (coords[name] + steps) % size
            result.append((space * 8 + dp, linear_of(moved)))
    return result


def all_reduce_sum(flat):
    coords = chip_coords(lax.axis_index("space"), lax.axis_index("dp"))
    pieces = flat
    for name, size in RING_AXES:
        me = coords[name]
        chunks = pieces.reshape(size, pieces.shape[0] // size, pieces.shape[1])
        total = lax.dynamic_index_in_dim(chunks, me, 0, keepdims=False)
        for steps in range(1, size):
            outgoing = lax.dynamic_index_in_dim(chunks, (me + steps) % size, 0, keepdims=False)
            total = total + lax.ppermute(outgoing, MESH_AXES, ring_pairs(name, size, steps))
        pieces = total
    for name, size in reversed(RING_AXES):
        me = coords[name]
        stacked = jnp.zeros((size,) + pieces.shape, pieces.dtype)
        stacked = lax.dynamic_update_index_in_dim(stacked, pieces, me, 0)
        for steps in range(1, size):
            arrived = lax.ppermute(pieces, MESH_AXES, ring_pairs(name, size, steps))
            stacked = lax.dynamic_update_index_in_dim(stacked, arrived, (me - steps) % size, 0)
        pieces = stacked.reshape(size * pieces.shape[0], pieces.shape[1])
    return pieces


def share_grads(weight_sums, bias_sums):
    flat = jnp.concatenate([weight_sums.reshape(-1), bias_sums.reshape(-1)])
    rows = 4096
    padded = jnp.pad(flat, (0, rows * 128 - flat.shape[0])).reshape(rows, 128)
    summed = all_reduce_sum(padded).reshape(-1)
    weight_total = summed[: weight_sums.size].reshape(weight_sums.shape)
    bias_total = summed[weight_sums.size : flat.shape[0]].reshape(bias_sums.shape)
    return weight_total, bias_total


def silu_slope(values):
    sigma = jax.nn.sigmoid(values)
    return sigma * (1.0 + values * (1.0 - sigma))


def local(volume, neighbours, active, cotangent, weight_one, weight_two, bias_one, bias_two):
    slot_count, channels = (volume.shape[1], volume.shape[2])
    position = lax.axis_index("space")
    own_alive = lax.dynamic_slice_in_dim(active[0], position * slot_count, slot_count, 0)
    near_table = lax.dynamic_slice_in_dim(neighbours[0], position * slot_count, slot_count, 0)
    safe_slot = jnp.maximum(near_table, 0)
    source_offset = safe_slot // slot_count - position + 3
    pool_rows = jnp.where(
        near_table < 0, 7 * slot_count, source_offset * slot_count + safe_slot % slot_count
    )
    live_mask = own_alive.astype(jnp.float32)[:, None, None]
    cells = jnp.asarray(cell_grid())
    to_cells = one_hot(jnp.arange(grid_width, dtype=jnp.int32), cells)
    valid = jnp.zeros((grid_width,), jnp.float32).at[cells].set(1.0)
    place = placement()
    back_rows = jnp.transpose(
        weight_two.reshape(channels, 27, channels)[:, ::-1, :], (2, 1, 0)
    ).reshape(channels, 27 * channels)
    masked = volume[0] * live_mask.astype(jnp.bfloat16)
    masked_grid = exact_dot(masked, to_cells, "scn,gn->scg")
    pieces_x = halo_pieces(masked_grid, pool_rows)
    hidden_pre = conv_grid(masked_grid, pieces_x, place, weight_one) + bias_one[None, :, None]
    hidden = (jax.nn.silu(hidden_pre) * live_mask).astype(jnp.bfloat16)
    pieces_h = halo_pieces(hidden, pool_rows)
    out_pre = conv_grid(hidden, pieces_h, place, weight_two) + bias_two[None, :, None]
    result = (jax.nn.silu(out_pre) * live_mask).astype(jnp.bfloat16)
    upstream = exact_dot(cotangent[0], to_cells, "scn,gn->scg")
    grad_out = (upstream.astype(jnp.float32) * live_mask * silu_slope(out_pre)).astype(jnp.bfloat16)
    grad_w_two = weight_grad(grad_out, hidden, pieces_h, place)
    grad_b_two = jnp.sum(grad_out.astype(jnp.float32), axis=(0, 2))
    pieces_g = halo_pieces(grad_out, pool_rows)
    hidden_grad = conv_grid(grad_out, pieces_g, place, back_rows)
    grad_hidden = (hidden_grad * (live_mask * valid) * silu_slope(hidden_pre)).astype(jnp.bfloat16)
    grad_w_one = weight_grad(grad_hidden, masked_grid, pieces_x, place)
    grad_b_one = jnp.sum(grad_hidden.astype(jnp.float32), axis=(0, 2))
    shared_all = share_grads(
        jnp.concatenate([grad_w_one, grad_w_two], axis=0),
        jnp.stack([grad_b_one, grad_b_two], axis=0),
    )
    total_w_one, total_w_two = (shared_all[0][:channels], shared_all[0][channels:])
    total_b_one, total_b_two = (shared_all[1][0], shared_all[1][1])
    output = exact_dot(result, to_cells, "scg,gn->scn")[None]
    return (output, total_w_one, total_w_two, total_b_one, total_b_two)


def solution(mesh):
    in_specs = (
        P("dp", "space", None, None),
        P("dp", None, None),
        P("dp", None),
        P("dp", "space", None, None),
        P(),
        P(),
        P(),
        P(),
    )
    out_specs = (P("dp", "space", None, None), P(), P(), P(), P())
    return jax.shard_map(local, mesh=mesh, in_specs=in_specs, out_specs=out_specs, check_vma=False)
```

```python
import jax
import numpy as np
import jax.numpy as jnp
from jax import lax
from jax.sharding import PartitionSpec as P
from jax.experimental import pallas as pl
from jax.experimental.pallas import tpu as pltpu

EDGE = 8


OFFSETS = [
    (a, b, c) for a in (-1, 0, 1) for b in (-1, 0, 1) for c in (-1, 0, 1) if (a, b, c) != (0, 0, 0)
]
grid_width = 896
flat_width = 1280


def shifted(value, axis, steps):
    count = lax.axis_size(axis)
    leading, last = (max(0, -steps), min(count, count - steps))
    return lax.ppermute(value, axis, [(source, source + steps) for source in range(leading, last)])


def face_index(offset):
    if offset[0] != 0:
        return 1 if offset[0] < 0 else 0
    if offset[1] != 0:
        return 3 if offset[1] < 0 else 2
    return 5 if offset[2] < 0 else 4


def face_span(shift_by, edge_len):
    if shift_by < 0:
        return slice(edge_len - 1, edge_len)
    if shift_by > 0:
        return slice(0, 1)
    return slice(0, edge_len)


def target(shift_by, edge_len):
    if shift_by < 0:
        return slice(0, 1)
    if shift_by > 0:
        return slice(edge_len + 1, edge_len + 2)
    return slice(1, edge_len + 1)


def grid_at(p, q, r):
    return p * (EDGE + 2) ** 2 + q * (EDGE + 2) + r


def face_cells():
    last = EDGE - 1
    cells = []
    for fixed_axis in range(3):
        for fixed_at in (0, last):
            for u in range(EDGE):
                for w in range(EDGE):
                    spot = [u, w]
                    spot.insert(fixed_axis, fixed_at)
                    cells.append(grid_at(*spot))
    return np.array(cells, np.int32)


def piece_layout():
    sources, targets, groups = [], [], []
    face_area = EDGE * EDGE
    for nonzero in (1, 2, 3):
        for k, offset in enumerate(OFFSETS):
            if sum(v != 0 for v in offset) != nonzero:
                continue
            a, b, c = offset
            base = face_index(offset) * face_area
            face = np.arange(base, base + face_area).reshape(EDGE, EDGE)
            if a != 0:
                part = face[face_span(b, EDGE), face_span(c, EDGE)]
            elif b != 0:
                part = face[:, face_span(c, EDGE)]
            else:
                part = face
            sources.extend(part.reshape(-1).tolist())
            groups.extend([k] * part.size)
            for pp in range(EDGE + 2)[target(a, EDGE)]:
                for qq in range(EDGE + 2)[target(b, EDGE)]:
                    for rr in range(EDGE + 2)[target(c, EDGE)]:
                        targets.append(grid_at(pp, qq, rr))
    return np.array(sources, np.int32), np.array(targets, np.int32), np.array(groups, np.int32)


def cell_grid():
    return np.array(
        [grid_at(p, q, r) for p in range(EDGE) for q in range(EDGE) for r in range(EDGE)], np.int32
    )


def one_hot(rows, columns):
    return (jnp.asarray(rows)[:, None] == jnp.asarray(columns)[None, :]).astype(jnp.bfloat16)


def placement():
    grid_ids = jnp.arange(grid_width, dtype=jnp.int32)
    cells = jnp.asarray(cell_grid())
    valid = jnp.zeros((grid_width,), jnp.int32).at[cells].set(1)
    center_target = jnp.where(valid > 0, grid_ids + grid_at(1, 1, 1), -1)
    from_center = one_hot(center_target, jnp.arange(flat_width, dtype=jnp.int32))
    piece_sources, piece_targets, piece_groups = piece_layout()
    from_pieces = one_hot(piece_targets, jnp.arange(flat_width, dtype=jnp.int32))
    return from_center, from_pieces


def exact_dot(left, right, spec):
    return jnp.einsum(spec, left, right, preferred_element_type=jnp.float32).astype(left.dtype)


def padded_whole(grid_ref, piece_ref, center_ref, halo_ref, brick):
    whole = jnp.dot(grid_ref[brick], center_ref[...], preferred_element_type=jnp.float32)
    return whole + jnp.dot(piece_ref[brick], halo_ref[...], preferred_element_type=jnp.float32)


def stacked_windows(whole):
    windows = []
    for b in range(3):
        for c in range(3):
            start = b * (EDGE + 2) + c
            moved = whole if start == 0 else pltpu.roll(whole, flat_width - start, 1)
            windows.append(moved.astype(jnp.bfloat16))
    return jnp.concatenate(windows, axis=0)


def conv_kernel(grid_ref, piece_ref, center_ref, halo_ref, taps_ref, out_ref):
    plane = (EDGE + 2) ** 2
    depth = taps_ref.shape[1] // 3

    def one_brick(brick, carry):
        windows = stacked_windows(padded_whole(grid_ref, piece_ref, center_ref, halo_ref, brick))
        summed = None
        for a in range(3):
            product = jnp.dot(
                taps_ref[:, a * depth : (a + 1) * depth], windows, preferred_element_type=jnp.float32
            )
            if a:
                product = pltpu.roll(product, flat_width - a * plane, 1)
            summed = product if summed is None else summed + product
        out_ref[brick] = summed[:, :grid_width]
        return carry

    lax.fori_loop(0, grid_ref.shape[0], one_brick, 0)


def weight_grad_kernel(grad_ref, grid_ref, piece_ref, center_ref, halo_ref, out_ref):
    plane = (EDGE + 2) ** 2
    depth = out_ref.shape[1] // 3
    out_ref[...] = jnp.zeros(out_ref.shape, jnp.float32)

    def one_brick(brick, carry):
        windows = stacked_windows(padded_whole(grid_ref, piece_ref, center_ref, halo_ref, brick))
        grad_cells = grad_ref[brick].astype(jnp.float32)
        grad_wide = jnp.concatenate(
            [grad_cells, jnp.zeros((grad_cells.shape[0], flat_width - grid_width), jnp.float32)],
            axis=1,
        )
        for a in range(3):
            moved = grad_wide if a == 0 else pltpu.roll(grad_wide, a * plane, 1)
            out_ref[:, a * depth : (a + 1) * depth] += lax.dot_general(
                moved.astype(jnp.bfloat16),
                windows,
                (((1,), (1,)), ((), ())),
                preferred_element_type=jnp.float32,
            )
        return carry

    lax.fori_loop(0, grid_ref.shape[0], one_brick, 0)


def vmem_specs(count):
    return [pl.BlockSpec(memory_space=pltpu.VMEM)] * count


def conv_grid(grid_cells, pieces, place, weight_rows):
    slot_count, channels = (grid_cells.shape[0], weight_rows.shape[0])
    return pl.pallas_call(
        conv_kernel,
        out_shape=jax.ShapeDtypeStruct((slot_count, channels, grid_width), jnp.float32),
        in_specs=vmem_specs(5),
        out_specs=pl.BlockSpec(memory_space=pltpu.VMEM),
        cost_estimate=pl.CostEstimate(
            flops=2 * slot_count * channels * flat_width * (weight_rows.shape[1] + 1400),
            bytes_accessed=grid_cells.size * 2 + pieces.size * 2 + 3 * 2**20 + slot_count * channels * grid_width * 4,
            transcendentals=0,
        ),
    )(grid_cells, pieces, place[0], place[1], weight_rows)


def weight_grad(grad_cells, grid_cells, pieces, place):
    slot_count, channels = (grid_cells.shape[0], grid_cells.shape[1])
    return pl.pallas_call(
        weight_grad_kernel,
        out_shape=jax.ShapeDtypeStruct((channels, 27 * channels), jnp.float32),
        in_specs=vmem_specs(5),
        out_specs=pl.BlockSpec(memory_space=pltpu.VMEM),
        cost_estimate=pl.CostEstimate(
            flops=2 * slot_count * channels * flat_width * (27 * channels + 1400),
            bytes_accessed=grid_cells.size * 4 + pieces.size * 2 + 3 * 2**20 + 27 * channels * channels * 4,
            transcendentals=0,
        ),
    )(grad_cells, grid_cells, pieces, place[0], place[1])


def build_pool(outer_faces):
    slot_count, channels, width = outer_faces.shape
    face_area = width // 6
    first_faces = outer_faces[:, :, : 2 * face_area]
    filler = jnp.zeros((slot_count, channels, width - 2 * face_area), outer_faces.dtype)
    received = {}
    for offset in (-1, 1):
        received[offset] = shifted(outer_faces, "space", -offset)
    for offset in (-3, -2, 2, 3):
        received[offset] = jnp.concatenate([shifted(first_faces, "space", -offset), filler], axis=2)
    received[0] = outer_faces
    zero_row = jnp.zeros((1, channels, width), outer_faces.dtype)
    return jnp.concatenate([received[k] for k in (-3, -2, -1, 0, 1, 2, 3)] + [zero_row], axis=0)


def halo_pieces(grid_cells, pool_rows):
    faces = exact_dot(grid_cells, one_hot(jnp.arange(grid_width, dtype=jnp.int32), face_cells()), "scg,gf->scf")
    pool = build_pool(faces)
    rows = pool.shape[0]
    piece_sources, piece_targets, piece_groups = piece_layout()
    table = exact_dot(pool, one_hot(jnp.arange(faces.shape[2], dtype=jnp.int32), piece_sources), "scf,fe->sce")
    chosen = jnp.take(pool_rows, jnp.asarray(piece_groups), axis=1)
    pick = (chosen[:, None, :] == jnp.arange(rows, dtype=jnp.int32)[None, :, None]).astype(jnp.float32)
    picked = jnp.sum(pick[:, :, None, :] * table.astype(jnp.float32)[None], axis=1)
    return picked.astype(grid_cells.dtype)


REDUCE_STAGES = (("core", 2), ("x", 4), ("y", 4), ("z", 4))


def own_coords():
    space = lax.axis_index("space")
    dp = lax.axis_index("dp")
    return {"core": space % 2, "x": dp % 4, "y": space // 2 % 4, "z": dp // 4 * 2 + space // 8}


def mesh_id(coords, name, value):
    moved = dict(coords)
    moved[name] = value
    space = ((moved["z"] % 2) * 4 + moved["y"]) * 2 + moved["core"]
    return (space, moved["z"] // 2 * 4 + moved["x"])


def all_reduce_kernel(*refs):
    x_ref, out_ref = refs[0], refs[1]
    rest = refs[2:]
    sums = rest[0:3]
    reduce_slots = rest[3:7]
    gather_slots = rest[7:11]
    gathered = rest[11:14]
    send_sems, recv_sems = rest[14], rest[15]
    coords = own_coords()
    barrier = pltpu.get_barrier_semaphore()
    partner_count = 0
    for name, size in REDUCE_STAGES:
        for steps in range(1, size):
            pl.semaphore_signal(
                barrier, 1, device_id=mesh_id(coords, name, (coords[name] + steps) % size),
                device_id_type=pl.DeviceIdType.MESH,
            )
            partner_count += 1
    pl.semaphore_wait(barrier, partner_count)
    copy_id = 0
    source = x_ref
    for stage, (name, size) in enumerate(REDUCE_STAGES):
        me = coords[name]
        chunk = source.shape[0] // size
        copies = []
        for steps in range(1, size):
            target = (me + steps) % size
            copy = pltpu.make_async_remote_copy(
                src_ref=source.at[pl.ds(pl.multiple_of(target * chunk, chunk), chunk)],
                dst_ref=reduce_slots[stage].at[steps - 1],
                send_sem=send_sems.at[copy_id],
                recv_sem=recv_sems.at[copy_id],
                device_id=mesh_id(coords, name, target),
                device_id_type=pl.DeviceIdType.MESH,
            )
            copy.start()
            copies.append(copy)
            copy_id += 1
        for copy in copies:
            copy.wait()
        total = source[pl.ds(pl.multiple_of(me * chunk, chunk), chunk)]
        for steps in range(1, size):
            total = total + reduce_slots[stage][steps - 1]
        if stage < 3:
            sums[stage][...] = total
            source = sums[stage]
        else:
            gathered[0][pl.ds(pl.multiple_of(me * chunk, chunk), chunk)] = total
    holders = list(gathered[:3]) + [out_ref]
    for level, (name, size) in enumerate(reversed(REDUCE_STAGES)):
        me = coords[name]
        stage = len(REDUCE_STAGES) - 1 - level
        holder = holders[level]
        piece = holder.shape[0] // size
        mine = holder.at[pl.ds(pl.multiple_of(me * piece, piece), piece)]
        copies = []
        for steps in range(1, size):
            copy = pltpu.make_async_remote_copy(
                src_ref=mine,
                dst_ref=gather_slots[level].at[steps - 1],
                send_sem=send_sems.at[copy_id],
                recv_sem=recv_sems.at[copy_id],
                device_id=mesh_id(coords, name, (me + steps) % size),
                device_id_type=pl.DeviceIdType.MESH,
            )
            copy.start()
            copies.append(copy)
            copy_id += 1
        for copy in copies:
            copy.wait()
        for steps in range(1, size):
            origin = (me - steps + size) % size
            holder[pl.ds(pl.multiple_of(origin * piece, piece), piece)] = gather_slots[level][steps - 1]
        if level + 1 < len(holders):
            upper = holders[level + 1]
            next_me = coords[REDUCE_STAGES[stage - 1][0]]
            span = holder.shape[0]
            upper[pl.ds(pl.multiple_of(next_me * span, span), span)] = holder[...]


def all_reduce_rows(flat):
    rows, lanes = flat.shape
    sizes = [s for _, s in REDUCE_STAGES]
    reduce_shapes, gather_shapes = [], []
    current = rows
    for size in sizes:
        current //= size
        reduce_shapes.append((size - 1, current, lanes))
    sum_shapes = [(rows // 2, lanes), (rows // 8, lanes), (rows // 32, lanes)]
    piece = current
    gathered_shapes = []
    for size in reversed(sizes):
        gather_shapes.append((size - 1, piece, lanes))
        piece *= size
        gathered_shapes.append((piece, lanes))
    copies = 2 * sum(s - 1 for s in sizes)
    scratch = (
        [pltpu.VMEM(s, jnp.float32) for s in sum_shapes]
        + [pltpu.VMEM(s, jnp.float32) for s in reduce_shapes]
        + [pltpu.VMEM(s, jnp.float32) for s in gather_shapes]
        + [pltpu.VMEM(s, jnp.float32) for s in gathered_shapes[:3]]
        + [pltpu.SemaphoreType.DMA((copies,)), pltpu.SemaphoreType.DMA((copies,))]
    )
    return pl.pallas_call(
        all_reduce_kernel,
        out_shape=jax.ShapeDtypeStruct(flat.shape, flat.dtype),
        in_specs=[pl.BlockSpec(memory_space=pltpu.VMEM)],
        out_specs=pl.BlockSpec(memory_space=pltpu.VMEM),
        scratch_shapes=scratch,
        compiler_params=pltpu.CompilerParams(collective_id=0, has_side_effects=True),
    )(flat)


def share_grads(weight_sums, bias_sums):
    flat = jnp.concatenate([weight_sums.reshape(-1), bias_sums.reshape(-1)])
    rows = 4096
    padded = jnp.pad(flat, (0, rows * 128 - flat.shape[0])).reshape(rows, 128)
    summed = all_reduce_rows(padded).reshape(-1)
    weight_total = summed[: weight_sums.size].reshape(weight_sums.shape)
    bias_total = summed[weight_sums.size : flat.shape[0]].reshape(bias_sums.shape)
    return weight_total, bias_total


def silu_slope(values):
    sigma = jax.nn.sigmoid(values)
    return sigma * (1.0 + values * (1.0 - sigma))


def local(volume, neighbours, active, cotangent, weight_one, weight_two, bias_one, bias_two):
    slot_count, channels = (volume.shape[1], volume.shape[2])
    position = lax.axis_index("space")
    own_alive = lax.dynamic_slice_in_dim(active[0], position * slot_count, slot_count, 0)
    near_table = lax.dynamic_slice_in_dim(neighbours[0], position * slot_count, slot_count, 0)
    safe_slot = jnp.maximum(near_table, 0)
    source_offset = safe_slot // slot_count - position + 3
    pool_rows = jnp.where(
        near_table < 0, 7 * slot_count, source_offset * slot_count + safe_slot % slot_count
    )
    live_mask = own_alive.astype(jnp.float32)[:, None, None]
    cells = jnp.asarray(cell_grid())
    to_cells = one_hot(jnp.arange(grid_width, dtype=jnp.int32), cells)
    valid = jnp.zeros((grid_width,), jnp.float32).at[cells].set(1.0)
    place = placement()
    back_rows = jnp.transpose(
        weight_two.reshape(channels, 27, channels)[:, ::-1, :], (2, 1, 0)
    ).reshape(channels, 27 * channels)
    masked = volume[0] * live_mask.astype(jnp.bfloat16)
    masked_grid = exact_dot(masked, to_cells, "scn,gn->scg")
    pieces_x = halo_pieces(masked_grid, pool_rows)
    hidden_pre = conv_grid(masked_grid, pieces_x, place, weight_one) + bias_one[None, :, None]
    hidden = (jax.nn.silu(hidden_pre) * live_mask).astype(jnp.bfloat16)
    pieces_h = halo_pieces(hidden, pool_rows)
    out_pre = conv_grid(hidden, pieces_h, place, weight_two) + bias_two[None, :, None]
    result = (jax.nn.silu(out_pre) * live_mask).astype(jnp.bfloat16)
    upstream = exact_dot(cotangent[0], to_cells, "scn,gn->scg")
    grad_out = (upstream.astype(jnp.float32) * live_mask * silu_slope(out_pre)).astype(jnp.bfloat16)
    grad_w_two = weight_grad(grad_out, hidden, pieces_h, place)
    grad_b_two = jnp.sum(grad_out.astype(jnp.float32), axis=(0, 2))
    pieces_g = halo_pieces(grad_out, pool_rows)
    hidden_grad = conv_grid(grad_out, pieces_g, place, back_rows)
    grad_hidden = (hidden_grad * (live_mask * valid) * silu_slope(hidden_pre)).astype(jnp.bfloat16)
    grad_w_one = weight_grad(grad_hidden, masked_grid, pieces_x, place)
    grad_b_one = jnp.sum(grad_hidden.astype(jnp.float32), axis=(0, 2))
    shared_all = share_grads(
        jnp.concatenate([grad_w_one, grad_w_two], axis=0),
        jnp.stack([grad_b_one, grad_b_two], axis=0),
    )
    total_w_one, total_w_two = (shared_all[0][:channels], shared_all[0][channels:])
    total_b_one, total_b_two = (shared_all[1][0], shared_all[1][1])
    output = exact_dot(result, to_cells, "scg,gn->scn")[None]
    return (output, total_w_one, total_w_two, total_b_one, total_b_two)


def solution(mesh):
    in_specs = (
        P("dp", "space", None, None),
        P("dp", None, None),
        P("dp", None),
        P("dp", "space", None, None),
        P(),
        P(),
        P(),
        P(),
    )
    out_specs = (P("dp", "space", None, None), P(), P(), P(), P())
    return jax.shard_map(local, mesh=mesh, in_specs=in_specs, out_specs=out_specs, check_vma=False)
```

```python
import jax
import numpy as np
import jax.numpy as jnp
from jax import lax
from jax.sharding import PartitionSpec as P
from jax.experimental import pallas as pl
from jax.experimental.pallas import tpu as pltpu

EDGE = 8


OFFSETS = [
    (a, b, c) for a in (-1, 0, 1) for b in (-1, 0, 1) for c in (-1, 0, 1) if (a, b, c) != (0, 0, 0)
]
grid_width = 896
flat_width = 1280


def shifted(value, axis, steps):
    count = lax.axis_size(axis)
    leading, last = (max(0, -steps), min(count, count - steps))
    return lax.ppermute(value, axis, [(source, source + steps) for source in range(leading, last)])


def face_index(offset):
    if offset[0] != 0:
        return 1 if offset[0] < 0 else 0
    if offset[1] != 0:
        return 3 if offset[1] < 0 else 2
    return 5 if offset[2] < 0 else 4


def face_span(shift_by, edge_len):
    if shift_by < 0:
        return slice(edge_len - 1, edge_len)
    if shift_by > 0:
        return slice(0, 1)
    return slice(0, edge_len)


def target(shift_by, edge_len):
    if shift_by < 0:
        return slice(0, 1)
    if shift_by > 0:
        return slice(edge_len + 1, edge_len + 2)
    return slice(1, edge_len + 1)


def grid_at(p, q, r):
    return p * (EDGE + 2) ** 2 + q * (EDGE + 2) + r


def face_cells():
    last = EDGE - 1
    cells = []
    for fixed_axis in range(3):
        for fixed_at in (0, last):
            for u in range(EDGE):
                for w in range(EDGE):
                    spot = [u, w]
                    spot.insert(fixed_axis, fixed_at)
                    cells.append(grid_at(*spot))
    return np.array(cells, np.int32)


def piece_layout():
    sources, targets, groups = [], [], []
    face_area = EDGE * EDGE
    for nonzero in (1, 2, 3):
        for k, offset in enumerate(OFFSETS):
            if sum(v != 0 for v in offset) != nonzero:
                continue
            a, b, c = offset
            base = face_index(offset) * face_area
            face = np.arange(base, base + face_area).reshape(EDGE, EDGE)
            if a != 0:
                part = face[face_span(b, EDGE), face_span(c, EDGE)]
            elif b != 0:
                part = face[:, face_span(c, EDGE)]
            else:
                part = face
            sources.extend(part.reshape(-1).tolist())
            groups.extend([k] * part.size)
            for pp in range(EDGE + 2)[target(a, EDGE)]:
                for qq in range(EDGE + 2)[target(b, EDGE)]:
                    for rr in range(EDGE + 2)[target(c, EDGE)]:
                        targets.append(grid_at(pp, qq, rr))
    return np.array(sources, np.int32), np.array(targets, np.int32), np.array(groups, np.int32)


def cell_grid():
    return np.array(
        [grid_at(p, q, r) for p in range(EDGE) for q in range(EDGE) for r in range(EDGE)], np.int32
    )


def one_hot(rows, columns):
    return (jnp.asarray(rows)[:, None] == jnp.asarray(columns)[None, :]).astype(jnp.bfloat16)


def placement():
    grid_ids = jnp.arange(grid_width, dtype=jnp.int32)
    cells = jnp.asarray(cell_grid())
    valid = jnp.zeros((grid_width,), jnp.int32).at[cells].set(1)
    center_target = jnp.where(valid > 0, grid_ids + grid_at(1, 1, 1), -1)
    from_center = one_hot(center_target, jnp.arange(flat_width, dtype=jnp.int32))
    piece_sources, piece_targets, piece_groups = piece_layout()
    from_pieces = one_hot(piece_targets, jnp.arange(flat_width, dtype=jnp.int32))
    return from_center, from_pieces


def exact_dot(left, right, spec):
    return jnp.einsum(spec, left, right, preferred_element_type=jnp.float32).astype(left.dtype)


def stacked_windows(whole):
    windows = []
    for b in range(3):
        for c in range(3):
            start = b * (EDGE + 2) + c
            moved = whole if start == 0 else pltpu.roll(whole, flat_width - start, 1)
            windows.append(moved.astype(jnp.bfloat16))
    return jnp.concatenate(windows, axis=0)


def fill_padded(grid_ref, piece_ref, center_ref, halo_ref, whole_ref):
    whole_ref[...] = jnp.dot(
        grid_ref[...], center_ref[...], preferred_element_type=jnp.float32
    ) + jnp.dot(piece_ref[...], halo_ref[...], preferred_element_type=jnp.float32)


def conv_kernel(grid_ref, piece_ref, center_ref, halo_ref, taps_ref, out_ref, whole_ref):
    plane = (EDGE + 2) ** 2
    channels = out_ref.shape[1]
    fill_padded(grid_ref, piece_ref, center_ref, halo_ref, whole_ref)

    def one_brick(brick, carry):
        whole = whole_ref[pl.ds(pl.multiple_of(brick * channels, channels), channels), :]
        product = jnp.dot(taps_ref[...], stacked_windows(whole), preferred_element_type=jnp.float32)
        summed = product[:channels]
        for a in (1, 2):
            summed = summed + pltpu.roll(
                product[a * channels : (a + 1) * channels], flat_width - a * plane, 1
            )
        out_ref[brick] = summed[:, :grid_width]
        return carry

    lax.fori_loop(0, out_ref.shape[0], one_brick, 0)


def weight_grad_kernel(grad_ref, grid_ref, piece_ref, center_ref, halo_ref, out_ref, whole_ref):
    plane = (EDGE + 2) ** 2
    channels = grad_ref.shape[1]
    fill_padded(grid_ref, piece_ref, center_ref, halo_ref, whole_ref)
    out_ref[...] = jnp.zeros(out_ref.shape, jnp.float32)

    def one_brick(brick, carry):
        whole = whole_ref[pl.ds(pl.multiple_of(brick * channels, channels), channels), :]
        grad_cells = grad_ref[brick].astype(jnp.float32)
        grad_wide = jnp.concatenate(
            [grad_cells, jnp.zeros((channels, flat_width - grid_width), jnp.float32)], axis=1
        )
        moved = [grad_wide] + [pltpu.roll(grad_wide, a * plane, 1) for a in (1, 2)]
        out_ref[...] += lax.dot_general(
            jnp.concatenate(moved, axis=0).astype(jnp.bfloat16),
            stacked_windows(whole),
            (((1,), (1,)), ((), ())),
            preferred_element_type=jnp.float32,
        )
        return carry

    lax.fori_loop(0, grad_ref.shape[0], one_brick, 0)


def vmem_specs(count):
    return [pl.BlockSpec(memory_space=pltpu.VMEM)] * count


def tap_rows(weight_rows):
    channels = weight_rows.shape[0]
    return jnp.transpose(weight_rows.reshape(channels, 3, 9 * channels), (1, 0, 2)).reshape(
        3 * channels, 9 * channels
    )


def conv_grid(grid_cells, pieces, place, weight_rows):
    slot_count, channels = (grid_cells.shape[0], weight_rows.shape[0])
    return pl.pallas_call(
        conv_kernel,
        out_shape=jax.ShapeDtypeStruct((slot_count, channels, grid_width), jnp.float32),
        in_specs=vmem_specs(5),
        out_specs=pl.BlockSpec(memory_space=pltpu.VMEM),
        scratch_shapes=[pltpu.VMEM((slot_count * channels, flat_width), jnp.float32)],
        cost_estimate=pl.CostEstimate(
            flops=2 * slot_count * channels * flat_width * (weight_rows.shape[1] + 1400),
            bytes_accessed=grid_cells.size * 2 + pieces.size * 2 + 3 * 2**20 + slot_count * channels * grid_width * 4,
            transcendentals=0,
        ),
    )(
        grid_cells.reshape(slot_count * channels, grid_width),
        pieces.reshape(slot_count * channels, pieces.shape[2]),
        place[0],
        place[1],
        tap_rows(weight_rows),
    )


def weight_grad(grad_cells, grid_cells, pieces, place):
    slot_count, channels = (grid_cells.shape[0], grid_cells.shape[1])
    per_depth = pl.pallas_call(
        weight_grad_kernel,
        out_shape=jax.ShapeDtypeStruct((3 * channels, 9 * channels), jnp.float32),
        in_specs=vmem_specs(5),
        out_specs=pl.BlockSpec(memory_space=pltpu.VMEM),
        scratch_shapes=[pltpu.VMEM((slot_count * channels, flat_width), jnp.float32)],
        cost_estimate=pl.CostEstimate(
            flops=2 * slot_count * channels * flat_width * (27 * channels + 1400),
            bytes_accessed=grid_cells.size * 4 + pieces.size * 2 + 3 * 2**20 + 27 * channels * channels * 4,
            transcendentals=0,
        ),
    )(
        grad_cells,
        grid_cells.reshape(slot_count * channels, grid_width),
        pieces.reshape(slot_count * channels, pieces.shape[2]),
        place[0],
        place[1],
    )
    return jnp.transpose(per_depth.reshape(3, channels, 9 * channels), (1, 0, 2)).reshape(
        channels, 27 * channels
    )


def build_pool(outer_faces):
    slot_count, channels, width = outer_faces.shape
    face_area = width // 6
    first_faces = outer_faces[:, :, : 2 * face_area]
    filler = jnp.zeros((slot_count, channels, width - 2 * face_area), outer_faces.dtype)
    received = {}
    for offset in (-1, 1):
        received[offset] = shifted(outer_faces, "space", -offset)
    for offset in (-3, -2, 2, 3):
        received[offset] = jnp.concatenate([shifted(first_faces, "space", -offset), filler], axis=2)
    received[0] = outer_faces
    zero_row = jnp.zeros((1, channels, width), outer_faces.dtype)
    return jnp.concatenate([received[k] for k in (-3, -2, -1, 0, 1, 2, 3)] + [zero_row], axis=0)


def halo_pieces(grid_cells, pool_rows):
    faces = exact_dot(grid_cells, one_hot(jnp.arange(grid_width, dtype=jnp.int32), face_cells()), "scg,gf->scf")
    pool = build_pool(faces)
    rows = pool.shape[0]
    piece_sources, piece_targets, piece_groups = piece_layout()
    table = exact_dot(pool, one_hot(jnp.arange(faces.shape[2], dtype=jnp.int32), piece_sources), "scf,fe->sce")
    chosen = jnp.take(pool_rows, jnp.asarray(piece_groups), axis=1)
    pick = (chosen[:, None, :] == jnp.arange(rows, dtype=jnp.int32)[None, :, None]).astype(jnp.float32)
    picked = jnp.sum(pick[:, :, None, :] * table.astype(jnp.float32)[None], axis=1)
    return picked.astype(grid_cells.dtype)


REDUCE_STAGES = (("core", 2), ("x", 4), ("y", 4), ("z", 4))


def own_coords():
    space = lax.axis_index("space")
    dp = lax.axis_index("dp")
    return {"core": space % 2, "x": dp % 4, "y": space // 2 % 4, "z": dp // 4 * 2 + space // 8}


def mesh_id(coords, name, value):
    moved = dict(coords)
    moved[name] = value
    space = ((moved["z"] % 2) * 4 + moved["y"]) * 2 + moved["core"]
    return (space, moved["z"] // 2 * 4 + moved["x"])


def all_reduce_kernel(*refs):
    x_ref, out_ref = refs[0], refs[1]
    rest = refs[2:]
    sums = rest[0:3]
    reduce_slots = rest[3:7]
    gather_slots = rest[7:11]
    gathered = rest[11:14]
    send_sems, recv_sems = rest[14], rest[15]
    coords = own_coords()
    barrier = pltpu.get_barrier_semaphore()
    partner_count = 0
    for name, size in REDUCE_STAGES:
        for steps in range(1, size):
            pl.semaphore_signal(
                barrier, 1, device_id=mesh_id(coords, name, (coords[name] + steps) % size),
                device_id_type=pl.DeviceIdType.MESH,
            )
            partner_count += 1
    pl.semaphore_wait(barrier, partner_count)
    copy_id = 0
    source = x_ref
    for stage, (name, size) in enumerate(REDUCE_STAGES):
        me = coords[name]
        chunk = source.shape[0] // size
        copies = []
        for steps in range(1, size):
            target = (me + steps) % size
            copy = pltpu.make_async_remote_copy(
                src_ref=source.at[pl.ds(pl.multiple_of(target * chunk, chunk), chunk)],
                dst_ref=reduce_slots[stage].at[steps - 1],
                send_sem=send_sems.at[copy_id],
                recv_sem=recv_sems.at[copy_id],
                device_id=mesh_id(coords, name, target),
                device_id_type=pl.DeviceIdType.MESH,
            )
            copy.start()
            copies.append(copy)
            copy_id += 1
        for copy in copies:
            copy.wait()
        total = source[pl.ds(pl.multiple_of(me * chunk, chunk), chunk)]
        for steps in range(1, size):
            total = total + reduce_slots[stage][steps - 1]
        if stage < 3:
            sums[stage][...] = total
            source = sums[stage]
        else:
            gathered[0][pl.ds(pl.multiple_of(me * chunk, chunk), chunk)] = total
    holders = list(gathered[:3]) + [out_ref]
    for level, (name, size) in enumerate(reversed(REDUCE_STAGES)):
        me = coords[name]
        stage = len(REDUCE_STAGES) - 1 - level
        holder = holders[level]
        piece = holder.shape[0] // size
        mine = holder.at[pl.ds(pl.multiple_of(me * piece, piece), piece)]
        copies = []
        for steps in range(1, size):
            copy = pltpu.make_async_remote_copy(
                src_ref=mine,
                dst_ref=gather_slots[level].at[steps - 1],
                send_sem=send_sems.at[copy_id],
                recv_sem=recv_sems.at[copy_id],
                device_id=mesh_id(coords, name, (me + steps) % size),
                device_id_type=pl.DeviceIdType.MESH,
            )
            copy.start()
            copies.append(copy)
            copy_id += 1
        for copy in copies:
            copy.wait()
        for steps in range(1, size):
            origin = (me - steps + size) % size
            holder[pl.ds(pl.multiple_of(origin * piece, piece), piece)] = gather_slots[level][steps - 1]
        if level + 1 < len(holders):
            upper = holders[level + 1]
            next_me = coords[REDUCE_STAGES[stage - 1][0]]
            span = holder.shape[0]
            upper[pl.ds(pl.multiple_of(next_me * span, span), span)] = holder[...]


def all_reduce_rows(flat):
    rows, lanes = flat.shape
    sizes = [s for _, s in REDUCE_STAGES]
    reduce_shapes, gather_shapes = [], []
    current = rows
    for size in sizes:
        current //= size
        reduce_shapes.append((size - 1, current, lanes))
    sum_shapes = [(rows // 2, lanes), (rows // 8, lanes), (rows // 32, lanes)]
    piece = current
    gathered_shapes = []
    for size in reversed(sizes):
        gather_shapes.append((size - 1, piece, lanes))
        piece *= size
        gathered_shapes.append((piece, lanes))
    copies = 2 * sum(s - 1 for s in sizes)
    scratch = (
        [pltpu.VMEM(s, jnp.float32) for s in sum_shapes]
        + [pltpu.VMEM(s, jnp.float32) for s in reduce_shapes]
        + [pltpu.VMEM(s, jnp.float32) for s in gather_shapes]
        + [pltpu.VMEM(s, jnp.float32) for s in gathered_shapes[:3]]
        + [pltpu.SemaphoreType.DMA((copies,)), pltpu.SemaphoreType.DMA((copies,))]
    )
    return pl.pallas_call(
        all_reduce_kernel,
        out_shape=jax.ShapeDtypeStruct(flat.shape, flat.dtype),
        in_specs=[pl.BlockSpec(memory_space=pltpu.VMEM)],
        out_specs=pl.BlockSpec(memory_space=pltpu.VMEM),
        scratch_shapes=scratch,
        compiler_params=pltpu.CompilerParams(collective_id=0, has_side_effects=True),
    )(flat)


def share_grads(weight_sums, bias_sums):
    flat = jnp.concatenate([weight_sums.reshape(-1), bias_sums.reshape(-1)])
    rows = 4096
    padded = jnp.pad(flat, (0, rows * 128 - flat.shape[0])).reshape(rows, 128)
    summed = all_reduce_rows(padded).reshape(-1)
    weight_total = summed[: weight_sums.size].reshape(weight_sums.shape)
    bias_total = summed[weight_sums.size : flat.shape[0]].reshape(bias_sums.shape)
    return weight_total, bias_total


def silu_slope(values):
    sigma = jax.nn.sigmoid(values)
    return sigma * (1.0 + values * (1.0 - sigma))


def local(volume, neighbours, active, cotangent, weight_one, weight_two, bias_one, bias_two):
    slot_count, channels = (volume.shape[1], volume.shape[2])
    position = lax.axis_index("space")
    own_alive = lax.dynamic_slice_in_dim(active[0], position * slot_count, slot_count, 0)
    near_table = lax.dynamic_slice_in_dim(neighbours[0], position * slot_count, slot_count, 0)
    safe_slot = jnp.maximum(near_table, 0)
    source_offset = safe_slot // slot_count - position + 3
    pool_rows = jnp.where(
        near_table < 0, 7 * slot_count, source_offset * slot_count + safe_slot % slot_count
    )
    live_mask = own_alive.astype(jnp.float32)[:, None, None]
    cells = jnp.asarray(cell_grid())
    to_cells = one_hot(jnp.arange(grid_width, dtype=jnp.int32), cells)
    valid = jnp.zeros((grid_width,), jnp.float32).at[cells].set(1.0)
    place = placement()
    back_rows = jnp.transpose(
        weight_two.reshape(channels, 27, channels)[:, ::-1, :], (2, 1, 0)
    ).reshape(channels, 27 * channels)
    masked = volume[0] * live_mask.astype(jnp.bfloat16)
    masked_grid = exact_dot(masked, to_cells, "scn,gn->scg")
    pieces_x = halo_pieces(masked_grid, pool_rows)
    hidden_pre = conv_grid(masked_grid, pieces_x, place, weight_one) + bias_one[None, :, None]
    hidden = (jax.nn.silu(hidden_pre) * live_mask).astype(jnp.bfloat16)
    pieces_h = halo_pieces(hidden, pool_rows)
    out_pre = conv_grid(hidden, pieces_h, place, weight_two) + bias_two[None, :, None]
    result = (jax.nn.silu(out_pre) * live_mask).astype(jnp.bfloat16)
    upstream = exact_dot(cotangent[0], to_cells, "scn,gn->scg")
    grad_out = (upstream.astype(jnp.float32) * live_mask * silu_slope(out_pre)).astype(jnp.bfloat16)
    grad_w_two = weight_grad(grad_out, hidden, pieces_h, place)
    grad_b_two = jnp.sum(grad_out.astype(jnp.float32), axis=(0, 2))
    pieces_g = halo_pieces(grad_out, pool_rows)
    hidden_grad = conv_grid(grad_out, pieces_g, place, back_rows)
    grad_hidden = (hidden_grad * (live_mask * valid) * silu_slope(hidden_pre)).astype(jnp.bfloat16)
    grad_w_one = weight_grad(grad_hidden, masked_grid, pieces_x, place)
    grad_b_one = jnp.sum(grad_hidden.astype(jnp.float32), axis=(0, 2))
    shared_all = share_grads(
        jnp.concatenate([grad_w_one, grad_w_two], axis=0),
        jnp.stack([grad_b_one, grad_b_two], axis=0),
    )
    total_w_one, total_w_two = (shared_all[0][:channels], shared_all[0][channels:])
    total_b_one, total_b_two = (shared_all[1][0], shared_all[1][1])
    output = exact_dot(result, to_cells, "scg,gn->scn")[None]
    return (output, total_w_one, total_w_two, total_b_one, total_b_two)


def solution(mesh):
    in_specs = (
        P("dp", "space", None, None),
        P("dp", None, None),
        P("dp", None),
        P("dp", "space", None, None),
        P(),
        P(),
        P(),
        P(),
    )
    out_specs = (P("dp", "space", None, None), P(), P(), P(), P())
    return jax.shard_map(local, mesh=mesh, in_specs=in_specs, out_specs=out_specs, check_vma=False)
```

```python
import jax
import numpy as np
import jax.numpy as jnp
from jax import lax
from jax.sharding import PartitionSpec as P
from jax.experimental import pallas as pl
from jax.experimental.pallas import tpu as pltpu

EDGE = 8


OFFSETS = [
    (a, b, c) for a in (-1, 0, 1) for b in (-1, 0, 1) for c in (-1, 0, 1) if (a, b, c) != (0, 0, 0)
]
grid_width = 896
flat_width = 1280


def shifted(value, axis, steps):
    count = lax.axis_size(axis)
    leading, last = (max(0, -steps), min(count, count - steps))
    return lax.ppermute(value, axis, [(source, source + steps) for source in range(leading, last)])


def face_index(offset):
    if offset[0] != 0:
        return 1 if offset[0] < 0 else 0
    if offset[1] != 0:
        return 3 if offset[1] < 0 else 2
    return 5 if offset[2] < 0 else 4


def face_span(shift_by, edge_len):
    if shift_by < 0:
        return slice(edge_len - 1, edge_len)
    if shift_by > 0:
        return slice(0, 1)
    return slice(0, edge_len)


def target(shift_by, edge_len):
    if shift_by < 0:
        return slice(0, 1)
    if shift_by > 0:
        return slice(edge_len + 1, edge_len + 2)
    return slice(1, edge_len + 1)


def grid_at(p, q, r):
    return p * (EDGE + 2) ** 2 + q * (EDGE + 2) + r


def face_cells():
    last = EDGE - 1
    cells = []
    for fixed_axis in range(3):
        for fixed_at in (0, last):
            for u in range(EDGE):
                for w in range(EDGE):
                    spot = [u, w]
                    spot.insert(fixed_axis, fixed_at)
                    cells.append(grid_at(*spot))
    return np.array(cells, np.int32)


def piece_layout():
    sources, targets, groups = [], [], []
    face_area = EDGE * EDGE
    for nonzero in (1, 2, 3):
        for k, offset in enumerate(OFFSETS):
            if sum(v != 0 for v in offset) != nonzero:
                continue
            a, b, c = offset
            base = face_index(offset) * face_area
            face = np.arange(base, base + face_area).reshape(EDGE, EDGE)
            if a != 0:
                part = face[face_span(b, EDGE), face_span(c, EDGE)]
            elif b != 0:
                part = face[:, face_span(c, EDGE)]
            else:
                part = face
            sources.extend(part.reshape(-1).tolist())
            groups.extend([k] * part.size)
            for pp in range(EDGE + 2)[target(a, EDGE)]:
                for qq in range(EDGE + 2)[target(b, EDGE)]:
                    for rr in range(EDGE + 2)[target(c, EDGE)]:
                        targets.append(grid_at(pp, qq, rr))
    return np.array(sources, np.int32), np.array(targets, np.int32), np.array(groups, np.int32)


def cell_grid():
    return np.array(
        [grid_at(p, q, r) for p in range(EDGE) for q in range(EDGE) for r in range(EDGE)], np.int32
    )


def one_hot(rows, columns):
    return (jnp.asarray(rows)[:, None] == jnp.asarray(columns)[None, :]).astype(jnp.bfloat16)


def placement():
    grid_ids = jnp.arange(grid_width, dtype=jnp.int32)
    cells = jnp.asarray(cell_grid())
    valid = jnp.zeros((grid_width,), jnp.int32).at[cells].set(1)
    center_target = jnp.where(valid > 0, grid_ids + grid_at(1, 1, 1), -1)
    from_center = one_hot(center_target, jnp.arange(flat_width, dtype=jnp.int32))
    piece_sources, piece_targets, piece_groups = piece_layout()
    from_pieces = one_hot(piece_targets, jnp.arange(flat_width, dtype=jnp.int32))
    return from_center, from_pieces


def exact_dot(left, right, spec):
    return jnp.einsum(spec, left, right, preferred_element_type=jnp.float32).astype(left.dtype)


def stacked_windows(whole):
    windows = []
    for b in range(3):
        for c in range(3):
            start = b * (EDGE + 2) + c
            moved = whole if start == 0 else pltpu.roll(whole, flat_width - start, 1)
            windows.append(moved.astype(jnp.bfloat16))
    return jnp.concatenate(windows, axis=0)


def fill_padded(grid_ref, piece_ref, center_ref, halo_ref, whole_ref):
    whole_ref[...] = jnp.dot(
        grid_ref[...], center_ref[...], preferred_element_type=jnp.float32
    ) + jnp.dot(piece_ref[...], halo_ref[...], preferred_element_type=jnp.float32)


def conv_kernel(grid_ref, piece_ref, center_ref, halo_ref, taps_ref, out_ref, whole_ref):
    plane = (EDGE + 2) ** 2
    channels = out_ref.shape[1]
    fill_padded(grid_ref, piece_ref, center_ref, halo_ref, whole_ref)

    def one_brick(brick, carry):
        whole = whole_ref[pl.ds(pl.multiple_of(brick * channels, channels), channels), :]
        product = jnp.dot(taps_ref[...], stacked_windows(whole), preferred_element_type=jnp.float32)
        summed = product[:channels]
        for a in (1, 2):
            summed = summed + pltpu.roll(
                product[a * channels : (a + 1) * channels], flat_width - a * plane, 1
            )
        out_ref[brick] = summed[:, :grid_width]
        return carry

    lax.fori_loop(0, out_ref.shape[0], one_brick, 0)


def weight_grad_kernel(grad_ref, grid_ref, piece_ref, center_ref, halo_ref, out_ref, whole_ref):
    plane = (EDGE + 2) ** 2
    channels = grad_ref.shape[1]
    fill_padded(grid_ref, piece_ref, center_ref, halo_ref, whole_ref)
    out_ref[...] = jnp.zeros(out_ref.shape, jnp.float32)

    def one_brick(brick, carry):
        whole = whole_ref[pl.ds(pl.multiple_of(brick * channels, channels), channels), :]
        grad_cells = grad_ref[brick].astype(jnp.float32)
        grad_wide = jnp.concatenate(
            [grad_cells, jnp.zeros((channels, flat_width - grid_width), jnp.float32)], axis=1
        )
        moved = [grad_wide] + [pltpu.roll(grad_wide, a * plane, 1) for a in (1, 2)]
        out_ref[...] += lax.dot_general(
            jnp.concatenate(moved, axis=0).astype(jnp.bfloat16),
            stacked_windows(whole),
            (((1,), (1,)), ((), ())),
            preferred_element_type=jnp.float32,
        )
        return carry

    lax.fori_loop(0, grad_ref.shape[0], one_brick, 0)


def vmem_specs(count):
    return [pl.BlockSpec(memory_space=pltpu.VMEM)] * count


def tap_rows(weight_rows):
    channels = weight_rows.shape[0]
    return jnp.transpose(weight_rows.reshape(channels, 3, 9 * channels), (1, 0, 2)).reshape(
        3 * channels, 9 * channels
    )


def conv_grid(grid_cells, pieces, place, weight_rows):
    slot_count, channels = (grid_cells.shape[0], weight_rows.shape[0])
    return pl.pallas_call(
        conv_kernel,
        out_shape=jax.ShapeDtypeStruct((slot_count, channels, grid_width), jnp.float32),
        in_specs=vmem_specs(5),
        out_specs=pl.BlockSpec(memory_space=pltpu.VMEM),
        scratch_shapes=[pltpu.VMEM((slot_count * channels, flat_width), jnp.float32)],
        cost_estimate=pl.CostEstimate(
            flops=2 * slot_count * channels * flat_width * (weight_rows.shape[1] + 1400),
            bytes_accessed=grid_cells.size * 2 + pieces.size * 2 + 3 * 2**20 + slot_count * channels * grid_width * 4,
            transcendentals=0,
        ),
    )(
        grid_cells.reshape(slot_count * channels, grid_width),
        pieces.reshape(slot_count * channels, pieces.shape[2]),
        place[0],
        place[1],
        tap_rows(weight_rows),
    )


def weight_grad(grad_cells, grid_cells, pieces, place):
    slot_count, channels = (grid_cells.shape[0], grid_cells.shape[1])
    per_depth = pl.pallas_call(
        weight_grad_kernel,
        out_shape=jax.ShapeDtypeStruct((3 * channels, 9 * channels), jnp.float32),
        in_specs=vmem_specs(5),
        out_specs=pl.BlockSpec(memory_space=pltpu.VMEM),
        scratch_shapes=[pltpu.VMEM((slot_count * channels, flat_width), jnp.float32)],
        cost_estimate=pl.CostEstimate(
            flops=2 * slot_count * channels * flat_width * (27 * channels + 1400),
            bytes_accessed=grid_cells.size * 4 + pieces.size * 2 + 3 * 2**20 + 27 * channels * channels * 4,
            transcendentals=0,
        ),
    )(
        grad_cells,
        grid_cells.reshape(slot_count * channels, grid_width),
        pieces.reshape(slot_count * channels, pieces.shape[2]),
        place[0],
        place[1],
    )
    return jnp.transpose(per_depth.reshape(3, channels, 9 * channels), (1, 0, 2)).reshape(
        channels, 27 * channels
    )


HALO_SHIFTS = (-3, -2, -1, 1, 2, 3)


def halo_kernel(faces_ref, pool_ref, send_sems, recv_sems):
    me = lax.axis_index("space")
    column = lax.axis_index("dp")
    count = lax.axis_size("space")
    centre = len(HALO_SHIFTS) // 2
    first_lanes = 2 * EDGE * EDGE
    pool_ref[...] = jnp.zeros(pool_ref.shape, pool_ref.dtype)
    pool_ref[centre] = faces_ref[...]
    barrier = pltpu.get_barrier_semaphore()
    partners = 0
    for shift in HALO_SHIFTS:
        target = me - shift
        reachable = (target >= 0) & (target < count)
        partners = partners + reachable.astype(jnp.int32)

        @pl.when(reachable)
        def _():
            pl.semaphore_signal(
                barrier, 1, device_id=(target, column), device_id_type=pl.DeviceIdType.MESH
            )

    pl.semaphore_wait(barrier, partners)
    copies = []
    for index, shift in enumerate(HALO_SHIFTS):
        target = me - shift
        lanes = pl.ds(0, first_lanes) if abs(shift) > 1 else pl.ds(0, faces_ref.shape[2])
        copy = pltpu.make_async_remote_copy(
            src_ref=faces_ref.at[:, :, lanes],
            dst_ref=pool_ref.at[shift + centre, :, :, lanes],
            send_sem=send_sems.at[index],
            recv_sem=recv_sems.at[index],
            device_id=(jnp.clip(target, 0, count - 1), column),
            device_id_type=pl.DeviceIdType.MESH,
        )
        sends = (target >= 0) & (target < count)
        receives = (me + shift >= 0) & (me + shift < count)
        copies.append((copy, sends, receives))

        @pl.when(sends)
        def _():
            copy.start()

    for copy, sends, receives in copies:

        @pl.when(sends)
        def _():
            copy.wait_send()

        @pl.when(receives)
        def _():
            copy.wait_recv()


def build_pool(outer_faces):
    slot_count, channels, width = outer_faces.shape
    groups = len(HALO_SHIFTS) + 1
    pool = pl.pallas_call(
        halo_kernel,
        out_shape=jax.ShapeDtypeStruct((groups, slot_count, channels, width), outer_faces.dtype),
        in_specs=[pl.BlockSpec(memory_space=pltpu.VMEM)],
        out_specs=pl.BlockSpec(memory_space=pltpu.VMEM),
        scratch_shapes=[
            pltpu.SemaphoreType.DMA((len(HALO_SHIFTS),)),
            pltpu.SemaphoreType.DMA((len(HALO_SHIFTS),)),
        ],
        compiler_params=pltpu.CompilerParams(collective_id=1, has_side_effects=True),
    )(outer_faces)
    return pool.reshape(groups * slot_count, channels, width)


def halo_pieces(grid_cells, pool_rows):
    faces = exact_dot(grid_cells, one_hot(jnp.arange(grid_width, dtype=jnp.int32), face_cells()), "scg,gf->scf")
    pool = build_pool(faces)
    rows = pool.shape[0]
    piece_sources, piece_targets, piece_groups = piece_layout()
    table = exact_dot(pool, one_hot(jnp.arange(faces.shape[2], dtype=jnp.int32), piece_sources), "scf,fe->sce")
    chosen = jnp.take(pool_rows, jnp.asarray(piece_groups), axis=1)
    pick = (chosen[:, None, :] == jnp.arange(rows, dtype=jnp.int32)[None, :, None]).astype(jnp.float32)
    picked = jnp.sum(pick[:, :, None, :] * table.astype(jnp.float32)[None], axis=1)
    return picked.astype(grid_cells.dtype)


REDUCE_STAGES = (("core", 2), ("x", 4), ("y", 4), ("z", 4))


def own_coords():
    space = lax.axis_index("space")
    dp = lax.axis_index("dp")
    return {"core": space % 2, "x": dp % 4, "y": space // 2 % 4, "z": dp // 4 * 2 + space // 8}


def mesh_id(coords, name, value):
    moved = dict(coords)
    moved[name] = value
    space = ((moved["z"] % 2) * 4 + moved["y"]) * 2 + moved["core"]
    return (space, moved["z"] // 2 * 4 + moved["x"])


def all_reduce_kernel(*refs):
    x_ref, out_ref = refs[0], refs[1]
    rest = refs[2:]
    sums = rest[0:3]
    reduce_slots = rest[3:7]
    gather_slots = rest[7:11]
    gathered = rest[11:14]
    send_sems, recv_sems = rest[14], rest[15]
    coords = own_coords()
    barrier = pltpu.get_barrier_semaphore()
    partner_count = 0
    for name, size in REDUCE_STAGES:
        for steps in range(1, size):
            pl.semaphore_signal(
                barrier, 1, device_id=mesh_id(coords, name, (coords[name] + steps) % size),
                device_id_type=pl.DeviceIdType.MESH,
            )
            partner_count += 1
    pl.semaphore_wait(barrier, partner_count)
    copy_id = 0
    source = x_ref
    for stage, (name, size) in enumerate(REDUCE_STAGES):
        me = coords[name]
        chunk = source.shape[0] // size
        copies = []
        for steps in range(1, size):
            target = (me + steps) % size
            copy = pltpu.make_async_remote_copy(
                src_ref=source.at[pl.ds(pl.multiple_of(target * chunk, chunk), chunk)],
                dst_ref=reduce_slots[stage].at[steps - 1],
                send_sem=send_sems.at[copy_id],
                recv_sem=recv_sems.at[copy_id],
                device_id=mesh_id(coords, name, target),
                device_id_type=pl.DeviceIdType.MESH,
            )
            copy.start()
            copies.append(copy)
            copy_id += 1
        for copy in copies:
            copy.wait()
        total = source[pl.ds(pl.multiple_of(me * chunk, chunk), chunk)]
        for steps in range(1, size):
            total = total + reduce_slots[stage][steps - 1]
        if stage < 3:
            sums[stage][...] = total
            source = sums[stage]
        else:
            gathered[0][pl.ds(pl.multiple_of(me * chunk, chunk), chunk)] = total
    holders = list(gathered[:3]) + [out_ref]
    for level, (name, size) in enumerate(reversed(REDUCE_STAGES)):
        me = coords[name]
        stage = len(REDUCE_STAGES) - 1 - level
        holder = holders[level]
        piece = holder.shape[0] // size
        mine = holder.at[pl.ds(pl.multiple_of(me * piece, piece), piece)]
        copies = []
        for steps in range(1, size):
            copy = pltpu.make_async_remote_copy(
                src_ref=mine,
                dst_ref=gather_slots[level].at[steps - 1],
                send_sem=send_sems.at[copy_id],
                recv_sem=recv_sems.at[copy_id],
                device_id=mesh_id(coords, name, (me + steps) % size),
                device_id_type=pl.DeviceIdType.MESH,
            )
            copy.start()
            copies.append(copy)
            copy_id += 1
        for copy in copies:
            copy.wait()
        for steps in range(1, size):
            origin = (me - steps + size) % size
            holder[pl.ds(pl.multiple_of(origin * piece, piece), piece)] = gather_slots[level][steps - 1]
        if level + 1 < len(holders):
            upper = holders[level + 1]
            next_me = coords[REDUCE_STAGES[stage - 1][0]]
            span = holder.shape[0]
            upper[pl.ds(pl.multiple_of(next_me * span, span), span)] = holder[...]


def all_reduce_rows(flat):
    rows, lanes = flat.shape
    sizes = [s for _, s in REDUCE_STAGES]
    reduce_shapes, gather_shapes = [], []
    current = rows
    for size in sizes:
        current //= size
        reduce_shapes.append((size - 1, current, lanes))
    sum_shapes = [(rows // 2, lanes), (rows // 8, lanes), (rows // 32, lanes)]
    piece = current
    gathered_shapes = []
    for size in reversed(sizes):
        gather_shapes.append((size - 1, piece, lanes))
        piece *= size
        gathered_shapes.append((piece, lanes))
    copies = 2 * sum(s - 1 for s in sizes)
    scratch = (
        [pltpu.VMEM(s, jnp.float32) for s in sum_shapes]
        + [pltpu.VMEM(s, jnp.float32) for s in reduce_shapes]
        + [pltpu.VMEM(s, jnp.float32) for s in gather_shapes]
        + [pltpu.VMEM(s, jnp.float32) for s in gathered_shapes[:3]]
        + [pltpu.SemaphoreType.DMA((copies,)), pltpu.SemaphoreType.DMA((copies,))]
    )
    return pl.pallas_call(
        all_reduce_kernel,
        out_shape=jax.ShapeDtypeStruct(flat.shape, flat.dtype),
        in_specs=[pl.BlockSpec(memory_space=pltpu.VMEM)],
        out_specs=pl.BlockSpec(memory_space=pltpu.VMEM),
        scratch_shapes=scratch,
        compiler_params=pltpu.CompilerParams(collective_id=0, has_side_effects=True),
    )(flat)


def share_grads(weight_sums, bias_sums):
    flat = jnp.concatenate([weight_sums.reshape(-1), bias_sums.reshape(-1)])
    rows = 4096
    padded = jnp.pad(flat, (0, rows * 128 - flat.shape[0])).reshape(rows, 128)
    summed = all_reduce_rows(padded).reshape(-1)
    weight_total = summed[: weight_sums.size].reshape(weight_sums.shape)
    bias_total = summed[weight_sums.size : flat.shape[0]].reshape(bias_sums.shape)
    return weight_total, bias_total


def silu_slope(values):
    sigma = jax.nn.sigmoid(values)
    return sigma * (1.0 + values * (1.0 - sigma))


def local(volume, neighbours, active, cotangent, weight_one, weight_two, bias_one, bias_two):
    slot_count, channels = (volume.shape[1], volume.shape[2])
    position = lax.axis_index("space")
    own_alive = lax.dynamic_slice_in_dim(active[0], position * slot_count, slot_count, 0)
    near_table = lax.dynamic_slice_in_dim(neighbours[0], position * slot_count, slot_count, 0)
    safe_slot = jnp.maximum(near_table, 0)
    source_offset = safe_slot // slot_count - position + 3
    pool_rows = jnp.where(
        near_table < 0, 7 * slot_count, source_offset * slot_count + safe_slot % slot_count
    )
    live_mask = own_alive.astype(jnp.float32)[:, None, None]
    cells = jnp.asarray(cell_grid())
    to_cells = one_hot(jnp.arange(grid_width, dtype=jnp.int32), cells)
    valid = jnp.zeros((grid_width,), jnp.float32).at[cells].set(1.0)
    place = placement()
    back_rows = jnp.transpose(
        weight_two.reshape(channels, 27, channels)[:, ::-1, :], (2, 1, 0)
    ).reshape(channels, 27 * channels)
    masked = volume[0] * live_mask.astype(jnp.bfloat16)
    masked_grid = exact_dot(masked, to_cells, "scn,gn->scg")
    pieces_x = halo_pieces(masked_grid, pool_rows)
    hidden_pre = conv_grid(masked_grid, pieces_x, place, weight_one) + bias_one[None, :, None]
    hidden = (jax.nn.silu(hidden_pre) * live_mask).astype(jnp.bfloat16)
    pieces_h = halo_pieces(hidden, pool_rows)
    out_pre = conv_grid(hidden, pieces_h, place, weight_two) + bias_two[None, :, None]
    result = (jax.nn.silu(out_pre) * live_mask).astype(jnp.bfloat16)
    upstream = exact_dot(cotangent[0], to_cells, "scn,gn->scg")
    grad_out = (upstream.astype(jnp.float32) * live_mask * silu_slope(out_pre)).astype(jnp.bfloat16)
    grad_w_two = weight_grad(grad_out, hidden, pieces_h, place)
    grad_b_two = jnp.sum(grad_out.astype(jnp.float32), axis=(0, 2))
    pieces_g = halo_pieces(grad_out, pool_rows)
    hidden_grad = conv_grid(grad_out, pieces_g, place, back_rows)
    grad_hidden = (hidden_grad * (live_mask * valid) * silu_slope(hidden_pre)).astype(jnp.bfloat16)
    grad_w_one = weight_grad(grad_hidden, masked_grid, pieces_x, place)
    grad_b_one = jnp.sum(grad_hidden.astype(jnp.float32), axis=(0, 2))
    shared_all = share_grads(
        jnp.concatenate([grad_w_one, grad_w_two], axis=0),
        jnp.stack([grad_b_one, grad_b_two], axis=0),
    )
    total_w_one, total_w_two = (shared_all[0][:channels], shared_all[0][channels:])
    total_b_one, total_b_two = (shared_all[1][0], shared_all[1][1])
    output = exact_dot(result, to_cells, "scg,gn->scn")[None]
    return (output, total_w_one, total_w_two, total_b_one, total_b_two)


def solution(mesh):
    in_specs = (
        P("dp", "space", None, None),
        P("dp", None, None),
        P("dp", None),
        P("dp", "space", None, None),
        P(),
        P(),
        P(),
        P(),
    )
    out_specs = (P("dp", "space", None, None), P(), P(), P(), P())
    return jax.shard_map(local, mesh=mesh, in_specs=in_specs, out_specs=out_specs, check_vma=False)
```

```python
import jax
import numpy as np
import jax.numpy as jnp
from jax import lax
from jax.sharding import PartitionSpec as P
from jax.experimental import pallas as pl
from jax.experimental.pallas import tpu as pltpu

EDGE = 8


OFFSETS = [
    (a, b, c) for a in (-1, 0, 1) for b in (-1, 0, 1) for c in (-1, 0, 1) if (a, b, c) != (0, 0, 0)
]
grid_width = 896
flat_width = 1280


def shifted(value, axis, steps):
    count = lax.axis_size(axis)
    leading, last = (max(0, -steps), min(count, count - steps))
    return lax.ppermute(value, axis, [(source, source + steps) for source in range(leading, last)])


def face_index(offset):
    if offset[0] != 0:
        return 1 if offset[0] < 0 else 0
    if offset[1] != 0:
        return 3 if offset[1] < 0 else 2
    return 5 if offset[2] < 0 else 4


def face_span(shift_by, edge_len):
    if shift_by < 0:
        return slice(edge_len - 1, edge_len)
    if shift_by > 0:
        return slice(0, 1)
    return slice(0, edge_len)


def target(shift_by, edge_len):
    if shift_by < 0:
        return slice(0, 1)
    if shift_by > 0:
        return slice(edge_len + 1, edge_len + 2)
    return slice(1, edge_len + 1)


def grid_at(p, q, r):
    return p * (EDGE + 2) ** 2 + q * (EDGE + 2) + r


def face_cells():
    last = EDGE - 1
    cells = []
    for fixed_axis in range(3):
        for fixed_at in (0, last):
            for u in range(EDGE):
                for w in range(EDGE):
                    spot = [u, w]
                    spot.insert(fixed_axis, fixed_at)
                    cells.append(grid_at(*spot))
    return np.array(cells, np.int32)


def piece_layout():
    sources, targets, groups = [], [], []
    face_area = EDGE * EDGE
    for nonzero in (1, 2, 3):
        for k, offset in enumerate(OFFSETS):
            if sum(v != 0 for v in offset) != nonzero:
                continue
            a, b, c = offset
            base = face_index(offset) * face_area
            face = np.arange(base, base + face_area).reshape(EDGE, EDGE)
            if a != 0:
                part = face[face_span(b, EDGE), face_span(c, EDGE)]
            elif b != 0:
                part = face[:, face_span(c, EDGE)]
            else:
                part = face
            sources.extend(part.reshape(-1).tolist())
            groups.extend([k] * part.size)
            for pp in range(EDGE + 2)[target(a, EDGE)]:
                for qq in range(EDGE + 2)[target(b, EDGE)]:
                    for rr in range(EDGE + 2)[target(c, EDGE)]:
                        targets.append(grid_at(pp, qq, rr))
    return np.array(sources, np.int32), np.array(targets, np.int32), np.array(groups, np.int32)


def cell_grid():
    return np.array(
        [grid_at(p, q, r) for p in range(EDGE) for q in range(EDGE) for r in range(EDGE)], np.int32
    )


def one_hot(rows, columns):
    return (jnp.asarray(rows)[:, None] == jnp.asarray(columns)[None, :]).astype(jnp.bfloat16)


def placement():
    grid_ids = jnp.arange(grid_width, dtype=jnp.int32)
    cells = jnp.asarray(cell_grid())
    valid = jnp.zeros((grid_width,), jnp.int32).at[cells].set(1)
    center_target = jnp.where(valid > 0, grid_ids + grid_at(1, 1, 1), -1)
    from_center = one_hot(center_target, jnp.arange(flat_width, dtype=jnp.int32))
    piece_sources, piece_targets, piece_groups = piece_layout()
    from_pieces = one_hot(piece_targets, jnp.arange(flat_width, dtype=jnp.int32))
    return from_center, from_pieces


def exact_dot(left, right, spec):
    return jnp.einsum(spec, left, right, preferred_element_type=jnp.float32).astype(left.dtype)


def stacked_windows(whole):
    windows = []
    for b in range(3):
        for c in range(3):
            start = b * (EDGE + 2) + c
            moved = whole if start == 0 else pltpu.roll(whole, flat_width - start, 1)
            windows.append(moved.astype(jnp.bfloat16))
    return jnp.concatenate(windows, axis=0)


def fill_padded(grid_ref, piece_ref, center_ref, halo_ref, whole_ref):
    whole_ref[...] = jnp.dot(
        grid_ref[...], center_ref[...], preferred_element_type=jnp.float32
    ) + jnp.dot(piece_ref[...], halo_ref[...], preferred_element_type=jnp.float32)


def conv_kernel(grid_ref, piece_ref, center_ref, halo_ref, taps_ref, out_ref, whole_ref):
    plane = (EDGE + 2) ** 2
    channels = out_ref.shape[1]
    fill_padded(grid_ref, piece_ref, center_ref, halo_ref, whole_ref)

    def one_brick(brick, carry):
        whole = whole_ref[pl.ds(pl.multiple_of(brick * channels, channels), channels), :]
        product = jnp.dot(taps_ref[...], stacked_windows(whole), preferred_element_type=jnp.float32)
        summed = product[:channels]
        for a in (1, 2):
            summed = summed + pltpu.roll(
                product[a * channels : (a + 1) * channels], flat_width - a * plane, 1
            )
        out_ref[brick] = summed[:, :grid_width]
        return carry

    lax.fori_loop(0, out_ref.shape[0], one_brick, 0)


def weight_grad_kernel(grad_ref, grid_ref, piece_ref, center_ref, halo_ref, out_ref, whole_ref):
    plane = (EDGE + 2) ** 2
    channels = grad_ref.shape[1]
    fill_padded(grid_ref, piece_ref, center_ref, halo_ref, whole_ref)
    out_ref[...] = jnp.zeros(out_ref.shape, jnp.float32)

    def one_brick(brick, carry):
        whole = whole_ref[pl.ds(pl.multiple_of(brick * channels, channels), channels), :]
        grad_cells = grad_ref[brick].astype(jnp.float32)
        grad_wide = jnp.concatenate(
            [grad_cells, jnp.zeros((channels, flat_width - grid_width), jnp.float32)], axis=1
        )
        moved = [grad_wide] + [pltpu.roll(grad_wide, a * plane, 1) for a in (1, 2)]
        out_ref[...] += lax.dot_general(
            jnp.concatenate(moved, axis=0).astype(jnp.bfloat16),
            stacked_windows(whole),
            (((1,), (1,)), ((), ())),
            preferred_element_type=jnp.float32,
        )
        return carry

    lax.fori_loop(0, grad_ref.shape[0], one_brick, 0)


def vmem_specs(count):
    return [pl.BlockSpec(memory_space=pltpu.VMEM)] * count


def tap_rows(weight_rows):
    channels = weight_rows.shape[0]
    return jnp.transpose(weight_rows.reshape(channels, 3, 9 * channels), (1, 0, 2)).reshape(
        3 * channels, 9 * channels
    )


def conv_grid(grid_cells, pieces, place, weight_rows):
    slot_count, channels = (grid_cells.shape[0], weight_rows.shape[0])
    return pl.pallas_call(
        conv_kernel,
        out_shape=jax.ShapeDtypeStruct((slot_count, channels, grid_width), jnp.float32),
        in_specs=vmem_specs(5),
        out_specs=pl.BlockSpec(memory_space=pltpu.VMEM),
        scratch_shapes=[pltpu.VMEM((slot_count * channels, flat_width), jnp.float32)],
        cost_estimate=pl.CostEstimate(
            flops=2 * slot_count * channels * flat_width * (weight_rows.shape[1] + 1400),
            bytes_accessed=grid_cells.size * 2 + pieces.size * 2 + 3 * 2**20 + slot_count * channels * grid_width * 4,
            transcendentals=0,
        ),
    )(
        grid_cells.reshape(slot_count * channels, grid_width),
        pieces.reshape(slot_count * channels, pieces.shape[2]),
        place[0],
        place[1],
        tap_rows(weight_rows),
    )


def weight_grad(grad_cells, grid_cells, pieces, place):
    slot_count, channels = (grid_cells.shape[0], grid_cells.shape[1])
    per_depth = pl.pallas_call(
        weight_grad_kernel,
        out_shape=jax.ShapeDtypeStruct((3 * channels, 9 * channels), jnp.float32),
        in_specs=vmem_specs(5),
        out_specs=pl.BlockSpec(memory_space=pltpu.VMEM),
        scratch_shapes=[pltpu.VMEM((slot_count * channels, flat_width), jnp.float32)],
        cost_estimate=pl.CostEstimate(
            flops=2 * slot_count * channels * flat_width * (27 * channels + 1400),
            bytes_accessed=grid_cells.size * 4 + pieces.size * 2 + 3 * 2**20 + 27 * channels * channels * 4,
            transcendentals=0,
        ),
    )(
        grad_cells,
        grid_cells.reshape(slot_count * channels, grid_width),
        pieces.reshape(slot_count * channels, pieces.shape[2]),
        place[0],
        place[1],
    )
    return jnp.transpose(per_depth.reshape(3, channels, 9 * channels), (1, 0, 2)).reshape(
        channels, 27 * channels
    )


HALO_SHIFTS = (-3, -2, -1, 1, 2, 3)


def halo_kernel(faces_ref, pool_ref, send_sems, recv_sems):
    me = lax.axis_index("space")
    column = lax.axis_index("dp")
    count = lax.axis_size("space")
    centre = len(HALO_SHIFTS) // 2
    first_lanes = 2 * EDGE * EDGE
    pool_ref[...] = jnp.zeros(pool_ref.shape, pool_ref.dtype)
    pool_ref[centre] = faces_ref[...]
    barrier = pltpu.get_barrier_semaphore()
    partners = 0
    for shift in HALO_SHIFTS:
        target = me - shift
        reachable = (target >= 0) & (target < count)
        partners = partners + reachable.astype(jnp.int32)

        @pl.when(reachable)
        def _():
            pl.semaphore_signal(
                barrier, 1, device_id=(target, column), device_id_type=pl.DeviceIdType.MESH
            )

    pl.semaphore_wait(barrier, partners)
    copies = []
    for index, shift in enumerate(HALO_SHIFTS):
        target = me - shift
        lanes = pl.ds(0, first_lanes) if abs(shift) > 1 else pl.ds(0, faces_ref.shape[2])
        copy = pltpu.make_async_remote_copy(
            src_ref=faces_ref.at[:, :, lanes],
            dst_ref=pool_ref.at[shift + centre, :, :, lanes],
            send_sem=send_sems.at[index],
            recv_sem=recv_sems.at[index],
            device_id=(jnp.clip(target, 0, count - 1), column),
            device_id_type=pl.DeviceIdType.MESH,
        )
        sends = (target >= 0) & (target < count)
        receives = (me + shift >= 0) & (me + shift < count)
        copies.append((copy, sends, receives))

        @pl.when(sends)
        def _():
            copy.start()

    for copy, sends, receives in copies:

        @pl.when(sends)
        def _():
            copy.wait_send()

        @pl.when(receives)
        def _():
            copy.wait_recv()


def build_pool(outer_faces):
    slot_count, channels, width = outer_faces.shape
    groups = len(HALO_SHIFTS) + 1
    pool = pl.pallas_call(
        halo_kernel,
        out_shape=jax.ShapeDtypeStruct((groups, slot_count, channels, width), outer_faces.dtype),
        in_specs=[pl.BlockSpec(memory_space=pltpu.VMEM)],
        out_specs=pl.BlockSpec(memory_space=pltpu.VMEM),
        scratch_shapes=[
            pltpu.SemaphoreType.DMA((len(HALO_SHIFTS),)),
            pltpu.SemaphoreType.DMA((len(HALO_SHIFTS),)),
        ],
        compiler_params=pltpu.CompilerParams(collective_id=1, has_side_effects=True),
    )(outer_faces)
    return pool.reshape(groups * slot_count, channels, width)


def halo_pieces(grid_cells, pool_rows):
    faces = exact_dot(grid_cells, one_hot(jnp.arange(grid_width, dtype=jnp.int32), face_cells()), "scg,gf->scf")
    pool = build_pool(faces)
    rows = pool.shape[0]
    piece_sources, piece_targets, piece_groups = piece_layout()
    table = exact_dot(pool, one_hot(jnp.arange(faces.shape[2], dtype=jnp.int32), piece_sources), "scf,fe->sce")
    chosen = jnp.take(pool_rows, jnp.asarray(piece_groups), axis=1)
    pick = (chosen[:, None, :] == jnp.arange(rows, dtype=jnp.int32)[None, :, None]).astype(jnp.float32)
    picked = jnp.sum(pick[:, :, None, :] * table.astype(jnp.float32)[None], axis=1)
    return picked.astype(grid_cells.dtype)


REDUCE_ORDERS = ((("core", 2), ("x", 4), ("y", 4), ("z", 4)), (("core", 2), ("y", 4), ("z", 4), ("x", 4)))


def own_coords():
    space = lax.axis_index("space")
    dp = lax.axis_index("dp")
    return {"core": space % 2, "x": dp % 4, "y": space // 2 % 4, "z": dp // 4 * 2 + space // 8}


def mesh_id(coords, name, value):
    moved = dict(coords)
    moved[name] = value
    space = ((moved["z"] % 2) * 4 + moved["y"]) * 2 + moved["core"]
    return (space, moved["z"] // 2 * 4 + moved["x"])


def exchange(copies):
    for copy in copies:
        copy.start()
    for copy in copies:
        copy.wait()


def all_reduce_kernel(*refs):
    lines = len(REDUCE_ORDERS)
    depth = len(REDUCE_ORDERS[0])
    x_ref, out_ref = refs[0], refs[1]
    per_line = (len(refs) - 4) // lines
    scratch = [refs[2 + p * per_line : 2 + (p + 1) * per_line] for p in range(lines)]
    send_sems, recv_sems = refs[-2], refs[-1]
    coords = own_coords()
    barrier = pltpu.get_barrier_semaphore()
    partner_count = 0
    for name, size in REDUCE_ORDERS[0]:
        for steps in range(1, size):
            pl.semaphore_signal(
                barrier, 1, device_id=mesh_id(coords, name, (coords[name] + steps) % size),
                device_id_type=pl.DeviceIdType.MESH,
            )
            partner_count += 1
    pl.semaphore_wait(barrier, partner_count)
    part = x_ref.shape[0] // lines
    sources = [x_ref.at[pl.ds(p * part, part)] for p in range(lines)]
    copy_id = 0
    for stage in range(depth):
        copies = []
        for p in range(lines):
            name, size = REDUCE_ORDERS[p][stage]
            me = coords[name]
            chunk = sources[p].shape[0] // size
            for steps in range(1, size):
                target = (me + steps) % size
                copies.append(pltpu.make_async_remote_copy(
                    src_ref=sources[p].at[pl.ds(pl.multiple_of(target * chunk, chunk), chunk)],
                    dst_ref=scratch[p][depth - 1 + stage].at[steps - 1],
                    send_sem=send_sems.at[copy_id],
                    recv_sem=recv_sems.at[copy_id],
                    device_id=mesh_id(coords, name, target),
                    device_id_type=pl.DeviceIdType.MESH,
                ))
                copy_id += 1
        exchange(copies)
        for p in range(lines):
            name, size = REDUCE_ORDERS[p][stage]
            me = coords[name]
            chunk = sources[p].shape[0] // size
            slots = scratch[p][depth - 1 + stage]
            total = sources[p][pl.ds(pl.multiple_of(me * chunk, chunk), chunk)]
            for steps in range(1, size):
                total = total + slots[steps - 1]
            if stage < depth - 1:
                scratch[p][stage][...] = total
                sources[p] = scratch[p][stage]
            else:
                scratch[p][2 * depth - 1][pl.ds(pl.multiple_of(me * chunk, chunk), chunk)] = total
    holders = [list(scratch[p][2 * depth - 1 : 2 * depth - 1 + depth - 1]) + [out_ref.at[pl.ds(p * part, part)]] for p in range(lines)]
    for level in range(depth):
        stage = depth - 1 - level
        copies = []
        for p in range(lines):
            name, size = REDUCE_ORDERS[p][stage]
            me = coords[name]
            holder = holders[p][level]
            piece = holder.shape[0] // size
            for steps in range(1, size):
                copies.append(pltpu.make_async_remote_copy(
                    src_ref=holder.at[pl.ds(pl.multiple_of(me * piece, piece), piece)],
                    dst_ref=scratch[p][3 * depth - 2 + level].at[steps - 1],
                    send_sem=send_sems.at[copy_id],
                    recv_sem=recv_sems.at[copy_id],
                    device_id=mesh_id(coords, name, (me + steps) % size),
                    device_id_type=pl.DeviceIdType.MESH,
                ))
                copy_id += 1
        exchange(copies)
        for p in range(lines):
            name, size = REDUCE_ORDERS[p][stage]
            me = coords[name]
            holder = holders[p][level]
            piece = holder.shape[0] // size
            slots = scratch[p][3 * depth - 2 + level]
            for steps in range(1, size):
                origin = (me - steps + size) % size
                holder[pl.ds(pl.multiple_of(origin * piece, piece), piece)] = slots[steps - 1]
            if level + 1 < depth:
                upper = holders[p][level + 1]
                next_me = coords[REDUCE_ORDERS[p][stage - 1][0]]
                span = holder.shape[0]
                upper[pl.ds(pl.multiple_of(next_me * span, span), span)] = holder[...]


def all_reduce_rows(flat):
    rows, lanes = flat.shape
    lines = len(REDUCE_ORDERS)
    part = rows // lines
    scratch = []
    copies = 0
    for order in REDUCE_ORDERS:
        sizes = [s for _, s in order]
        sums, reduce_slots, gather_slots, gathered = [], [], [], []
        current = part
        for size in sizes:
            current //= size
            reduce_slots.append((size - 1, current, lanes))
            sums.append((current, lanes))
        piece = current
        for size in reversed(sizes):
            gather_slots.append((size - 1, piece, lanes))
            piece *= size
            gathered.append((piece, lanes))
        shapes = sums[:-1] + reduce_slots + gathered[:-1] + gather_slots
        scratch += [pltpu.VMEM(s, jnp.float32) for s in shapes]
        copies += 2 * sum(s - 1 for s in sizes)
    scratch += [pltpu.SemaphoreType.DMA((copies,)), pltpu.SemaphoreType.DMA((copies,))]
    return pl.pallas_call(
        all_reduce_kernel,
        out_shape=jax.ShapeDtypeStruct(flat.shape, flat.dtype),
        in_specs=[pl.BlockSpec(memory_space=pltpu.VMEM)],
        out_specs=pl.BlockSpec(memory_space=pltpu.VMEM),
        scratch_shapes=scratch,
        compiler_params=pltpu.CompilerParams(collective_id=0, has_side_effects=True),
    )(flat)


def share_grads(weight_sums, bias_sums):
    flat = jnp.concatenate([weight_sums.reshape(-1), bias_sums.reshape(-1)])
    rows = 4096
    padded = jnp.pad(flat, (0, rows * 128 - flat.shape[0])).reshape(rows, 128)
    summed = all_reduce_rows(padded).reshape(-1)
    weight_total = summed[: weight_sums.size].reshape(weight_sums.shape)
    bias_total = summed[weight_sums.size : flat.shape[0]].reshape(bias_sums.shape)
    return weight_total, bias_total


def silu_slope(values):
    sigma = jax.nn.sigmoid(values)
    return sigma * (1.0 + values * (1.0 - sigma))


def local(volume, neighbours, active, cotangent, weight_one, weight_two, bias_one, bias_two):
    slot_count, channels = (volume.shape[1], volume.shape[2])
    position = lax.axis_index("space")
    own_alive = lax.dynamic_slice_in_dim(active[0], position * slot_count, slot_count, 0)
    near_table = lax.dynamic_slice_in_dim(neighbours[0], position * slot_count, slot_count, 0)
    safe_slot = jnp.maximum(near_table, 0)
    source_offset = safe_slot // slot_count - position + 3
    pool_rows = jnp.where(
        near_table < 0, 7 * slot_count, source_offset * slot_count + safe_slot % slot_count
    )
    live_mask = own_alive.astype(jnp.float32)[:, None, None]
    cells = jnp.asarray(cell_grid())
    to_cells = one_hot(jnp.arange(grid_width, dtype=jnp.int32), cells)
    valid = jnp.zeros((grid_width,), jnp.float32).at[cells].set(1.0)
    place = placement()
    back_rows = jnp.transpose(
        weight_two.reshape(channels, 27, channels)[:, ::-1, :], (2, 1, 0)
    ).reshape(channels, 27 * channels)
    masked = volume[0] * live_mask.astype(jnp.bfloat16)
    masked_grid = exact_dot(masked, to_cells, "scn,gn->scg")
    pieces_x = halo_pieces(masked_grid, pool_rows)
    hidden_pre = conv_grid(masked_grid, pieces_x, place, weight_one) + bias_one[None, :, None]
    hidden = (jax.nn.silu(hidden_pre) * live_mask).astype(jnp.bfloat16)
    pieces_h = halo_pieces(hidden, pool_rows)
    out_pre = conv_grid(hidden, pieces_h, place, weight_two) + bias_two[None, :, None]
    result = (jax.nn.silu(out_pre) * live_mask).astype(jnp.bfloat16)
    upstream = exact_dot(cotangent[0], to_cells, "scn,gn->scg")
    grad_out = (upstream.astype(jnp.float32) * live_mask * silu_slope(out_pre)).astype(jnp.bfloat16)
    grad_w_two = weight_grad(grad_out, hidden, pieces_h, place)
    grad_b_two = jnp.sum(grad_out.astype(jnp.float32), axis=(0, 2))
    pieces_g = halo_pieces(grad_out, pool_rows)
    hidden_grad = conv_grid(grad_out, pieces_g, place, back_rows)
    grad_hidden = (hidden_grad * (live_mask * valid) * silu_slope(hidden_pre)).astype(jnp.bfloat16)
    grad_w_one = weight_grad(grad_hidden, masked_grid, pieces_x, place)
    grad_b_one = jnp.sum(grad_hidden.astype(jnp.float32), axis=(0, 2))
    shared_all = share_grads(
        jnp.concatenate([grad_w_one, grad_w_two], axis=0),
        jnp.stack([grad_b_one, grad_b_two], axis=0),
    )
    total_w_one, total_w_two = (shared_all[0][:channels], shared_all[0][channels:])
    total_b_one, total_b_two = (shared_all[1][0], shared_all[1][1])
    output = exact_dot(result, to_cells, "scg,gn->scn")[None]
    return (output, total_w_one, total_w_two, total_b_one, total_b_two)


def solution(mesh):
    in_specs = (
        P("dp", "space", None, None),
        P("dp", None, None),
        P("dp", None),
        P("dp", "space", None, None),
        P(),
        P(),
        P(),
        P(),
    )
    out_specs = (P("dp", "space", None, None), P(), P(), P(), P())
    return jax.shard_map(local, mesh=mesh, in_specs=in_specs, out_specs=out_specs, check_vma=False)
```

```python
import jax
import numpy as np
import jax.numpy as jnp
from jax import lax
from jax.sharding import PartitionSpec as P
from jax.experimental import pallas as pl
from jax.experimental.pallas import tpu as pltpu

EDGE = 8


OFFSETS = [
    (a, b, c) for a in (-1, 0, 1) for b in (-1, 0, 1) for c in (-1, 0, 1) if (a, b, c) != (0, 0, 0)
]
grid_width = 896
flat_width = 1280


def shifted(value, axis, steps):
    count = lax.axis_size(axis)
    leading, last = (max(0, -steps), min(count, count - steps))
    return lax.ppermute(value, axis, [(source, source + steps) for source in range(leading, last)])


def face_index(offset):
    if offset[0] != 0:
        return 1 if offset[0] < 0 else 0
    if offset[1] != 0:
        return 3 if offset[1] < 0 else 2
    return 5 if offset[2] < 0 else 4


def face_span(shift_by, edge_len):
    if shift_by < 0:
        return slice(edge_len - 1, edge_len)
    if shift_by > 0:
        return slice(0, 1)
    return slice(0, edge_len)


def target(shift_by, edge_len):
    if shift_by < 0:
        return slice(0, 1)
    if shift_by > 0:
        return slice(edge_len + 1, edge_len + 2)
    return slice(1, edge_len + 1)


def grid_at(p, q, r):
    return p * (EDGE + 2) ** 2 + q * (EDGE + 2) + r


def face_cells():
    last = EDGE - 1
    cells = []
    for fixed_axis in range(3):
        for fixed_at in (0, last):
            for u in range(EDGE):
                for w in range(EDGE):
                    spot = [u, w]
                    spot.insert(fixed_axis, fixed_at)
                    cells.append(grid_at(*spot))
    return np.array(cells, np.int32)


def piece_layout():
    sources, targets, groups = [], [], []
    face_area = EDGE * EDGE
    for nonzero in (1, 2, 3):
        for k, offset in enumerate(OFFSETS):
            if sum(v != 0 for v in offset) != nonzero:
                continue
            a, b, c = offset
            base = face_index(offset) * face_area
            face = np.arange(base, base + face_area).reshape(EDGE, EDGE)
            if a != 0:
                part = face[face_span(b, EDGE), face_span(c, EDGE)]
            elif b != 0:
                part = face[:, face_span(c, EDGE)]
            else:
                part = face
            sources.extend(part.reshape(-1).tolist())
            groups.extend([k] * part.size)
            for pp in range(EDGE + 2)[target(a, EDGE)]:
                for qq in range(EDGE + 2)[target(b, EDGE)]:
                    for rr in range(EDGE + 2)[target(c, EDGE)]:
                        targets.append(grid_at(pp, qq, rr))
    sources, targets, groups = (np.array(v, np.int32) for v in (sources, targets, groups))
    order = np.argsort(sources >= 2 * face_area, kind="stable")
    return sources[order], targets[order], groups[order]


def cell_grid():
    return np.array(
        [grid_at(p, q, r) for p in range(EDGE) for q in range(EDGE) for r in range(EDGE)], np.int32
    )


def one_hot(rows, columns):
    return (jnp.asarray(rows)[:, None] == jnp.asarray(columns)[None, :]).astype(jnp.bfloat16)


def placement():
    grid_ids = jnp.arange(grid_width, dtype=jnp.int32)
    cells = jnp.asarray(cell_grid())
    valid = jnp.zeros((grid_width,), jnp.int32).at[cells].set(1)
    center_target = jnp.where(valid > 0, grid_ids + grid_at(1, 1, 1), -1)
    from_center = one_hot(center_target, jnp.arange(flat_width, dtype=jnp.int32))
    piece_sources, piece_targets, piece_groups = piece_layout()
    from_pieces = one_hot(piece_targets, jnp.arange(flat_width, dtype=jnp.int32))
    return from_center, from_pieces


def exact_dot(left, right, spec):
    return jnp.einsum(spec, left, right, preferred_element_type=jnp.float32).astype(left.dtype)


def stacked_windows(whole):
    windows = []
    for b in range(3):
        for c in range(3):
            start = b * (EDGE + 2) + c
            moved = whole if start == 0 else pltpu.roll(whole, flat_width - start, 1)
            windows.append(moved.astype(jnp.bfloat16))
    return jnp.concatenate(windows, axis=0)


def fill_padded(grid_ref, piece_ref, center_ref, halo_ref, whole_ref):
    whole_ref[...] = jnp.dot(
        grid_ref[...], center_ref[...], preferred_element_type=jnp.float32
    ) + jnp.dot(piece_ref[...], halo_ref[...], preferred_element_type=jnp.float32)


def conv_kernel(grid_ref, piece_ref, center_ref, halo_ref, taps_ref, out_ref, whole_ref):
    plane = (EDGE + 2) ** 2
    channels = out_ref.shape[1]
    fill_padded(grid_ref, piece_ref, center_ref, halo_ref, whole_ref)

    def one_brick(brick, carry):
        whole = whole_ref[pl.ds(pl.multiple_of(brick * channels, channels), channels), :]
        product = jnp.dot(taps_ref[...], stacked_windows(whole), preferred_element_type=jnp.float32)
        summed = product[:channels]
        for a in (1, 2):
            summed = summed + pltpu.roll(
                product[a * channels : (a + 1) * channels], flat_width - a * plane, 1
            )
        out_ref[brick] = summed[:, :grid_width]
        return carry

    lax.fori_loop(0, out_ref.shape[0], one_brick, 0)


def weight_grad_kernel(grad_ref, grid_ref, piece_ref, center_ref, halo_ref, out_ref, whole_ref):
    plane = (EDGE + 2) ** 2
    channels = grad_ref.shape[1]
    fill_padded(grid_ref, piece_ref, center_ref, halo_ref, whole_ref)
    out_ref[...] = jnp.zeros(out_ref.shape, jnp.float32)

    def one_brick(brick, carry):
        whole = whole_ref[pl.ds(pl.multiple_of(brick * channels, channels), channels), :]
        grad_cells = grad_ref[brick].astype(jnp.float32)
        grad_wide = jnp.concatenate(
            [grad_cells, jnp.zeros((channels, flat_width - grid_width), jnp.float32)], axis=1
        )
        moved = [grad_wide] + [pltpu.roll(grad_wide, a * plane, 1) for a in (1, 2)]
        out_ref[...] += lax.dot_general(
            jnp.concatenate(moved, axis=0).astype(jnp.bfloat16),
            stacked_windows(whole),
            (((1,), (1,)), ((), ())),
            preferred_element_type=jnp.float32,
        )
        return carry

    lax.fori_loop(0, grad_ref.shape[0], one_brick, 0)


def vmem_specs(count):
    return [pl.BlockSpec(memory_space=pltpu.VMEM)] * count


def tap_rows(weight_rows):
    channels = weight_rows.shape[0]
    return jnp.transpose(weight_rows.reshape(channels, 3, 9 * channels), (1, 0, 2)).reshape(
        3 * channels, 9 * channels
    )


def conv_grid(grid_cells, pieces, place, weight_rows):
    slot_count, channels = (grid_cells.shape[0], weight_rows.shape[0])
    return pl.pallas_call(
        conv_kernel,
        out_shape=jax.ShapeDtypeStruct((slot_count, channels, grid_width), jnp.float32),
        in_specs=vmem_specs(5),
        out_specs=pl.BlockSpec(memory_space=pltpu.VMEM),
        scratch_shapes=[pltpu.VMEM((slot_count * channels, flat_width), jnp.float32)],
        cost_estimate=pl.CostEstimate(
            flops=2 * slot_count * channels * flat_width * (weight_rows.shape[1] + 1400),
            bytes_accessed=grid_cells.size * 2 + pieces.size * 2 + 3 * 2**20 + slot_count * channels * grid_width * 4,
            transcendentals=0,
        ),
    )(
        grid_cells.reshape(slot_count * channels, grid_width),
        pieces.reshape(slot_count * channels, pieces.shape[2]),
        place[0],
        place[1],
        tap_rows(weight_rows),
    )


def weight_grad(grad_cells, grid_cells, pieces, place):
    slot_count, channels = (grid_cells.shape[0], grid_cells.shape[1])
    per_depth = pl.pallas_call(
        weight_grad_kernel,
        out_shape=jax.ShapeDtypeStruct((3 * channels, 9 * channels), jnp.float32),
        in_specs=vmem_specs(5),
        out_specs=pl.BlockSpec(memory_space=pltpu.VMEM),
        scratch_shapes=[pltpu.VMEM((slot_count * channels, flat_width), jnp.float32)],
        cost_estimate=pl.CostEstimate(
            flops=2 * slot_count * channels * flat_width * (27 * channels + 1400),
            bytes_accessed=grid_cells.size * 4 + pieces.size * 2 + 3 * 2**20 + 27 * channels * channels * 4,
            transcendentals=0,
        ),
    )(
        grad_cells,
        grid_cells.reshape(slot_count * channels, grid_width),
        pieces.reshape(slot_count * channels, pieces.shape[2]),
        place[0],
        place[1],
    )
    return per_depth


def from_depth_rows(per_depth):
    channels = per_depth.shape[0] // 3
    return jnp.transpose(per_depth.reshape(3, channels, 9 * channels), (1, 0, 2)).reshape(
        channels, 27 * channels
    )


HALO_SHIFTS = (-3, -2, -1, 1, 2, 3)


def halo_kernel(faces_ref, pool_ref, send_sems, recv_sems):
    me = lax.axis_index("space")
    column = lax.axis_index("dp")
    count = lax.axis_size("space")
    centre = len(HALO_SHIFTS) // 2
    first_lanes = 2 * EDGE * EDGE
    pool_ref[...] = jnp.zeros(pool_ref.shape, pool_ref.dtype)
    pool_ref[centre] = faces_ref[...]
    barrier = pltpu.get_barrier_semaphore()
    partners = 0
    for shift in HALO_SHIFTS:
        target = me - shift
        reachable = (target >= 0) & (target < count)
        partners = partners + reachable.astype(jnp.int32)

        @pl.when(reachable)
        def _():
            pl.semaphore_signal(
                barrier, 1, device_id=(target, column), device_id_type=pl.DeviceIdType.MESH
            )

    pl.semaphore_wait(barrier, partners)
    copies = []
    for index, shift in enumerate(HALO_SHIFTS):
        target = me - shift
        lanes = pl.ds(0, first_lanes) if abs(shift) > 1 else pl.ds(0, faces_ref.shape[2])
        copy = pltpu.make_async_remote_copy(
            src_ref=faces_ref.at[:, :, lanes],
            dst_ref=pool_ref.at[shift + centre, :, :, lanes],
            send_sem=send_sems.at[index],
            recv_sem=recv_sems.at[index],
            device_id=(jnp.clip(target, 0, count - 1), column),
            device_id_type=pl.DeviceIdType.MESH,
        )
        sends = (target >= 0) & (target < count)
        receives = (me + shift >= 0) & (me + shift < count)
        copies.append((copy, sends, receives))

        @pl.when(sends)
        def _():
            copy.start()

    for copy, sends, receives in copies:

        @pl.when(sends)
        def _():
            copy.wait_send()

        @pl.when(receives)
        def _():
            copy.wait_recv()


def build_pool(outer_faces):
    slot_count, channels, width = outer_faces.shape
    groups = len(HALO_SHIFTS) + 1
    pool = pl.pallas_call(
        halo_kernel,
        out_shape=jax.ShapeDtypeStruct((groups, slot_count, channels, width), outer_faces.dtype),
        in_specs=[pl.BlockSpec(memory_space=pltpu.VMEM)],
        out_specs=pl.BlockSpec(memory_space=pltpu.VMEM),
        scratch_shapes=[
            pltpu.SemaphoreType.DMA((len(HALO_SHIFTS),)),
            pltpu.SemaphoreType.DMA((len(HALO_SHIFTS),)),
        ],
        compiler_params=pltpu.CompilerParams(collective_id=1, has_side_effects=True),
    )(outer_faces)
    return pool.reshape(groups * slot_count, channels, width)


def halo_pieces(grid_cells, pool_rows):
    faces = exact_dot(grid_cells, one_hot(jnp.arange(grid_width, dtype=jnp.int32), face_cells()), "scg,gf->scf")
    pool = build_pool(faces)
    rows = pool.shape[0]
    piece_sources, piece_targets, piece_groups = piece_layout()
    split = 2 * EDGE * EDGE
    leading = int(np.sum(piece_sources < split))
    table = jnp.concatenate(
        [
            exact_dot(pool[:, :, :split], one_hot(jnp.arange(split, dtype=jnp.int32), piece_sources[:leading]), "scf,fe->sce"),
            exact_dot(pool[:, :, split:], one_hot(jnp.arange(split, faces.shape[2], dtype=jnp.int32), piece_sources[leading:]), "scf,fe->sce"),
        ],
        axis=2,
    )
    chosen = jnp.take(pool_rows, jnp.asarray(piece_groups), axis=1)
    pick = (chosen[:, None, :] == jnp.arange(rows, dtype=jnp.int32)[None, :, None]).astype(jnp.float32)
    picked = jnp.sum(pick[:, :, None, :] * table.astype(jnp.float32)[None], axis=1)
    return picked.astype(grid_cells.dtype)


REDUCE_ORDERS = ((("core", 2), ("x", 4), ("y", 4), ("z", 4)), (("core", 2), ("y", 4), ("z", 4), ("x", 4)))


def own_coords():
    space = lax.axis_index("space")
    dp = lax.axis_index("dp")
    return {"core": space % 2, "x": dp % 4, "y": space // 2 % 4, "z": dp // 4 * 2 + space // 8}


def mesh_id(coords, name, value):
    moved = dict(coords)
    moved[name] = value
    space = ((moved["z"] % 2) * 4 + moved["y"]) * 2 + moved["core"]
    return (space, moved["z"] // 2 * 4 + moved["x"])


def exchange(copies):
    for copy in copies:
        copy.start()
    for copy in copies:
        copy.wait()


def all_reduce_kernel(*refs):
    lines = len(REDUCE_ORDERS)
    depth = len(REDUCE_ORDERS[0])
    x_ref, out_ref = refs[0], refs[1]
    per_line = (len(refs) - 4) // lines
    scratch = [refs[2 + p * per_line : 2 + (p + 1) * per_line] for p in range(lines)]
    send_sems, recv_sems = refs[-2], refs[-1]
    coords = own_coords()
    barrier = pltpu.get_barrier_semaphore()
    partner_count = 0
    for name, size in REDUCE_ORDERS[0]:
        for steps in range(1, size):
            pl.semaphore_signal(
                barrier, 1, device_id=mesh_id(coords, name, (coords[name] + steps) % size),
                device_id_type=pl.DeviceIdType.MESH,
            )
            partner_count += 1
    pl.semaphore_wait(barrier, partner_count)
    part = x_ref.shape[0] // lines
    sources = [x_ref.at[pl.ds(p * part, part)] for p in range(lines)]
    copy_id = 0
    for stage in range(depth):
        copies = []
        for p in range(lines):
            name, size = REDUCE_ORDERS[p][stage]
            me = coords[name]
            chunk = sources[p].shape[0] // size
            for steps in range(1, size):
                target = (me + steps) % size
                copies.append(pltpu.make_async_remote_copy(
                    src_ref=sources[p].at[pl.ds(pl.multiple_of(target * chunk, chunk), chunk)],
                    dst_ref=scratch[p][depth - 1 + stage].at[steps - 1],
                    send_sem=send_sems.at[copy_id],
                    recv_sem=recv_sems.at[copy_id],
                    device_id=mesh_id(coords, name, target),
                    device_id_type=pl.DeviceIdType.MESH,
                ))
                copy_id += 1
        exchange(copies)
        for p in range(lines):
            name, size = REDUCE_ORDERS[p][stage]
            me = coords[name]
            chunk = sources[p].shape[0] // size
            slots = scratch[p][depth - 1 + stage]
            total = sources[p][pl.ds(pl.multiple_of(me * chunk, chunk), chunk)]
            for steps in range(1, size):
                total = total + slots[steps - 1]
            if stage < depth - 1:
                scratch[p][stage][...] = total
                sources[p] = scratch[p][stage]
            else:
                scratch[p][2 * depth - 1][pl.ds(pl.multiple_of(me * chunk, chunk), chunk)] = total
    holders = [list(scratch[p][2 * depth - 1 : 2 * depth - 1 + depth - 1]) + [out_ref.at[pl.ds(p * part, part)]] for p in range(lines)]
    for level in range(depth):
        stage = depth - 1 - level
        copies = []
        for p in range(lines):
            name, size = REDUCE_ORDERS[p][stage]
            me = coords[name]
            holder = holders[p][level]
            piece = holder.shape[0] // size
            for steps in range(1, size):
                copies.append(pltpu.make_async_remote_copy(
                    src_ref=holder.at[pl.ds(pl.multiple_of(me * piece, piece), piece)],
                    dst_ref=scratch[p][3 * depth - 2 + level].at[steps - 1],
                    send_sem=send_sems.at[copy_id],
                    recv_sem=recv_sems.at[copy_id],
                    device_id=mesh_id(coords, name, (me + steps) % size),
                    device_id_type=pl.DeviceIdType.MESH,
                ))
                copy_id += 1
        exchange(copies)
        for p in range(lines):
            name, size = REDUCE_ORDERS[p][stage]
            me = coords[name]
            holder = holders[p][level]
            piece = holder.shape[0] // size
            slots = scratch[p][3 * depth - 2 + level]
            for steps in range(1, size):
                origin = (me - steps + size) % size
                holder[pl.ds(pl.multiple_of(origin * piece, piece), piece)] = slots[steps - 1]
            if level + 1 < depth:
                upper = holders[p][level + 1]
                next_me = coords[REDUCE_ORDERS[p][stage - 1][0]]
                span = holder.shape[0]
                upper[pl.ds(pl.multiple_of(next_me * span, span), span)] = holder[...]


def all_reduce_rows(flat):
    rows, lanes = flat.shape
    lines = len(REDUCE_ORDERS)
    part = rows // lines
    scratch = []
    copies = 0
    for order in REDUCE_ORDERS:
        sizes = [s for _, s in order]
        sums, reduce_slots, gather_slots, gathered = [], [], [], []
        current = part
        for size in sizes:
            current //= size
            reduce_slots.append((size - 1, current, lanes))
            sums.append((current, lanes))
        piece = current
        for size in reversed(sizes):
            gather_slots.append((size - 1, piece, lanes))
            piece *= size
            gathered.append((piece, lanes))
        shapes = sums[:-1] + reduce_slots + gathered[:-1] + gather_slots
        scratch += [pltpu.VMEM(s, jnp.float32) for s in shapes]
        copies += 2 * sum(s - 1 for s in sizes)
    scratch += [pltpu.SemaphoreType.DMA((copies,)), pltpu.SemaphoreType.DMA((copies,))]
    return pl.pallas_call(
        all_reduce_kernel,
        out_shape=jax.ShapeDtypeStruct(flat.shape, flat.dtype),
        in_specs=[pl.BlockSpec(memory_space=pltpu.VMEM)],
        out_specs=pl.BlockSpec(memory_space=pltpu.VMEM),
        scratch_shapes=scratch,
        compiler_params=pltpu.CompilerParams(collective_id=0, has_side_effects=True),
    )(flat)


def share_grads(weight_sums, bias_sums):
    flat = jnp.concatenate([weight_sums.reshape(-1), bias_sums.reshape(-1)])
    rows = 4096
    padded = jnp.pad(flat, (0, rows * 128 - flat.shape[0])).reshape(rows, 128)
    summed = all_reduce_rows(padded).reshape(-1)
    weight_total = summed[: weight_sums.size].reshape(weight_sums.shape)
    bias_total = summed[weight_sums.size : flat.shape[0]].reshape(bias_sums.shape)
    return weight_total, bias_total


def silu_slope(values):
    sigma = jax.nn.sigmoid(values)
    return sigma * (1.0 + values * (1.0 - sigma))


def local(volume, neighbours, active, cotangent, weight_one, weight_two, bias_one, bias_two):
    slot_count, channels = (volume.shape[1], volume.shape[2])
    position = lax.axis_index("space")
    own_alive = lax.dynamic_slice_in_dim(active[0], position * slot_count, slot_count, 0)
    near_table = lax.dynamic_slice_in_dim(neighbours[0], position * slot_count, slot_count, 0)
    safe_slot = jnp.maximum(near_table, 0)
    source_offset = safe_slot // slot_count - position + 3
    pool_rows = jnp.where(
        near_table < 0, 7 * slot_count, source_offset * slot_count + safe_slot % slot_count
    )
    live_mask = own_alive.astype(jnp.float32)[:, None, None]
    cells = jnp.asarray(cell_grid())
    to_cells = one_hot(jnp.arange(grid_width, dtype=jnp.int32), cells)
    valid = jnp.zeros((grid_width,), jnp.float32).at[cells].set(1.0)
    place = placement()
    back_rows = jnp.transpose(
        weight_two.reshape(channels, 27, channels)[:, ::-1, :], (2, 1, 0)
    ).reshape(channels, 27 * channels)
    masked = volume[0] * live_mask.astype(jnp.bfloat16)
    masked_grid = exact_dot(masked, to_cells, "scn,gn->scg")
    pieces_x = halo_pieces(masked_grid, pool_rows)
    hidden_pre = conv_grid(masked_grid, pieces_x, place, weight_one) + bias_one[None, :, None]
    hidden = (jax.nn.silu(hidden_pre) * live_mask).astype(jnp.bfloat16)
    pieces_h = halo_pieces(hidden, pool_rows)
    out_pre = conv_grid(hidden, pieces_h, place, weight_two) + bias_two[None, :, None]
    result = (jax.nn.silu(out_pre) * live_mask).astype(jnp.bfloat16)
    upstream = exact_dot(cotangent[0], to_cells, "scn,gn->scg")
    grad_out = (upstream.astype(jnp.float32) * live_mask * silu_slope(out_pre)).astype(jnp.bfloat16)
    grad_w_two = weight_grad(grad_out, hidden, pieces_h, place)
    grad_b_two = jnp.sum(grad_out.astype(jnp.float32), axis=(0, 2))
    pieces_g = halo_pieces(grad_out, pool_rows)
    hidden_grad = conv_grid(grad_out, pieces_g, place, back_rows)
    grad_hidden = (hidden_grad * (live_mask * valid) * silu_slope(hidden_pre)).astype(jnp.bfloat16)
    grad_w_one = weight_grad(grad_hidden, masked_grid, pieces_x, place)
    grad_b_one = jnp.sum(grad_hidden.astype(jnp.float32), axis=(0, 2))
    shared_all = share_grads(
        jnp.concatenate([grad_w_one, grad_w_two], axis=0),
        jnp.stack([grad_b_one, grad_b_two], axis=0),
    )
    total_w_one = from_depth_rows(shared_all[0][: 3 * channels])
    total_w_two = from_depth_rows(shared_all[0][3 * channels :])
    total_b_one, total_b_two = (shared_all[1][0], shared_all[1][1])
    output = exact_dot(result, to_cells, "scg,gn->scn")[None]
    return (output, total_w_one, total_w_two, total_b_one, total_b_two)


def solution(mesh):
    in_specs = (
        P("dp", "space", None, None),
        P("dp", None, None),
        P("dp", None),
        P("dp", "space", None, None),
        P(),
        P(),
        P(),
        P(),
    )
    out_specs = (P("dp", "space", None, None), P(), P(), P(), P())
    return jax.shard_map(local, mesh=mesh, in_specs=in_specs, out_specs=out_specs, check_vma=False)
```

```python
import jax
import numpy as np
import jax.numpy as jnp
from jax import lax
from jax.sharding import PartitionSpec as P
from jax.experimental import pallas as pl
from jax.experimental.pallas import tpu as pltpu

EDGE = 8


OFFSETS = [
    (a, b, c) for a in (-1, 0, 1) for b in (-1, 0, 1) for c in (-1, 0, 1) if (a, b, c) != (0, 0, 0)
]
grid_width = 896
flat_width = 1280


def shifted(value, axis, steps):
    count = lax.axis_size(axis)
    leading, last = (max(0, -steps), min(count, count - steps))
    return lax.ppermute(value, axis, [(source, source + steps) for source in range(leading, last)])


def face_index(offset):
    if offset[0] != 0:
        return 1 if offset[0] < 0 else 0
    if offset[1] != 0:
        return 3 if offset[1] < 0 else 2
    return 5 if offset[2] < 0 else 4


def face_span(shift_by, edge_len):
    if shift_by < 0:
        return slice(edge_len - 1, edge_len)
    if shift_by > 0:
        return slice(0, 1)
    return slice(0, edge_len)


def target(shift_by, edge_len):
    if shift_by < 0:
        return slice(0, 1)
    if shift_by > 0:
        return slice(edge_len + 1, edge_len + 2)
    return slice(1, edge_len + 1)


def grid_at(p, q, r):
    return p * (EDGE + 2) ** 2 + q * (EDGE + 2) + r


def face_cells():
    last = EDGE - 1
    cells = []
    for fixed_axis in range(3):
        for fixed_at in (0, last):
            for u in range(EDGE):
                for w in range(EDGE):
                    spot = [u, w]
                    spot.insert(fixed_axis, fixed_at)
                    cells.append(grid_at(*spot))
    return np.array(cells, np.int32)


def piece_layout():
    sources, targets, groups = [], [], []
    face_area = EDGE * EDGE
    for nonzero in (1, 2, 3):
        for k, offset in enumerate(OFFSETS):
            if sum(v != 0 for v in offset) != nonzero:
                continue
            a, b, c = offset
            base = face_index(offset) * face_area
            face = np.arange(base, base + face_area).reshape(EDGE, EDGE)
            if a != 0:
                part = face[face_span(b, EDGE), face_span(c, EDGE)]
            elif b != 0:
                part = face[:, face_span(c, EDGE)]
            else:
                part = face
            sources.extend(part.reshape(-1).tolist())
            groups.extend([k] * part.size)
            for pp in range(EDGE + 2)[target(a, EDGE)]:
                for qq in range(EDGE + 2)[target(b, EDGE)]:
                    for rr in range(EDGE + 2)[target(c, EDGE)]:
                        targets.append(grid_at(pp, qq, rr))
    return np.array(sources, np.int32), np.array(targets, np.int32), np.array(groups, np.int32)


def cell_grid():
    return np.array(
        [grid_at(p, q, r) for p in range(EDGE) for q in range(EDGE) for r in range(EDGE)], np.int32
    )


def one_hot(rows, columns):
    return (jnp.asarray(rows)[:, None] == jnp.asarray(columns)[None, :]).astype(jnp.bfloat16)


def placement():
    grid_ids = jnp.arange(grid_width, dtype=jnp.int32)
    cells = jnp.asarray(cell_grid())
    valid = jnp.zeros((grid_width,), jnp.int32).at[cells].set(1)
    center_target = jnp.where(valid > 0, grid_ids + grid_at(1, 1, 1), -1)
    from_center = one_hot(center_target, jnp.arange(flat_width, dtype=jnp.int32))
    piece_sources, piece_targets, piece_groups = piece_layout()
    from_pieces = one_hot(piece_targets, jnp.arange(flat_width, dtype=jnp.int32))
    return from_center, from_pieces


def exact_dot(left, right, spec):
    return jnp.einsum(spec, left, right, preferred_element_type=jnp.float32).astype(left.dtype)


def stacked_windows(whole):
    windows = []
    for b in range(3):
        for c in range(3):
            start = b * (EDGE + 2) + c
            moved = whole if start == 0 else pltpu.roll(whole, flat_width - start, 1)
            windows.append(moved.astype(jnp.bfloat16))
    return jnp.concatenate(windows, axis=0)


def fill_padded(grid_ref, piece_ref, center_ref, halo_ref, whole_ref):
    whole_ref[...] = jnp.dot(
        grid_ref[...], center_ref[...], preferred_element_type=jnp.float32
    ) + jnp.dot(piece_ref[...], halo_ref[...], preferred_element_type=jnp.float32)


def conv_kernel(grid_ref, piece_ref, center_ref, halo_ref, taps_ref, out_ref, whole_ref):
    plane = (EDGE + 2) ** 2
    channels = out_ref.shape[1]
    fill_padded(grid_ref, piece_ref, center_ref, halo_ref, whole_ref)

    def one_brick(brick, carry):
        whole = whole_ref[pl.ds(pl.multiple_of(brick * channels, channels), channels), :]
        product = jnp.dot(taps_ref[...], stacked_windows(whole), preferred_element_type=jnp.float32)
        summed = product[:channels]
        for a in (1, 2):
            summed = summed + pltpu.roll(
                product[a * channels : (a + 1) * channels], flat_width - a * plane, 1
            )
        out_ref[brick] = summed[:, :grid_width]
        return carry

    lax.fori_loop(0, out_ref.shape[0], one_brick, 0)


def weight_grad_kernel(grad_ref, grid_ref, piece_ref, center_ref, halo_ref, out_ref, whole_ref):
    plane = (EDGE + 2) ** 2
    channels = grad_ref.shape[1]
    fill_padded(grid_ref, piece_ref, center_ref, halo_ref, whole_ref)
    out_ref[...] = jnp.zeros(out_ref.shape, jnp.float32)

    def one_brick(brick, carry):
        whole = whole_ref[pl.ds(pl.multiple_of(brick * channels, channels), channels), :]
        grad_cells = grad_ref[brick].astype(jnp.float32)
        grad_wide = jnp.concatenate(
            [grad_cells, jnp.zeros((channels, flat_width - grid_width), jnp.float32)], axis=1
        )
        moved = [grad_wide] + [pltpu.roll(grad_wide, a * plane, 1) for a in (1, 2)]
        out_ref[...] += lax.dot_general(
            jnp.concatenate(moved, axis=0).astype(jnp.bfloat16),
            stacked_windows(whole),
            (((1,), (1,)), ((), ())),
            preferred_element_type=jnp.float32,
        )
        return carry

    lax.fori_loop(0, grad_ref.shape[0], one_brick, 0)


def vmem_specs(count):
    return [pl.BlockSpec(memory_space=pltpu.VMEM)] * count


def tap_rows(weight_rows):
    channels = weight_rows.shape[0]
    return jnp.transpose(weight_rows.reshape(channels, 3, 9 * channels), (1, 0, 2)).reshape(
        3 * channels, 9 * channels
    )


def conv_grid(grid_cells, pieces, place, weight_rows):
    slot_count, channels = (grid_cells.shape[0], weight_rows.shape[0])
    return pl.pallas_call(
        conv_kernel,
        out_shape=jax.ShapeDtypeStruct((slot_count, channels, grid_width), jnp.float32),
        in_specs=vmem_specs(5),
        out_specs=pl.BlockSpec(memory_space=pltpu.VMEM),
        scratch_shapes=[pltpu.VMEM((slot_count * channels, flat_width), jnp.float32)],
        cost_estimate=pl.CostEstimate(
            flops=2 * slot_count * channels * flat_width * (weight_rows.shape[1] + 1400),
            bytes_accessed=grid_cells.size * 2 + pieces.size * 2 + 3 * 2**20 + slot_count * channels * grid_width * 4,
            transcendentals=0,
        ),
    )(
        grid_cells.reshape(slot_count * channels, grid_width),
        pieces.reshape(slot_count * channels, pieces.shape[2]),
        place[0],
        place[1],
        tap_rows(weight_rows),
    )


def weight_grad(grad_cells, grid_cells, pieces, place):
    slot_count, channels = (grid_cells.shape[0], grid_cells.shape[1])
    per_depth = pl.pallas_call(
        weight_grad_kernel,
        out_shape=jax.ShapeDtypeStruct((3 * channels, 9 * channels), jnp.float32),
        in_specs=vmem_specs(5),
        out_specs=pl.BlockSpec(memory_space=pltpu.VMEM),
        scratch_shapes=[pltpu.VMEM((slot_count * channels, flat_width), jnp.float32)],
        cost_estimate=pl.CostEstimate(
            flops=2 * slot_count * channels * flat_width * (27 * channels + 1400),
            bytes_accessed=grid_cells.size * 4 + pieces.size * 2 + 3 * 2**20 + 27 * channels * channels * 4,
            transcendentals=0,
        ),
    )(
        grad_cells,
        grid_cells.reshape(slot_count * channels, grid_width),
        pieces.reshape(slot_count * channels, pieces.shape[2]),
        place[0],
        place[1],
    )
    return jnp.transpose(per_depth.reshape(3, channels, 9 * channels), (1, 0, 2)).reshape(
        channels, 27 * channels
    )


HALO_SHIFTS = (-3, -2, -1, 1, 2, 3)


def halo_kernel(faces_ref, pool_ref, send_sems, recv_sems):
    me = lax.axis_index("space")
    column = lax.axis_index("dp")
    count = lax.axis_size("space")
    centre = len(HALO_SHIFTS) // 2
    first_lanes = 2 * EDGE * EDGE
    pool_ref[...] = jnp.zeros(pool_ref.shape, pool_ref.dtype)
    pool_ref[centre] = faces_ref[...]
    barrier = pltpu.get_barrier_semaphore()
    partners = 0
    for shift in HALO_SHIFTS:
        target = me - shift
        reachable = (target >= 0) & (target < count)
        partners = partners + reachable.astype(jnp.int32)

        @pl.when(reachable)
        def _():
            pl.semaphore_signal(
                barrier, 1, device_id=(target, column), device_id_type=pl.DeviceIdType.MESH
            )

    pl.semaphore_wait(barrier, partners)
    copies = []
    for index, shift in enumerate(HALO_SHIFTS):
        target = me - shift
        lanes = pl.ds(0, first_lanes) if abs(shift) > 1 else pl.ds(0, faces_ref.shape[2])
        copy = pltpu.make_async_remote_copy(
            src_ref=faces_ref.at[:, :, lanes],
            dst_ref=pool_ref.at[shift + centre, :, :, lanes],
            send_sem=send_sems.at[index],
            recv_sem=recv_sems.at[index],
            device_id=(jnp.clip(target, 0, count - 1), column),
            device_id_type=pl.DeviceIdType.MESH,
        )
        sends = (target >= 0) & (target < count)
        receives = (me + shift >= 0) & (me + shift < count)
        copies.append((copy, sends, receives))

        @pl.when(sends)
        def _():
            copy.start()

    for copy, sends, receives in copies:

        @pl.when(sends)
        def _():
            copy.wait_send()

        @pl.when(receives)
        def _():
            copy.wait_recv()


def build_pool(outer_faces):
    slot_count, channels, width = outer_faces.shape
    groups = len(HALO_SHIFTS) + 1
    pool = pl.pallas_call(
        halo_kernel,
        out_shape=jax.ShapeDtypeStruct((groups, slot_count, channels, width), outer_faces.dtype),
        in_specs=[pl.BlockSpec(memory_space=pltpu.VMEM)],
        out_specs=pl.BlockSpec(memory_space=pltpu.VMEM),
        scratch_shapes=[
            pltpu.SemaphoreType.DMA((len(HALO_SHIFTS),)),
            pltpu.SemaphoreType.DMA((len(HALO_SHIFTS),)),
        ],
        compiler_params=pltpu.CompilerParams(collective_id=1, has_side_effects=True),
    )(outer_faces)
    return pool.reshape(groups * slot_count, channels, width)


def halo_pieces(grid_cells, pool_rows):
    faces = exact_dot(grid_cells, one_hot(jnp.arange(grid_width, dtype=jnp.int32), face_cells()), "scg,gf->scf")
    pool = build_pool(faces)
    rows = pool.shape[0]
    piece_sources, piece_targets, piece_groups = piece_layout()
    table = exact_dot(pool, one_hot(jnp.arange(faces.shape[2], dtype=jnp.int32), piece_sources), "scf,fe->sce")
    chosen = jnp.take(pool_rows, jnp.asarray(piece_groups), axis=1)
    pick = (chosen[:, None, :] == jnp.arange(rows, dtype=jnp.int32)[None, :, None]).astype(table.dtype)
    return jnp.sum(pick[:, :, None, :] * table[None], axis=1)


REDUCE_ORDERS = ((("core", 2), ("x", 4), ("y", 4), ("z", 4)), (("core", 2), ("y", 4), ("z", 4), ("x", 4)))


def own_coords():
    space = lax.axis_index("space")
    dp = lax.axis_index("dp")
    return {"core": space % 2, "x": dp % 4, "y": space // 2 % 4, "z": dp // 4 * 2 + space // 8}


def mesh_id(coords, name, value):
    moved = dict(coords)
    moved[name] = value
    space = ((moved["z"] % 2) * 4 + moved["y"]) * 2 + moved["core"]
    return (space, moved["z"] // 2 * 4 + moved["x"])


def exchange(copies):
    for copy in copies:
        copy.start()
    for copy in copies:
        copy.wait()


def all_reduce_kernel(*refs):
    lines = len(REDUCE_ORDERS)
    depth = len(REDUCE_ORDERS[0])
    x_ref, out_ref = refs[0], refs[1]
    per_line = (len(refs) - 4) // lines
    scratch = [refs[2 + p * per_line : 2 + (p + 1) * per_line] for p in range(lines)]
    send_sems, recv_sems = refs[-2], refs[-1]
    coords = own_coords()
    barrier = pltpu.get_barrier_semaphore()
    partner_count = 0
    for name, size in REDUCE_ORDERS[0]:
        for steps in range(1, size):
            pl.semaphore_signal(
                barrier, 1, device_id=mesh_id(coords, name, (coords[name] + steps) % size),
                device_id_type=pl.DeviceIdType.MESH,
            )
            partner_count += 1
    pl.semaphore_wait(barrier, partner_count)
    part = x_ref.shape[0] // lines
    sources = [x_ref.at[pl.ds(p * part, part)] for p in range(lines)]
    copy_id = 0
    for stage in range(depth):
        copies = []
        for p in range(lines):
            name, size = REDUCE_ORDERS[p][stage]
            me = coords[name]
            chunk = sources[p].shape[0] // size
            for steps in range(1, size):
                target = (me + steps) % size
                copies.append(pltpu.make_async_remote_copy(
                    src_ref=sources[p].at[pl.ds(pl.multiple_of(target * chunk, chunk), chunk)],
                    dst_ref=scratch[p][depth - 1 + stage].at[steps - 1],
                    send_sem=send_sems.at[copy_id],
                    recv_sem=recv_sems.at[copy_id],
                    device_id=mesh_id(coords, name, target),
                    device_id_type=pl.DeviceIdType.MESH,
                ))
                copy_id += 1
        exchange(copies)
        for p in range(lines):
            name, size = REDUCE_ORDERS[p][stage]
            me = coords[name]
            chunk = sources[p].shape[0] // size
            slots = scratch[p][depth - 1 + stage]
            total = sources[p][pl.ds(pl.multiple_of(me * chunk, chunk), chunk)]
            for steps in range(1, size):
                total = total + slots[steps - 1]
            if stage < depth - 1:
                scratch[p][stage][...] = total
                sources[p] = scratch[p][stage]
            else:
                scratch[p][2 * depth - 1][pl.ds(pl.multiple_of(me * chunk, chunk), chunk)] = total
    holders = [list(scratch[p][2 * depth - 1 : 2 * depth - 1 + depth - 1]) + [out_ref.at[pl.ds(p * part, part)]] for p in range(lines)]
    for level in range(depth):
        stage = depth - 1 - level
        copies = []
        for p in range(lines):
            name, size = REDUCE_ORDERS[p][stage]
            me = coords[name]
            holder = holders[p][level]
            piece = holder.shape[0] // size
            for steps in range(1, size):
                copies.append(pltpu.make_async_remote_copy(
                    src_ref=holder.at[pl.ds(pl.multiple_of(me * piece, piece), piece)],
                    dst_ref=scratch[p][3 * depth - 2 + level].at[steps - 1],
                    send_sem=send_sems.at[copy_id],
                    recv_sem=recv_sems.at[copy_id],
                    device_id=mesh_id(coords, name, (me + steps) % size),
                    device_id_type=pl.DeviceIdType.MESH,
                ))
                copy_id += 1
        exchange(copies)
        for p in range(lines):
            name, size = REDUCE_ORDERS[p][stage]
            me = coords[name]
            holder = holders[p][level]
            piece = holder.shape[0] // size
            slots = scratch[p][3 * depth - 2 + level]
            for steps in range(1, size):
                origin = (me - steps + size) % size
                holder[pl.ds(pl.multiple_of(origin * piece, piece), piece)] = slots[steps - 1]
            if level + 1 < depth:
                upper = holders[p][level + 1]
                next_me = coords[REDUCE_ORDERS[p][stage - 1][0]]
                span = holder.shape[0]
                upper[pl.ds(pl.multiple_of(next_me * span, span), span)] = holder[...]


def all_reduce_rows(flat):
    rows, lanes = flat.shape
    lines = len(REDUCE_ORDERS)
    part = rows // lines
    scratch = []
    copies = 0
    for order in REDUCE_ORDERS:
        sizes = [s for _, s in order]
        sums, reduce_slots, gather_slots, gathered = [], [], [], []
        current = part
        for size in sizes:
            current //= size
            reduce_slots.append((size - 1, current, lanes))
            sums.append((current, lanes))
        piece = current
        for size in reversed(sizes):
            gather_slots.append((size - 1, piece, lanes))
            piece *= size
            gathered.append((piece, lanes))
        shapes = sums[:-1] + reduce_slots + gathered[:-1] + gather_slots
        scratch += [pltpu.VMEM(s, jnp.float32) for s in shapes]
        copies += 2 * sum(s - 1 for s in sizes)
    scratch += [pltpu.SemaphoreType.DMA((copies,)), pltpu.SemaphoreType.DMA((copies,))]
    return pl.pallas_call(
        all_reduce_kernel,
        out_shape=jax.ShapeDtypeStruct(flat.shape, flat.dtype),
        in_specs=[pl.BlockSpec(memory_space=pltpu.VMEM)],
        out_specs=pl.BlockSpec(memory_space=pltpu.VMEM),
        scratch_shapes=scratch,
        compiler_params=pltpu.CompilerParams(collective_id=0, has_side_effects=True),
    )(flat)


def share_grads(weight_sums, bias_sums):
    flat = jnp.concatenate([weight_sums.reshape(-1), bias_sums.reshape(-1)])
    rows = 4096
    padded = jnp.pad(flat, (0, rows * 128 - flat.shape[0])).reshape(rows, 128)
    summed = all_reduce_rows(padded).reshape(-1)
    weight_total = summed[: weight_sums.size].reshape(weight_sums.shape)
    bias_total = summed[weight_sums.size : flat.shape[0]].reshape(bias_sums.shape)
    return weight_total, bias_total


def silu_slope(values):
    sigma = jax.nn.sigmoid(values)
    return sigma * (1.0 + values * (1.0 - sigma))


def local(volume, neighbours, active, cotangent, weight_one, weight_two, bias_one, bias_two):
    slot_count, channels = (volume.shape[1], volume.shape[2])
    position = lax.axis_index("space")
    own_alive = lax.dynamic_slice_in_dim(active[0], position * slot_count, slot_count, 0)
    near_table = lax.dynamic_slice_in_dim(neighbours[0], position * slot_count, slot_count, 0)
    safe_slot = jnp.maximum(near_table, 0)
    source_offset = safe_slot // slot_count - position + 3
    pool_rows = jnp.where(
        near_table < 0, 7 * slot_count, source_offset * slot_count + safe_slot % slot_count
    )
    live_mask = own_alive.astype(jnp.float32)[:, None, None]
    cells = jnp.asarray(cell_grid())
    to_cells = one_hot(jnp.arange(grid_width, dtype=jnp.int32), cells)
    valid = jnp.zeros((grid_width,), jnp.float32).at[cells].set(1.0)
    place = placement()
    back_rows = jnp.transpose(
        weight_two.reshape(channels, 27, channels)[:, ::-1, :], (2, 1, 0)
    ).reshape(channels, 27 * channels)
    masked = volume[0] * live_mask.astype(jnp.bfloat16)
    masked_grid = exact_dot(masked, to_cells, "scn,gn->scg")
    pieces_x = halo_pieces(masked_grid, pool_rows)
    hidden_pre = conv_grid(masked_grid, pieces_x, place, weight_one) + bias_one[None, :, None]
    hidden = (jax.nn.silu(hidden_pre) * live_mask).astype(jnp.bfloat16)
    pieces_h = halo_pieces(hidden, pool_rows)
    out_pre = conv_grid(hidden, pieces_h, place, weight_two) + bias_two[None, :, None]
    result = (jax.nn.silu(out_pre) * live_mask).astype(jnp.bfloat16)
    upstream = exact_dot(cotangent[0], to_cells, "scn,gn->scg")
    grad_out = (upstream.astype(jnp.float32) * live_mask * silu_slope(out_pre)).astype(jnp.bfloat16)
    grad_w_two = weight_grad(grad_out, hidden, pieces_h, place)
    grad_b_two = jnp.sum(grad_out.astype(jnp.float32), axis=(0, 2))
    pieces_g = halo_pieces(grad_out, pool_rows)
    hidden_grad = conv_grid(grad_out, pieces_g, place, back_rows)
    grad_hidden = (hidden_grad * (live_mask * valid) * silu_slope(hidden_pre)).astype(jnp.bfloat16)
    grad_w_one = weight_grad(grad_hidden, masked_grid, pieces_x, place)
    grad_b_one = jnp.sum(grad_hidden.astype(jnp.float32), axis=(0, 2))
    shared_all = share_grads(
        jnp.concatenate([grad_w_one, grad_w_two], axis=0),
        jnp.stack([grad_b_one, grad_b_two], axis=0),
    )
    total_w_one, total_w_two = (shared_all[0][:channels], shared_all[0][channels:])
    total_b_one, total_b_two = (shared_all[1][0], shared_all[1][1])
    output = exact_dot(result, to_cells, "scg,gn->scn")[None]
    return (output, total_w_one, total_w_two, total_b_one, total_b_two)


def solution(mesh):
    in_specs = (
        P("dp", "space", None, None),
        P("dp", None, None),
        P("dp", None),
        P("dp", "space", None, None),
        P(),
        P(),
        P(),
        P(),
    )
    out_specs = (P("dp", "space", None, None), P(), P(), P(), P())
    return jax.shard_map(local, mesh=mesh, in_specs=in_specs, out_specs=out_specs, check_vma=False)
```

```python
import jax
import numpy as np
import jax.numpy as jnp
from jax import lax
from jax.sharding import PartitionSpec as P
from jax.experimental import pallas as pl
from jax.experimental.pallas import tpu as pltpu

EDGE = 8


OFFSETS = [
    (a, b, c) for a in (-1, 0, 1) for b in (-1, 0, 1) for c in (-1, 0, 1) if (a, b, c) != (0, 0, 0)
]
grid_width = 896
flat_width = 1280


def shifted(value, axis, steps):
    count = lax.axis_size(axis)
    leading, last = (max(0, -steps), min(count, count - steps))
    return lax.ppermute(value, axis, [(source, source + steps) for source in range(leading, last)])


def face_index(offset):
    if offset[0] != 0:
        return 1 if offset[0] < 0 else 0
    if offset[1] != 0:
        return 3 if offset[1] < 0 else 2
    return 5 if offset[2] < 0 else 4


def face_span(shift_by, edge_len):
    if shift_by < 0:
        return slice(edge_len - 1, edge_len)
    if shift_by > 0:
        return slice(0, 1)
    return slice(0, edge_len)


def target(shift_by, edge_len):
    if shift_by < 0:
        return slice(0, 1)
    if shift_by > 0:
        return slice(edge_len + 1, edge_len + 2)
    return slice(1, edge_len + 1)


def grid_at(p, q, r):
    return p * (EDGE + 2) ** 2 + q * (EDGE + 2) + r


def face_cells():
    last = EDGE - 1
    cells = []
    for fixed_axis in range(3):
        for fixed_at in (0, last):
            for u in range(EDGE):
                for w in range(EDGE):
                    spot = [u, w]
                    spot.insert(fixed_axis, fixed_at)
                    cells.append(grid_at(*spot))
    return np.array(cells, np.int32)


def piece_layout():
    sources, targets, groups = [], [], []
    face_area = EDGE * EDGE
    for nonzero in (1, 2, 3):
        for k, offset in enumerate(OFFSETS):
            if sum(v != 0 for v in offset) != nonzero:
                continue
            a, b, c = offset
            base = face_index(offset) * face_area
            face = np.arange(base, base + face_area).reshape(EDGE, EDGE)
            if a != 0:
                part = face[face_span(b, EDGE), face_span(c, EDGE)]
            elif b != 0:
                part = face[:, face_span(c, EDGE)]
            else:
                part = face
            sources.extend(part.reshape(-1).tolist())
            groups.extend([k] * part.size)
            for pp in range(EDGE + 2)[target(a, EDGE)]:
                for qq in range(EDGE + 2)[target(b, EDGE)]:
                    for rr in range(EDGE + 2)[target(c, EDGE)]:
                        targets.append(grid_at(pp, qq, rr))
    return np.array(sources, np.int32), np.array(targets, np.int32), np.array(groups, np.int32)


def cell_grid():
    return np.array(
        [grid_at(p, q, r) for p in range(EDGE) for q in range(EDGE) for r in range(EDGE)], np.int32
    )


def one_hot(rows, columns):
    return (jnp.asarray(rows)[:, None] == jnp.asarray(columns)[None, :]).astype(jnp.bfloat16)


def placement():
    grid_ids = jnp.arange(grid_width, dtype=jnp.int32)
    cells = jnp.asarray(cell_grid())
    valid = jnp.zeros((grid_width,), jnp.int32).at[cells].set(1)
    center_target = jnp.where(valid > 0, grid_ids + grid_at(1, 1, 1), -1)
    from_center = one_hot(center_target, jnp.arange(flat_width, dtype=jnp.int32))
    piece_sources, piece_targets, piece_groups = piece_layout()
    from_pieces = one_hot(piece_targets, jnp.arange(flat_width, dtype=jnp.int32))
    return from_center, from_pieces


def exact_dot(left, right, spec):
    return jnp.einsum(spec, left, right, preferred_element_type=jnp.float32).astype(left.dtype)


def stacked_windows(whole):
    windows = []
    for b in range(3):
        for c in range(3):
            start = b * (EDGE + 2) + c
            moved = whole if start == 0 else pltpu.roll(whole, flat_width - start, 1)
            windows.append(moved.astype(jnp.bfloat16))
    return jnp.concatenate(windows, axis=0)


def fill_padded(grid_ref, piece_ref, center_ref, halo_ref, whole_ref):
    whole_ref[...] = jnp.dot(
        grid_ref[...], center_ref[...], preferred_element_type=jnp.float32
    ) + jnp.dot(piece_ref[...], halo_ref[...], preferred_element_type=jnp.float32)


def conv_kernel(grid_ref, piece_ref, center_ref, halo_ref, taps_ref, out_ref, whole_ref):
    plane = (EDGE + 2) ** 2
    channels = out_ref.shape[1]
    fill_padded(grid_ref, piece_ref, center_ref, halo_ref, whole_ref)

    def one_brick(brick, carry):
        whole = whole_ref[pl.ds(pl.multiple_of(brick * channels, channels), channels), :]
        product = jnp.dot(taps_ref[...], stacked_windows(whole), preferred_element_type=jnp.float32)
        summed = product[:channels]
        for a in (1, 2):
            summed = summed + pltpu.roll(
                product[a * channels : (a + 1) * channels], flat_width - a * plane, 1
            )
        out_ref[brick] = summed[:, :grid_width]
        return carry

    lax.fori_loop(0, out_ref.shape[0], one_brick, 0)


def weight_grad_kernel(grad_ref, grid_ref, piece_ref, center_ref, halo_ref, out_ref, whole_ref):
    plane = (EDGE + 2) ** 2
    channels = grad_ref.shape[1]
    fill_padded(grid_ref, piece_ref, center_ref, halo_ref, whole_ref)
    out_ref[...] = jnp.zeros(out_ref.shape, jnp.float32)

    def one_brick(brick, carry):
        whole = whole_ref[pl.ds(pl.multiple_of(brick * channels, channels), channels), :]
        grad_cells = grad_ref[brick].astype(jnp.float32)
        grad_wide = jnp.concatenate(
            [grad_cells, jnp.zeros((channels, flat_width - grid_width), jnp.float32)], axis=1
        )
        moved = [grad_wide] + [pltpu.roll(grad_wide, a * plane, 1) for a in (1, 2)]
        out_ref[...] += lax.dot_general(
            jnp.concatenate(moved, axis=0).astype(jnp.bfloat16),
            stacked_windows(whole),
            (((1,), (1,)), ((), ())),
            preferred_element_type=jnp.float32,
        )
        return carry

    lax.fori_loop(0, grad_ref.shape[0], one_brick, 0)


def vmem_specs(count):
    return [pl.BlockSpec(memory_space=pltpu.VMEM)] * count


def tap_rows(weight_rows):
    channels = weight_rows.shape[0]
    return jnp.transpose(weight_rows.reshape(channels, 3, 9 * channels), (1, 0, 2)).reshape(
        3 * channels, 9 * channels
    )


def conv_grid(grid_cells, pieces, place, weight_rows):
    slot_count, channels = (grid_cells.shape[0], weight_rows.shape[0])
    return pl.pallas_call(
        conv_kernel,
        out_shape=jax.ShapeDtypeStruct((slot_count, channels, grid_width), jnp.float32),
        in_specs=vmem_specs(5),
        out_specs=pl.BlockSpec(memory_space=pltpu.VMEM),
        scratch_shapes=[pltpu.VMEM((slot_count * channels, flat_width), jnp.float32)],
        cost_estimate=pl.CostEstimate(
            flops=2 * slot_count * channels * flat_width * (weight_rows.shape[1] + 1400),
            bytes_accessed=grid_cells.size * 2 + pieces.size * 2 + 3 * 2**20 + slot_count * channels * grid_width * 4,
            transcendentals=0,
        ),
    )(
        grid_cells.reshape(slot_count * channels, grid_width),
        pieces.reshape(slot_count * channels, pieces.shape[2]),
        place[0],
        place[1],
        tap_rows(weight_rows),
    )


def weight_grad(grad_cells, grid_cells, pieces, place):
    slot_count, channels = (grid_cells.shape[0], grid_cells.shape[1])
    per_depth = pl.pallas_call(
        weight_grad_kernel,
        out_shape=jax.ShapeDtypeStruct((3 * channels, 9 * channels), jnp.float32),
        in_specs=vmem_specs(5),
        out_specs=pl.BlockSpec(memory_space=pltpu.VMEM),
        scratch_shapes=[pltpu.VMEM((slot_count * channels, flat_width), jnp.float32)],
        cost_estimate=pl.CostEstimate(
            flops=2 * slot_count * channels * flat_width * (27 * channels + 1400),
            bytes_accessed=grid_cells.size * 4 + pieces.size * 2 + 3 * 2**20 + 27 * channels * channels * 4,
            transcendentals=0,
        ),
    )(
        grad_cells,
        grid_cells.reshape(slot_count * channels, grid_width),
        pieces.reshape(slot_count * channels, pieces.shape[2]),
        place[0],
        place[1],
    )
    return jnp.transpose(per_depth.reshape(3, channels, 9 * channels), (1, 0, 2)).reshape(
        channels, 27 * channels
    )


HALO_SHIFTS = (-3, -2, -1, 1, 2, 3)


def halo_kernel(faces_ref, pool_ref, send_sems, recv_sems):
    me = lax.axis_index("space")
    column = lax.axis_index("dp")
    count = lax.axis_size("space")
    centre = len(HALO_SHIFTS) // 2
    first_lanes = 2 * EDGE * EDGE
    pool_ref[centre] = faces_ref[...]
    for shift in HALO_SHIFTS:
        slot = shift + centre
        arrives = (me + shift >= 0) & (me + shift < count)
        if abs(shift) > 1:
            pool_ref[slot, :, :, first_lanes:] = jnp.zeros(
                pool_ref.shape[1:3] + (pool_ref.shape[3] - first_lanes,), pool_ref.dtype
            )

        @pl.when(jnp.logical_not(arrives))
        def _():
            pool_ref[slot] = jnp.zeros(pool_ref.shape[1:], pool_ref.dtype)
    barrier = pltpu.get_barrier_semaphore()
    partners = 0
    for shift in HALO_SHIFTS:
        target = me - shift
        reachable = (target >= 0) & (target < count)
        partners = partners + reachable.astype(jnp.int32)

        @pl.when(reachable)
        def _():
            pl.semaphore_signal(
                barrier, 1, device_id=(target, column), device_id_type=pl.DeviceIdType.MESH
            )

    pl.semaphore_wait(barrier, partners)
    copies = []
    for index, shift in enumerate(HALO_SHIFTS):
        target = me - shift
        lanes = pl.ds(0, first_lanes) if abs(shift) > 1 else pl.ds(0, faces_ref.shape[2])
        copy = pltpu.make_async_remote_copy(
            src_ref=faces_ref.at[:, :, lanes],
            dst_ref=pool_ref.at[shift + centre, :, :, lanes],
            send_sem=send_sems.at[index],
            recv_sem=recv_sems.at[index],
            device_id=(jnp.clip(target, 0, count - 1), column),
            device_id_type=pl.DeviceIdType.MESH,
        )
        sends = (target >= 0) & (target < count)
        receives = (me + shift >= 0) & (me + shift < count)
        copies.append((copy, sends, receives))

        @pl.when(sends)
        def _():
            copy.start()

    for copy, sends, receives in copies:

        @pl.when(sends)
        def _():
            copy.wait_send()

        @pl.when(receives)
        def _():
            copy.wait_recv()


def build_pool(outer_faces):
    slot_count, channels, width = outer_faces.shape
    groups = len(HALO_SHIFTS) + 1
    pool = pl.pallas_call(
        halo_kernel,
        out_shape=jax.ShapeDtypeStruct((groups, slot_count, channels, width), outer_faces.dtype),
        in_specs=[pl.BlockSpec(memory_space=pltpu.VMEM)],
        out_specs=pl.BlockSpec(memory_space=pltpu.VMEM),
        scratch_shapes=[
            pltpu.SemaphoreType.DMA((len(HALO_SHIFTS),)),
            pltpu.SemaphoreType.DMA((len(HALO_SHIFTS),)),
        ],
        compiler_params=pltpu.CompilerParams(collective_id=1, has_side_effects=True),
    )(outer_faces)
    return pool.reshape(groups * slot_count, channels, width)


def halo_pieces(grid_cells, pool_rows):
    faces = exact_dot(grid_cells, one_hot(jnp.arange(grid_width, dtype=jnp.int32), face_cells()), "scg,gf->scf")
    pool = build_pool(faces)
    rows = pool.shape[0]
    piece_sources, piece_targets, piece_groups = piece_layout()
    table = exact_dot(pool, one_hot(jnp.arange(faces.shape[2], dtype=jnp.int32), piece_sources), "scf,fe->sce")
    chosen = jnp.take(pool_rows, jnp.asarray(piece_groups), axis=1)
    pick = (chosen[:, None, :] == jnp.arange(rows, dtype=jnp.int32)[None, :, None]).astype(table.dtype)
    return jnp.sum(pick[:, :, None, :] * table[None], axis=1)


REDUCE_ORDERS = ((("core", 2), ("x", 4), ("y", 4), ("z", 4)), (("core", 2), ("y", 4), ("z", 4), ("x", 4)))


def own_coords():
    space = lax.axis_index("space")
    dp = lax.axis_index("dp")
    return {"core": space % 2, "x": dp % 4, "y": space // 2 % 4, "z": dp // 4 * 2 + space // 8}


def mesh_id(coords, name, value):
    moved = dict(coords)
    moved[name] = value
    space = ((moved["z"] % 2) * 4 + moved["y"]) * 2 + moved["core"]
    return (space, moved["z"] // 2 * 4 + moved["x"])


def exchange(copies):
    for copy in copies:
        copy.start()
    for copy in copies:
        copy.wait()


def all_reduce_kernel(*refs):
    lines = len(REDUCE_ORDERS)
    depth = len(REDUCE_ORDERS[0])
    x_ref, out_ref = refs[0], refs[1]
    per_line = (len(refs) - 4) // lines
    scratch = [refs[2 + p * per_line : 2 + (p + 1) * per_line] for p in range(lines)]
    send_sems, recv_sems = refs[-2], refs[-1]
    coords = own_coords()
    barrier = pltpu.get_barrier_semaphore()
    partner_count = 0
    for name, size in REDUCE_ORDERS[0]:
        for steps in range(1, size):
            pl.semaphore_signal(
                barrier, 1, device_id=mesh_id(coords, name, (coords[name] + steps) % size),
                device_id_type=pl.DeviceIdType.MESH,
            )
            partner_count += 1
    pl.semaphore_wait(barrier, partner_count)
    part = x_ref.shape[0] // lines
    sources = [x_ref.at[pl.ds(p * part, part)] for p in range(lines)]
    copy_id = 0
    for stage in range(depth):
        copies = []
        for p in range(lines):
            name, size = REDUCE_ORDERS[p][stage]
            me = coords[name]
            chunk = sources[p].shape[0] // size
            for steps in range(1, size):
                target = (me + steps) % size
                copies.append(pltpu.make_async_remote_copy(
                    src_ref=sources[p].at[pl.ds(pl.multiple_of(target * chunk, chunk), chunk)],
                    dst_ref=scratch[p][depth - 1 + stage].at[steps - 1],
                    send_sem=send_sems.at[copy_id],
                    recv_sem=recv_sems.at[copy_id],
                    device_id=mesh_id(coords, name, target),
                    device_id_type=pl.DeviceIdType.MESH,
                ))
                copy_id += 1
        exchange(copies)
        for p in range(lines):
            name, size = REDUCE_ORDERS[p][stage]
            me = coords[name]
            chunk = sources[p].shape[0] // size
            slots = scratch[p][depth - 1 + stage]
            total = sources[p][pl.ds(pl.multiple_of(me * chunk, chunk), chunk)]
            for steps in range(1, size):
                total = total + slots[steps - 1]
            if stage < depth - 1:
                scratch[p][stage][...] = total
                sources[p] = scratch[p][stage]
            else:
                scratch[p][2 * depth - 1][pl.ds(pl.multiple_of(me * chunk, chunk), chunk)] = total
    holders = [list(scratch[p][2 * depth - 1 : 2 * depth - 1 + depth - 1]) + [out_ref.at[pl.ds(p * part, part)]] for p in range(lines)]
    for level in range(depth):
        stage = depth - 1 - level
        copies = []
        for p in range(lines):
            name, size = REDUCE_ORDERS[p][stage]
            me = coords[name]
            holder = holders[p][level]
            piece = holder.shape[0] // size
            for steps in range(1, size):
                copies.append(pltpu.make_async_remote_copy(
                    src_ref=holder.at[pl.ds(pl.multiple_of(me * piece, piece), piece)],
                    dst_ref=scratch[p][3 * depth - 2 + level].at[steps - 1],
                    send_sem=send_sems.at[copy_id],
                    recv_sem=recv_sems.at[copy_id],
                    device_id=mesh_id(coords, name, (me + steps) % size),
                    device_id_type=pl.DeviceIdType.MESH,
                ))
                copy_id += 1
        exchange(copies)
        for p in range(lines):
            name, size = REDUCE_ORDERS[p][stage]
            me = coords[name]
            holder = holders[p][level]
            piece = holder.shape[0] // size
            slots = scratch[p][3 * depth - 2 + level]
            for steps in range(1, size):
                origin = (me - steps + size) % size
                holder[pl.ds(pl.multiple_of(origin * piece, piece), piece)] = slots[steps - 1]
            if level + 1 < depth:
                upper = holders[p][level + 1]
                next_me = coords[REDUCE_ORDERS[p][stage - 1][0]]
                span = holder.shape[0]
                upper[pl.ds(pl.multiple_of(next_me * span, span), span)] = holder[...]


def all_reduce_rows(flat):
    rows, lanes = flat.shape
    lines = len(REDUCE_ORDERS)
    part = rows // lines
    scratch = []
    copies = 0
    for order in REDUCE_ORDERS:
        sizes = [s for _, s in order]
        sums, reduce_slots, gather_slots, gathered = [], [], [], []
        current = part
        for size in sizes:
            current //= size
            reduce_slots.append((size - 1, current, lanes))
            sums.append((current, lanes))
        piece = current
        for size in reversed(sizes):
            gather_slots.append((size - 1, piece, lanes))
            piece *= size
            gathered.append((piece, lanes))
        shapes = sums[:-1] + reduce_slots + gathered[:-1] + gather_slots
        scratch += [pltpu.VMEM(s, jnp.float32) for s in shapes]
        copies += 2 * sum(s - 1 for s in sizes)
    scratch += [pltpu.SemaphoreType.DMA((copies,)), pltpu.SemaphoreType.DMA((copies,))]
    return pl.pallas_call(
        all_reduce_kernel,
        out_shape=jax.ShapeDtypeStruct(flat.shape, flat.dtype),
        in_specs=[pl.BlockSpec(memory_space=pltpu.VMEM)],
        out_specs=pl.BlockSpec(memory_space=pltpu.VMEM),
        scratch_shapes=scratch,
        compiler_params=pltpu.CompilerParams(collective_id=0, has_side_effects=True),
    )(flat)


def share_grads(weight_sums, bias_sums):
    flat = jnp.concatenate([weight_sums.reshape(-1), bias_sums.reshape(-1)])
    rows = 4096
    padded = jnp.pad(flat, (0, rows * 128 - flat.shape[0])).reshape(rows, 128)
    summed = all_reduce_rows(padded).reshape(-1)
    weight_total = summed[: weight_sums.size].reshape(weight_sums.shape)
    bias_total = summed[weight_sums.size : flat.shape[0]].reshape(bias_sums.shape)
    return weight_total, bias_total


def silu_slope(values):
    sigma = jax.nn.sigmoid(values)
    return sigma * (1.0 + values * (1.0 - sigma))


def local(volume, neighbours, active, cotangent, weight_one, weight_two, bias_one, bias_two):
    slot_count, channels = (volume.shape[1], volume.shape[2])
    position = lax.axis_index("space")
    own_alive = lax.dynamic_slice_in_dim(active[0], position * slot_count, slot_count, 0)
    near_table = lax.dynamic_slice_in_dim(neighbours[0], position * slot_count, slot_count, 0)
    safe_slot = jnp.maximum(near_table, 0)
    source_offset = safe_slot // slot_count - position + 3
    pool_rows = jnp.where(
        near_table < 0, 7 * slot_count, source_offset * slot_count + safe_slot % slot_count
    )
    live_mask = own_alive.astype(jnp.float32)[:, None, None]
    cells = jnp.asarray(cell_grid())
    to_cells = one_hot(jnp.arange(grid_width, dtype=jnp.int32), cells)
    valid = jnp.zeros((grid_width,), jnp.float32).at[cells].set(1.0)
    place = placement()
    back_rows = jnp.transpose(
        weight_two.reshape(channels, 27, channels)[:, ::-1, :], (2, 1, 0)
    ).reshape(channels, 27 * channels)
    masked = volume[0] * live_mask.astype(jnp.bfloat16)
    masked_grid = exact_dot(masked, to_cells, "scn,gn->scg")
    pieces_x = halo_pieces(masked_grid, pool_rows)
    hidden_pre = conv_grid(masked_grid, pieces_x, place, weight_one) + bias_one[None, :, None]
    hidden = (jax.nn.silu(hidden_pre) * live_mask).astype(jnp.bfloat16)
    pieces_h = halo_pieces(hidden, pool_rows)
    out_pre = conv_grid(hidden, pieces_h, place, weight_two) + bias_two[None, :, None]
    result = (jax.nn.silu(out_pre) * live_mask).astype(jnp.bfloat16)
    upstream = exact_dot(cotangent[0], to_cells, "scn,gn->scg")
    grad_out = (upstream.astype(jnp.float32) * live_mask * silu_slope(out_pre)).astype(jnp.bfloat16)
    grad_w_two = weight_grad(grad_out, hidden, pieces_h, place)
    grad_b_two = jnp.sum(grad_out.astype(jnp.float32), axis=(0, 2))
    pieces_g = halo_pieces(grad_out, pool_rows)
    hidden_grad = conv_grid(grad_out, pieces_g, place, back_rows)
    grad_hidden = (hidden_grad * (live_mask * valid) * silu_slope(hidden_pre)).astype(jnp.bfloat16)
    grad_w_one = weight_grad(grad_hidden, masked_grid, pieces_x, place)
    grad_b_one = jnp.sum(grad_hidden.astype(jnp.float32), axis=(0, 2))
    shared_all = share_grads(
        jnp.concatenate([grad_w_one, grad_w_two], axis=0),
        jnp.stack([grad_b_one, grad_b_two], axis=0),
    )
    total_w_one, total_w_two = (shared_all[0][:channels], shared_all[0][channels:])
    total_b_one, total_b_two = (shared_all[1][0], shared_all[1][1])
    output = exact_dot(result, to_cells, "scg,gn->scn")[None]
    return (output, total_w_one, total_w_two, total_b_one, total_b_two)


def solution(mesh):
    in_specs = (
        P("dp", "space", None, None),
        P("dp", None, None),
        P("dp", None),
        P("dp", "space", None, None),
        P(),
        P(),
        P(),
        P(),
    )
    out_specs = (P("dp", "space", None, None), P(), P(), P(), P())
    return jax.shard_map(local, mesh=mesh, in_specs=in_specs, out_specs=out_specs, check_vma=False)
```

```python
import jax
import numpy as np
import jax.numpy as jnp
from jax import lax
from jax.sharding import PartitionSpec as P
from jax.experimental import pallas as pl
from jax.experimental.pallas import tpu as pltpu

EDGE = 8


OFFSETS = [
    (a, b, c) for a in (-1, 0, 1) for b in (-1, 0, 1) for c in (-1, 0, 1) if (a, b, c) != (0, 0, 0)
]
grid_width = 896
flat_width = 1280


def shifted(value, axis, steps):
    count = lax.axis_size(axis)
    leading, last = (max(0, -steps), min(count, count - steps))
    return lax.ppermute(value, axis, [(source, source + steps) for source in range(leading, last)])


def face_index(offset):
    if offset[0] != 0:
        return 1 if offset[0] < 0 else 0
    if offset[1] != 0:
        return 3 if offset[1] < 0 else 2
    return 5 if offset[2] < 0 else 4


def face_span(shift_by, edge_len):
    if shift_by < 0:
        return slice(edge_len - 1, edge_len)
    if shift_by > 0:
        return slice(0, 1)
    return slice(0, edge_len)


def target(shift_by, edge_len):
    if shift_by < 0:
        return slice(0, 1)
    if shift_by > 0:
        return slice(edge_len + 1, edge_len + 2)
    return slice(1, edge_len + 1)


def grid_at(p, q, r):
    return p * (EDGE + 2) ** 2 + q * (EDGE + 2) + r


def face_cells():
    last = EDGE - 1
    cells = []
    for fixed_axis in range(3):
        for fixed_at in (0, last):
            for u in range(EDGE):
                for w in range(EDGE):
                    spot = [u, w]
                    spot.insert(fixed_axis, fixed_at)
                    cells.append(grid_at(*spot))
    return np.array(cells, np.int32)


def piece_layout():
    sources, targets, groups = [], [], []
    face_area = EDGE * EDGE
    for nonzero in (1, 2, 3):
        for k, offset in enumerate(OFFSETS):
            if sum(v != 0 for v in offset) != nonzero:
                continue
            a, b, c = offset
            base = face_index(offset) * face_area
            face = np.arange(base, base + face_area).reshape(EDGE, EDGE)
            if a != 0:
                part = face[face_span(b, EDGE), face_span(c, EDGE)]
            elif b != 0:
                part = face[:, face_span(c, EDGE)]
            else:
                part = face
            sources.extend(part.reshape(-1).tolist())
            groups.extend([k] * part.size)
            for pp in range(EDGE + 2)[target(a, EDGE)]:
                for qq in range(EDGE + 2)[target(b, EDGE)]:
                    for rr in range(EDGE + 2)[target(c, EDGE)]:
                        targets.append(grid_at(pp, qq, rr))
    return np.array(sources, np.int32), np.array(targets, np.int32), np.array(groups, np.int32)


def cell_grid():
    return np.array(
        [grid_at(p, q, r) for p in range(EDGE) for q in range(EDGE) for r in range(EDGE)], np.int32
    )


def one_hot(rows, columns):
    return (jnp.asarray(rows)[:, None] == jnp.asarray(columns)[None, :]).astype(jnp.bfloat16)


def placement():
    grid_ids = jnp.arange(grid_width, dtype=jnp.int32)
    cells = jnp.asarray(cell_grid())
    valid = jnp.zeros((grid_width,), jnp.int32).at[cells].set(1)
    center_target = jnp.where(valid > 0, grid_ids + grid_at(1, 1, 1), -1)
    from_center = one_hot(center_target, jnp.arange(flat_width, dtype=jnp.int32))
    piece_sources, piece_targets, piece_groups = piece_layout()
    from_pieces = one_hot(piece_targets, jnp.arange(flat_width, dtype=jnp.int32))
    return from_center, from_pieces


def exact_dot(left, right, spec):
    return jnp.einsum(spec, left, right, preferred_element_type=jnp.float32).astype(left.dtype)


def stacked_windows(whole):
    windows = []
    for b in range(3):
        for c in range(3):
            start = b * (EDGE + 2) + c
            moved = whole if start == 0 else pltpu.roll(whole, flat_width - start, 1)
            windows.append(moved.astype(jnp.bfloat16))
    return jnp.concatenate(windows, axis=0)


def fill_padded(grid_ref, piece_ref, center_ref, halo_ref, whole_ref):
    whole_ref[...] = jnp.dot(
        grid_ref[...], center_ref[...], preferred_element_type=jnp.float32
    ) + jnp.dot(piece_ref[...], halo_ref[...], preferred_element_type=jnp.float32)


def conv_kernel(grid_ref, piece_ref, center_ref, halo_ref, taps_ref, out_ref, whole_ref):
    plane = (EDGE + 2) ** 2
    channels = out_ref.shape[1]
    fill_padded(grid_ref, piece_ref, center_ref, halo_ref, whole_ref)

    def one_brick(brick, carry):
        whole = whole_ref[pl.ds(pl.multiple_of(brick * channels, channels), channels), :]
        product = jnp.dot(taps_ref[...], stacked_windows(whole), preferred_element_type=jnp.float32)
        summed = product[:channels]
        for a in (1, 2):
            summed = summed + pltpu.roll(
                product[a * channels : (a + 1) * channels], flat_width - a * plane, 1
            )
        out_ref[brick] = summed[:, :grid_width]
        return carry

    lax.fori_loop(0, out_ref.shape[0], one_brick, 0)


def weight_grad_kernel(grad_ref, grid_ref, piece_ref, center_ref, halo_ref, out_ref, whole_ref):
    plane = (EDGE + 2) ** 2
    channels = grad_ref.shape[1]
    fill_padded(grid_ref, piece_ref, center_ref, halo_ref, whole_ref)
    out_ref[...] = jnp.zeros(out_ref.shape, jnp.float32)

    def one_brick(brick, carry):
        whole = whole_ref[pl.ds(pl.multiple_of(brick * channels, channels), channels), :]
        grad_cells = grad_ref[brick].astype(jnp.float32)
        grad_wide = jnp.concatenate(
            [grad_cells, jnp.zeros((channels, flat_width - grid_width), jnp.float32)], axis=1
        )
        moved = [grad_wide] + [pltpu.roll(grad_wide, a * plane, 1) for a in (1, 2)]
        out_ref[...] += lax.dot_general(
            jnp.concatenate(moved, axis=0).astype(jnp.bfloat16),
            stacked_windows(whole),
            (((1,), (1,)), ((), ())),
            preferred_element_type=jnp.float32,
        )
        return carry

    lax.fori_loop(0, grad_ref.shape[0], one_brick, 0)


def vmem_specs(count):
    return [pl.BlockSpec(memory_space=pltpu.VMEM)] * count


def tap_rows(weight_rows):
    channels = weight_rows.shape[0]
    return jnp.transpose(weight_rows.reshape(channels, 3, 9 * channels), (1, 0, 2)).reshape(
        3 * channels, 9 * channels
    )


def conv_grid(grid_cells, pieces, place, weight_rows):
    slot_count, channels = (grid_cells.shape[0], weight_rows.shape[0])
    return pl.pallas_call(
        conv_kernel,
        out_shape=jax.ShapeDtypeStruct((slot_count, channels, grid_width), jnp.float32),
        in_specs=vmem_specs(5),
        out_specs=pl.BlockSpec(memory_space=pltpu.VMEM),
        scratch_shapes=[pltpu.VMEM((slot_count * channels, flat_width), jnp.float32)],
        cost_estimate=pl.CostEstimate(
            flops=2 * slot_count * channels * flat_width * (weight_rows.shape[1] + 1400),
            bytes_accessed=grid_cells.size * 2 + pieces.size * 2 + 3 * 2**20 + slot_count * channels * grid_width * 4,
            transcendentals=0,
        ),
    )(
        grid_cells.reshape(slot_count * channels, grid_width),
        pieces.reshape(slot_count * channels, pieces.shape[2]),
        place[0],
        place[1],
        tap_rows(weight_rows),
    )


def weight_grad(grad_cells, grid_cells, pieces, place):
    slot_count, channels = (grid_cells.shape[0], grid_cells.shape[1])
    per_depth = pl.pallas_call(
        weight_grad_kernel,
        out_shape=jax.ShapeDtypeStruct((3 * channels, 9 * channels), jnp.float32),
        in_specs=vmem_specs(5),
        out_specs=pl.BlockSpec(memory_space=pltpu.VMEM),
        scratch_shapes=[pltpu.VMEM((slot_count * channels, flat_width), jnp.float32)],
        cost_estimate=pl.CostEstimate(
            flops=2 * slot_count * channels * flat_width * (27 * channels + 1400),
            bytes_accessed=grid_cells.size * 4 + pieces.size * 2 + 3 * 2**20 + 27 * channels * channels * 4,
            transcendentals=0,
        ),
    )(
        grad_cells,
        grid_cells.reshape(slot_count * channels, grid_width),
        pieces.reshape(slot_count * channels, pieces.shape[2]),
        place[0],
        place[1],
    )
    return jnp.transpose(per_depth.reshape(3, channels, 9 * channels), (1, 0, 2)).reshape(
        channels, 27 * channels
    )


HALO_SHIFTS = (-3, -2, -1, 1, 2, 3)


def halo_kernel(faces_ref, pool_ref, send_sems, recv_sems):
    me = lax.axis_index("space")
    column = lax.axis_index("dp")
    count = lax.axis_size("space")
    centre = len(HALO_SHIFTS) // 2
    first_lanes = 2 * EDGE * EDGE
    pool_ref[centre] = faces_ref[...]
    for shift in HALO_SHIFTS:
        slot = shift + centre
        arrives = (me + shift >= 0) & (me + shift < count)
        if abs(shift) > 1:
            pool_ref[slot, :, :, first_lanes:] = jnp.zeros(
                pool_ref.shape[1:3] + (pool_ref.shape[3] - first_lanes,), pool_ref.dtype
            )

        @pl.when(jnp.logical_not(arrives))
        def _():
            pool_ref[slot] = jnp.zeros(pool_ref.shape[1:], pool_ref.dtype)
    barrier = pltpu.get_barrier_semaphore()
    partners = 0
    for shift in HALO_SHIFTS:
        target = me - shift
        reachable = (target >= 0) & (target < count)
        partners = partners + reachable.astype(jnp.int32)

        @pl.when(reachable)
        def _():
            pl.semaphore_signal(
                barrier, 1, device_id=(target, column), device_id_type=pl.DeviceIdType.MESH
            )

    pl.semaphore_wait(barrier, partners)
    copies = []
    for index, shift in enumerate(HALO_SHIFTS):
        target = me - shift
        lanes = pl.ds(0, first_lanes) if abs(shift) > 1 else pl.ds(0, faces_ref.shape[2])
        copy = pltpu.make_async_remote_copy(
            src_ref=faces_ref.at[:, :, lanes],
            dst_ref=pool_ref.at[shift + centre, :, :, lanes],
            send_sem=send_sems.at[index],
            recv_sem=recv_sems.at[index],
            device_id=(jnp.clip(target, 0, count - 1), column),
            device_id_type=pl.DeviceIdType.MESH,
        )
        sends = (target >= 0) & (target < count)
        receives = (me + shift >= 0) & (me + shift < count)
        copies.append((copy, sends, receives))

        @pl.when(sends)
        def _():
            copy.start()

    for copy, sends, receives in copies:

        @pl.when(sends)
        def _():
            copy.wait_send()

        @pl.when(receives)
        def _():
            copy.wait_recv()


def build_pool(outer_faces):
    slot_count, channels, width = outer_faces.shape
    groups = len(HALO_SHIFTS) + 1
    pool = pl.pallas_call(
        halo_kernel,
        out_shape=jax.ShapeDtypeStruct((groups, slot_count, channels, width), outer_faces.dtype),
        in_specs=[pl.BlockSpec(memory_space=pltpu.VMEM)],
        out_specs=pl.BlockSpec(memory_space=pltpu.VMEM),
        scratch_shapes=[
            pltpu.SemaphoreType.DMA((len(HALO_SHIFTS),)),
            pltpu.SemaphoreType.DMA((len(HALO_SHIFTS),)),
        ],
        compiler_params=pltpu.CompilerParams(collective_id=1, has_side_effects=True),
    )(outer_faces)
    return pool.reshape(groups * slot_count, channels, width)


def halo_pieces(grid_cells, pool_rows):
    faces = exact_dot(grid_cells, one_hot(jnp.arange(grid_width, dtype=jnp.int32), face_cells()), "scg,gf->scf")
    pool = build_pool(faces)
    rows = pool.shape[0]
    piece_sources, piece_targets, piece_groups = piece_layout()
    table = exact_dot(pool, one_hot(jnp.arange(faces.shape[2], dtype=jnp.int32), piece_sources), "scf,fe->sce")
    chosen = jnp.take(pool_rows, jnp.asarray(piece_groups), axis=1)
    pick = (chosen[:, None, :] == jnp.arange(rows, dtype=jnp.int32)[None, :, None]).astype(table.dtype)
    return jnp.sum(pick[:, :, None, :] * table[None], axis=1)


REDUCE_ORDERS = ((("core", 2), ("x", 4), ("y", 4), ("z", 4)), (("core", 2), ("y", 4), ("z", 4), ("x", 4)))


def own_coords():
    space = lax.axis_index("space")
    dp = lax.axis_index("dp")
    return {"core": space % 2, "x": dp % 4, "y": space // 2 % 4, "z": dp // 4 * 2 + space // 8}


def mesh_id(coords, name, value):
    moved = dict(coords)
    moved[name] = value
    space = ((moved["z"] % 2) * 4 + moved["y"]) * 2 + moved["core"]
    return (space, moved["z"] // 2 * 4 + moved["x"])


def exchange(copies):
    for copy in copies:
        copy.start()
    for copy in copies:
        copy.wait()


def all_reduce_kernel(*refs):
    lines = len(REDUCE_ORDERS)
    depth = len(REDUCE_ORDERS[0])
    x_ref, out_ref = refs[0], refs[1]
    per_line = (len(refs) - 4) // lines
    scratch = [refs[2 + p * per_line : 2 + (p + 1) * per_line] for p in range(lines)]
    send_sems, recv_sems = refs[-2], refs[-1]
    coords = own_coords()
    barrier = pltpu.get_barrier_semaphore()
    partner_count = 0
    for name, size in REDUCE_ORDERS[0]:
        for steps in range(1, size):
            pl.semaphore_signal(
                barrier, 1, device_id=mesh_id(coords, name, (coords[name] + steps) % size),
                device_id_type=pl.DeviceIdType.MESH,
            )
            partner_count += 1
    pl.semaphore_wait(barrier, partner_count)
    part = x_ref.shape[0] // lines
    sources = [x_ref.at[pl.ds(p * part, part)] for p in range(lines)]
    copy_id = 0
    for stage in range(depth):
        copies = []
        for p in range(lines):
            name, size = REDUCE_ORDERS[p][stage]
            me = coords[name]
            chunk = sources[p].shape[0] // size
            for steps in range(1, size):
                target = (me + steps) % size
                copies.append(pltpu.make_async_remote_copy(
                    src_ref=sources[p].at[pl.ds(pl.multiple_of(target * chunk, chunk), chunk)],
                    dst_ref=scratch[p][depth - 1 + stage].at[steps - 1],
                    send_sem=send_sems.at[copy_id],
                    recv_sem=recv_sems.at[copy_id],
                    device_id=mesh_id(coords, name, target),
                    device_id_type=pl.DeviceIdType.MESH,
                ))
                copy_id += 1
        exchange(copies)
        for p in range(lines):
            name, size = REDUCE_ORDERS[p][stage]
            me = coords[name]
            chunk = sources[p].shape[0] // size
            slots = scratch[p][depth - 1 + stage]
            total = sources[p][pl.ds(pl.multiple_of(me * chunk, chunk), chunk)]
            for steps in range(1, size):
                total = total + slots[steps - 1]
            if stage < depth - 1:
                scratch[p][stage][...] = total
                sources[p] = scratch[p][stage]
            else:
                scratch[p][2 * depth - 1][pl.ds(pl.multiple_of(me * chunk, chunk), chunk)] = total
    holders = [list(scratch[p][2 * depth - 1 : 2 * depth - 1 + depth - 1]) + [out_ref.at[pl.ds(p * part, part)]] for p in range(lines)]
    for level in range(depth):
        stage = depth - 1 - level
        copies = []
        for p in range(lines):
            name, size = REDUCE_ORDERS[p][stage]
            me = coords[name]
            holder = holders[p][level]
            piece = holder.shape[0] // size
            for steps in range(1, size):
                copies.append(pltpu.make_async_remote_copy(
                    src_ref=holder.at[pl.ds(pl.multiple_of(me * piece, piece), piece)],
                    dst_ref=scratch[p][3 * depth - 2 + level].at[steps - 1],
                    send_sem=send_sems.at[copy_id],
                    recv_sem=recv_sems.at[copy_id],
                    device_id=mesh_id(coords, name, (me + steps) % size),
                    device_id_type=pl.DeviceIdType.MESH,
                ))
                copy_id += 1
        exchange(copies)
        for p in range(lines):
            name, size = REDUCE_ORDERS[p][stage]
            me = coords[name]
            holder = holders[p][level]
            piece = holder.shape[0] // size
            slots = scratch[p][3 * depth - 2 + level]
            for steps in range(1, size):
                origin = (me - steps + size) % size
                holder[pl.ds(pl.multiple_of(origin * piece, piece), piece)] = slots[steps - 1]
            if level + 1 < depth:
                upper = holders[p][level + 1]
                next_me = coords[REDUCE_ORDERS[p][stage - 1][0]]
                span = holder.shape[0]
                upper[pl.ds(pl.multiple_of(next_me * span, span), span)] = holder[...]


def all_reduce_rows(flat):
    rows, lanes = flat.shape
    lines = len(REDUCE_ORDERS)
    part = rows // lines
    scratch = []
    copies = 0
    for order in REDUCE_ORDERS:
        sizes = [s for _, s in order]
        sums, reduce_slots, gather_slots, gathered = [], [], [], []
        current = part
        for size in sizes:
            current //= size
            reduce_slots.append((size - 1, current, lanes))
            sums.append((current, lanes))
        piece = current
        for size in reversed(sizes):
            gather_slots.append((size - 1, piece, lanes))
            piece *= size
            gathered.append((piece, lanes))
        shapes = sums[:-1] + reduce_slots + gathered[:-1] + gather_slots
        scratch += [pltpu.VMEM(s, jnp.float32) for s in shapes]
        copies += 2 * sum(s - 1 for s in sizes)
    scratch += [pltpu.SemaphoreType.DMA((copies,)), pltpu.SemaphoreType.DMA((copies,))]
    return pl.pallas_call(
        all_reduce_kernel,
        out_shape=jax.ShapeDtypeStruct(flat.shape, flat.dtype),
        in_specs=[pl.BlockSpec(memory_space=pltpu.VMEM)],
        out_specs=pl.BlockSpec(memory_space=pltpu.VMEM),
        scratch_shapes=scratch,
        compiler_params=pltpu.CompilerParams(collective_id=0, has_side_effects=True),
    )(flat)


def share_grads(weight_sums, bias_sums):
    flat = jnp.concatenate([weight_sums.reshape(-1), bias_sums.reshape(-1)])
    rows = 4096
    padded = jnp.pad(flat, (0, rows * 128 - flat.shape[0])).reshape(rows, 128)
    summed = all_reduce_rows(padded).reshape(-1)
    weight_total = summed[: weight_sums.size].reshape(weight_sums.shape)
    bias_total = summed[weight_sums.size : flat.shape[0]].reshape(bias_sums.shape)
    return weight_total, bias_total


def silu_slope(values):
    sigma = jax.nn.sigmoid(values)
    return sigma * (1.0 + values * (1.0 - sigma))


def local(volume, neighbours, active, cotangent, weight_one, weight_two, bias_one, bias_two):
    slot_count, channels = (volume.shape[1], volume.shape[2])
    position = lax.axis_index("space")
    own_alive = lax.dynamic_slice_in_dim(active[0], position * slot_count, slot_count, 0)
    near_table = lax.dynamic_slice_in_dim(neighbours[0], position * slot_count, slot_count, 0)
    safe_slot = jnp.maximum(near_table, 0)
    source_offset = safe_slot // slot_count - position + 3
    pool_rows = jnp.where(
        near_table < 0, 7 * slot_count, source_offset * slot_count + safe_slot % slot_count
    )
    live_mask = own_alive.astype(jnp.float32)[:, None, None]
    cells = jnp.asarray(cell_grid())
    to_cells = one_hot(jnp.arange(grid_width, dtype=jnp.int32), cells)
    valid = jnp.zeros((grid_width,), jnp.float32).at[cells].set(1.0)
    place = placement()
    back_rows = jnp.transpose(
        weight_two.reshape(channels, 27, channels)[:, ::-1, :], (2, 1, 0)
    ).reshape(channels, 27 * channels)
    masked = volume[0] * live_mask.astype(jnp.bfloat16)
    masked_grid = exact_dot(masked, to_cells, "scn,gn->scg")
    pieces_x = halo_pieces(masked_grid, pool_rows)
    hidden_pre = conv_grid(masked_grid, pieces_x, place, weight_one) + bias_one[None, :, None]
    hidden = (jax.nn.silu(hidden_pre) * live_mask).astype(jnp.bfloat16)
    pieces_h = halo_pieces(hidden, pool_rows)
    out_pre = conv_grid(hidden, pieces_h, place, weight_two) + bias_two[None, :, None]
    result = (jax.nn.silu(out_pre) * live_mask).astype(jnp.bfloat16)
    upstream = exact_dot(cotangent[0], to_cells, "scn,gn->scg")
    grad_out = (upstream.astype(jnp.float32) * live_mask * silu_slope(out_pre)).astype(jnp.bfloat16)
    grad_w_two = weight_grad(grad_out, hidden, pieces_h, place)
    grad_b_two = jnp.einsum("scg,g->c", grad_out, jnp.ones((grid_width,), jnp.bfloat16), preferred_element_type=jnp.float32)
    pieces_g = halo_pieces(grad_out, pool_rows)
    hidden_grad = conv_grid(grad_out, pieces_g, place, back_rows)
    grad_hidden = (hidden_grad * (live_mask * valid) * silu_slope(hidden_pre)).astype(jnp.bfloat16)
    grad_w_one = weight_grad(grad_hidden, masked_grid, pieces_x, place)
    grad_b_one = jnp.einsum("scg,g->c", grad_hidden, jnp.ones((grid_width,), jnp.bfloat16), preferred_element_type=jnp.float32)
    shared_all = share_grads(
        jnp.concatenate([grad_w_one, grad_w_two], axis=0),
        jnp.stack([grad_b_one, grad_b_two], axis=0),
    )
    total_w_one, total_w_two = (shared_all[0][:channels], shared_all[0][channels:])
    total_b_one, total_b_two = (shared_all[1][0], shared_all[1][1])
    output = exact_dot(result, to_cells, "scg,gn->scn")[None]
    return (output, total_w_one, total_w_two, total_b_one, total_b_two)


def solution(mesh):
    in_specs = (
        P("dp", "space", None, None),
        P("dp", None, None),
        P("dp", None),
        P("dp", "space", None, None),
        P(),
        P(),
        P(),
        P(),
    )
    out_specs = (P("dp", "space", None, None), P(), P(), P(), P())
    return jax.shard_map(local, mesh=mesh, in_specs=in_specs, out_specs=out_specs, check_vma=False)
```
